256 devices in a mesh: contact: 32 (over y, x, core), body: 8 (over z).
Axes of the slice: x: 4, y: 4, z: 8, core: 2. Of those that a mesh axis runs over, the one named last changes fastest.
Arguments:
- jacobian: bfloat16 [4096, 2, 384, 384], P(('contact', 'body')), may hold values from -0.21875 to 0.21875
- tile_block: int32 [4096, 2], P(('contact', 'body')), may hold values from 0 to 31
- tile_count: int32 [256], P(('contact', 'body')), may hold values from 8 to 16, as said below
- vel_free: float32 [256, 384], P('body'), may hold values from -6 to 6
- inv_mass: float32 [256, 384], P('body'), may hold values from 0.25 to 2
- bias: float32 [4096, 384], P(('contact', 'body')), may hold values from -6 to 6
- step_scale: float32 [4096, 384], P(('contact', 'body')), may hold values from 0.05 to 0.5
- friction: float32 [4096, 128], P(('contact', 'body')), may hold values from 0.2 to 1
- impulse_start: float32 [4096, 384], P(('contact', 'body')), may hold values from -6 to 6
Outputs:
- impulse: float32 [4096, 384], P(('contact', 'body'))
- velocity: float32 [256, 384], P('body')
The draws below stay inside these ranges and needn't reach their ends.
Inputs may be any that keep to these rules, and one draw needn't show every extreme that they name: `tile_count`: some device has all 16 tile slots live in every draw.
All inputs are finite; a program needn't handle non-finite values.
Results may differ from the reference program's by a relative error of at most 0.0062.
Values may be sent and summed in bfloat16 or wider, within the bound.
A program may use at most 64 MiB of HBM per device.

```python
import math
import jax
import jax.numpy as jnp
from jax import lax

TC = 128
TILES_DEV = 16
SLAB_BLK = 32
ITERS = 2
CROW = 384
BDOF = 384
NDEV = 256
TILES = 4096
NBLK = 256
N_BODY = 8


def draw_tile_count(key, part):
    devices = TILES // TILES_DEV
    first_key, second_key = jax.random.split(jax.random.fold_in(key, 17))
    counts = jax.random.randint(first_key, (devices,), TILES_DEV // 2, TILES_DEV + 1)
    fullest = jax.random.randint(second_key, (), 0, devices)
    return jnp.where(jnp.arange(devices) == fullest, TILES_DEV, counts).astype(jnp.int32)


def touch_ends(drawn, rng, low, high):
    place = [jax.random.randint(jax.random.fold_in(rng, axis), (), 0, length) for axis, length in enumerate(drawn.shape)]
    widest = drawn.shape.index(max(drawn.shape))
    beside = place[:widest] + [(place[widest] + 1) % drawn.shape[widest]] + place[widest + 1:]
    return drawn.at[tuple(place)].set(low).at[tuple(beside)].set(high)


def steps_of(stream_key, extent, cuts, least, top_value):
    level, own = 1.0, jax.random.fold_in(stream_key, 6)
    for position, blocks in cuts:
        steps = jnp.exp(jax.random.uniform(jax.random.fold_in(own, position), (blocks,), jnp.float32, least / len(cuts), top_value / len(cuts)))
        level = level * jnp.repeat(steps, extent[position] // blocks).reshape([-1 if axis == position else 1 for axis in range(len(extent))])
    return level


def noise(rng, extent, deviation, bound, shards=(), kind=jnp.bfloat16):
    entries = deviation * jax.random.normal(rng, extent, jnp.float32)
    if shards:
        entries = entries * steps_of(rng, extent, shards, -0.22, 0.18)
    return jnp.clip(entries, -bound, bound).astype(kind)


def setup_inputs(seed: int = 0) -> dict:
    splits = jax.random.split(jax.random.key(seed), 10)
    return {
        "jacobian": noise(splits[0], (TILES, 2, BDOF, CROW), (2 * BDOF) ** -0.5, 0.21875, ((0, 256),)),
        "tile_block": touch_ends(jax.random.randint(splits[1], (TILES, 2), 0, SLAB_BLK), jax.random.fold_in(splits[1], 1), 0, SLAB_BLK - 1).astype(jnp.int32),
        "tile_count": draw_tile_count(jax.random.fold_in(splits[9], 71), 0),
        "vel_free": noise(splits[3], (NBLK, BDOF), 1.0, 6.0, ((0, 8),), jnp.float32),
        "inv_mass": jnp.clip(jnp.exp(math.log(2.0) - 2.0794415 * jax.random.uniform(splits[4], (NBLK, BDOF), jnp.float32) ** steps_of(splits[4], (NBLK, BDOF), ((0, 8),), -0.2, 0.2)), 0.25, 2.0),
        "bias": noise(splits[5], (TILES, CROW), 1.0, 6.0, ((0, 256),), jnp.float32),
        "step_scale": jnp.clip(jnp.exp(math.log(0.5) - 2.3025851 * jax.random.uniform(splits[6], (TILES, CROW), jnp.float32) ** steps_of(splits[6], (TILES, CROW), ((0, 256),), -0.2, 0.2)), 0.05, 0.5),
        "friction": jnp.clip(0.2 + 0.8 * jax.random.uniform(splits[7], (TILES, TC), jnp.float32) ** steps_of(splits[7], (TILES, TC), ((0, 256),), -0.2, 0.2), 0.2, 1.0),
        "impulse_start": noise(splits[8], (TILES, CROW), 1.0, 6.0, ((0, 256),), jnp.float32),
    }


def project(trial, friction):
    normal = trial[:, :TC]
    first = trial[:, TC:2 * TC]
    second = trial[:, 2 * TC:]
    tangent = jnp.sqrt(first * first + second * second)
    inside = tangent <= friction * normal
    below = friction * tangent <= -normal
    moved = (normal + friction * tangent) / (1.0 + friction * friction)
    safe = jnp.where(inside | below, 1.0, tangent)
    factor = jnp.where(inside, 1.0, jnp.where(below, 0.0, friction * moved / safe))
    new_normal = jnp.where(inside, normal, jnp.where(below, 0.0, moved))
    return jnp.concatenate([new_normal, first * factor, second * factor], axis=1)

def reference(jacobian, tile_block, tile_count, vel_free, inv_mass, bias, step_scale, friction, impulse_start):
    tile_ids = jnp.arange(TILES, dtype=jnp.int32)
    group = tile_ids // TILES_DEV
    live = tile_ids % TILES_DEV < tile_count[group]
    mask = live.astype(jnp.float32)[:, None]
    slab = group % N_BODY
    block_own = (slab * SLAB_BLK + tile_block[:, 0]).astype(jnp.int32)
    block_next = ((slab + 1) % N_BODY * SLAB_BLK + tile_block[:, 1]).astype(jnp.int32)
    jac_groups = jacobian.reshape(NDEV, TILES_DEV, 2, BDOF, CROW)

    def velocities(lam):
        lamb = lam.astype(jnp.bfloat16).reshape(NDEV, TILES_DEV, CROW)
        push = lax.map(lambda pair: jnp.einsum('tkbc,tc->tkb', pair[0].astype(jnp.float32), pair[1].astype(jnp.float32), precision=lax.Precision.HIGHEST), (jac_groups, lamb))
        push = push.reshape(TILES, 2, BDOF)
        total = jax.ops.segment_sum(push[:, 0], block_own, NBLK) + jax.ops.segment_sum(push[:, 1], block_next, NBLK)
        return vel_free + inv_mass * total

    def relative(vel):
        velb = vel.astype(jnp.bfloat16)
        rows = jnp.stack([velb[block_own], velb[block_next]], axis=1).reshape(NDEV, TILES_DEV, 2, BDOF)
        rel = lax.map(lambda pair: jnp.einsum('tkbc,tkb->tc', pair[0].astype(jnp.float32), pair[1].astype(jnp.float32), precision=lax.Precision.HIGHEST), (jac_groups, rows))
        return rel.reshape(TILES, CROW) + bias
    lam = impulse_start * mask
    for sweep in range(ITERS):
        vel = velocities(lam)
        rel = relative(vel)
        lam = project(lam - step_scale * rel, friction) * mask
    return (lam, velocities(lam))
```

```python
import functools

import jax
import jax.numpy as jnp
from jax import lax
from jax.experimental import pallas as pl
from jax.experimental.pallas import tpu as pltpu
from jax.sharding import PartitionSpec as P

ITERS = 2
MESH = pl.DeviceIdType.MESH


def project(trial, friction, contacts):
    normal = trial[:, :contacts]
    first = trial[:, contacts : 2 * contacts]
    second = trial[:, 2 * contacts :]
    tangent = jnp.sqrt(first * first + second * second)
    inside = tangent <= friction * normal
    below = friction * tangent <= -normal
    moved = (normal + friction * tangent) / (1.0 + friction * friction)
    safe = jnp.where(inside | below, 1.0, tangent)
    factor = jnp.where(inside, 1.0, jnp.where(below, 0.0, friction * moved / safe))
    new_normal = jnp.where(inside, normal, jnp.where(below, 0.0, moved))
    return jnp.concatenate([new_normal, first * factor, second * factor], axis=1)


def exchange_kernel(
    n_contact, n_body, last,
    own_ref, later_ref, vfree_ref, imass_ref, *rest,
):
    steps = n_contact.bit_length() - 1
    if last:
        vel_ref, recv_l, stage, recv_c, send_sem, recv_sem = rest
    else:
        velb_ref, velb_next_ref, recv_l, stage, recv_c, recv_v, send_sem, recv_sem = rest
    c = lax.axis_index("contact")
    b = lax.axis_index("body")
    up = lax.rem(b + 1, n_body)
    down = lax.rem(b + n_body - 1, n_body)
    partners = []
    for k in range(steps):
        width = 1 << k
        bit = lax.rem(c // width, 2)
        partners.append(c + (1 - 2 * bit) * width)

    barrier = pltpu.get_barrier_semaphore()
    for p in partners:
        pl.semaphore_signal(barrier, inc=1, device_id=(p, b), device_id_type=MESH)
    for nb in (up, down):
        pl.semaphore_signal(barrier, inc=1, device_id=(c, nb), device_id_type=MESH)
    pl.semaphore_wait(barrier, steps + 2)

    shift = pltpu.make_async_remote_copy(
        src_ref=later_ref, dst_ref=recv_l, send_sem=send_sem.at[0], recv_sem=recv_sem.at[0],
        device_id=(c, up), device_id_type=MESH,
    )
    shift.start()
    shift.wait()
    stage[0] = own_ref[...] + recv_l[...]
    copies = []
    for k in range(steps):
        copy = pltpu.make_async_remote_copy(
            src_ref=stage.at[k], dst_ref=recv_c.at[k],
            send_sem=send_sem.at[k + 1], recv_sem=recv_sem.at[k + 1],
            device_id=(partners[k], b), device_id_type=MESH,
        )
        copy.start()
        copy.wait_recv()
        stage[k + 1] = stage[k] + recv_c[k]
        copies.append(copy)
    vel = vfree_ref[...] + imass_ref[...] * stage[steps]
    if last:
        vel_ref[...] = vel
    else:
        velb_ref[...] = vel.astype(jnp.bfloat16)
        back = pltpu.make_async_remote_copy(
            src_ref=velb_ref, dst_ref=recv_v, send_sem=send_sem.at[steps + 1],
            recv_sem=recv_sem.at[steps + 1], device_id=(c, down), device_id_type=MESH,
        )
        back.start()
        back.wait()
        velb_next_ref[...] = recv_v[...]
    for copy in copies:
        copy.wait_send()


def exchange(own, later, vel_free, inv_mass, n_contact, n_body, last):
    shape = own.shape
    steps = n_contact.bit_length() - 1
    vspec = pl.BlockSpec(memory_space=pltpu.VMEM)
    if last:
        out_shape = jax.ShapeDtypeStruct(shape, jnp.float32)
        out_specs = vspec
        extra = []
    else:
        out_shape = (
            jax.ShapeDtypeStruct(shape, jnp.bfloat16),
            jax.ShapeDtypeStruct(shape, jnp.bfloat16),
        )
        out_specs = (vspec, vspec)
        extra = [pltpu.VMEM(shape, jnp.bfloat16)]
    scratch = [
        pltpu.VMEM(shape, jnp.float32),
        pltpu.VMEM((steps + 1,) + shape, jnp.float32),
        pltpu.VMEM((steps,) + shape, jnp.float32),
        *extra,
        pltpu.SemaphoreType.DMA((steps + 2,)),
        pltpu.SemaphoreType.DMA((steps + 2,)),
    ]
    return pl.pallas_call(
        functools.partial(exchange_kernel, n_contact, n_body, last),
        out_shape=out_shape,
        in_specs=[vspec] * 4,
        out_specs=out_specs,
        scratch_shapes=scratch,
        compiler_params=pltpu.CompilerParams(
            collective_id=1 if last else 0, has_side_effects=True
        ),
    )(own, later, vel_free, inv_mass)


def per_device(
    n_contact, n_body,
    jacobian, tile_block, tile_count, vel_free, inv_mass, bias, step_scale, friction, impulse_start,
):
    tiles_here = jacobian.shape[0]
    slab_blocks = vel_free.shape[0]
    contacts = friction.shape[1]
    order = jnp.arange(tiles_here, dtype=jnp.int32)
    mask = (order < tile_count[0]).astype(jnp.float32)[:, None]
    span = jnp.arange(slab_blocks, dtype=jnp.int32)
    pick_own = (tile_block[:, 0:1] == span[None, :]).astype(jnp.float32)
    pick_next = (tile_block[:, 1:2] == span[None, :]).astype(jnp.float32)
    pick_own_b = pick_own.astype(jnp.bfloat16)
    pick_next_b = pick_next.astype(jnp.bfloat16)

    def partials(lam):
        lamb = lam.astype(jnp.bfloat16)
        push = jnp.einsum("tkbc,tc->tkb", jacobian, lamb, preferred_element_type=jnp.float32)
        own = jnp.einsum("ts,tb->sb", pick_own, push[:, 0], precision=lax.Precision.HIGHEST)
        later = jnp.einsum("ts,tb->sb", pick_next, push[:, 1], precision=lax.Precision.HIGHEST)
        return own, later

    lam = impulse_start * mask
    for sweep in range(ITERS):
        own, later = partials(lam)
        velb, velb_next = exchange(own, later, vel_free, inv_mass, n_contact, n_body, False)
        rows_own = jnp.dot(pick_own_b, velb, preferred_element_type=jnp.float32).astype(
            jnp.bfloat16
        )
        rows_next = jnp.dot(pick_next_b, velb_next, preferred_element_type=jnp.float32).astype(
            jnp.bfloat16
        )
        rows = jnp.stack([rows_own, rows_next], axis=1)
        rel = jnp.einsum("tkbc,tkb->tc", jacobian, rows, preferred_element_type=jnp.float32) + bias
        lam = project(lam - step_scale * rel, friction, contacts) * mask
    own, later = partials(lam)
    velocity = exchange(own, later, vel_free, inv_mass, n_contact, n_body, True)
    return (lam, velocity)


def solution(mesh):
    n_contact = mesh.shape["contact"]
    n_body = mesh.shape["body"]
    placed = (
        P(("contact", "body"), None, None, None),
        P(("contact", "body"), None),
        P(("contact", "body")),
        P("body", None),
        P("body", None),
        P(("contact", "body"), None),
        P(("contact", "body"), None),
        P(("contact", "body"), None),
        P(("contact", "body"), None),
    )
    return jax.shard_map(
        functools.partial(per_device, n_contact, n_body),
        mesh=mesh,
        in_specs=placed,
        out_specs=(P(("contact", "body"), None), P("body", None)),
        check_vma=False,
    )
```

```python
import functools
import math

import jax
import jax.numpy as jnp
from jax import lax
from jax.experimental import pallas as pl
from jax.experimental.pallas import tpu as pltpu
from jax.sharding import PartitionSpec as P

ITERS = 2
MESH = pl.DeviceIdType.MESH


def project(trial, friction, contacts):
    normal = trial[:, :contacts]
    first = trial[:, contacts : 2 * contacts]
    second = trial[:, 2 * contacts :]
    tangent = jnp.sqrt(first * first + second * second)
    inside = tangent <= friction * normal
    below = friction * tangent <= -normal
    moved = (normal + friction * tangent) / (1.0 + friction * friction)
    safe = jnp.where(inside | below, 1.0, tangent)
    factor = jnp.where(inside, 1.0, jnp.where(below, 0.0, friction * moved / safe))
    new_normal = jnp.where(inside, normal, jnp.where(below, 0.0, moved))
    return jnp.concatenate([new_normal, first * factor, second * factor], axis=1)


def contact_groups(n_contact):
    rest = n_contact // 2
    gy = 1
    for d in range(1, int(math.isqrt(rest)) + 1):
        if rest % d == 0:
            gy = d
    return rest // gy, gy


def scatter_rows(pick_t_ref, push):
    tiles = push.shape[0]
    acc = None
    for t in range(tiles):
        term = pick_t_ref[:, t : t + 1] * push[t : t + 1, :]
        acc = term if acc is None else acc + term
    return acc


def gather_rows(pick_ref, vel_ref):
    blocks = vel_ref.shape[0]
    acc = None
    for s in range(blocks):
        term = pick_ref[:, s : s + 1] * vel_ref[s : s + 1, :].astype(jnp.float32)
        acc = term if acc is None else acc + term
    return acc


def sweep_kernel(n_contact, n_body, last, *refs):
    gx, gy = contact_groups(n_contact)
    if last:
        (push_ref, pto_ref, ptn_ref, vfree_ref, imass_ref,
         vel_out,
         later_buf, recv_l, p_buf, recv_core, xbuf, ybuf, vel_buf,
         s_sem, r_sem, sx_sem, rx_sem, sy_sem, ry_sem) = refs
    else:
        (push_ref, pto_ref, ptn_ref, vfree_ref, imass_ref, po_ref, pn_ref,
         rows_out,
         later_buf, recv_l, p_buf, recv_core, xbuf, ybuf, vel_buf, vel_next,
         s_sem, r_sem, sx_sem, rx_sem, sy_sem, ry_sem) = refs
    half = p_buf.shape[0] // 2
    c = lax.axis_index("contact")
    b = lax.axis_index("body")
    core = lax.rem(c, 2)
    x = lax.rem(c // 2, gx)
    y = c // (2 * gx)
    mate = c + 1 - 2 * core
    up = lax.rem(b + 1, n_body)
    down = lax.rem(b + n_body - 1, n_body)
    x_peers = [(y * gx + lax.rem(x + j, gx)) * 2 + core for j in range(1, gx)]
    y_peers = [(lax.rem(y + j, gy) * gx + x) * 2 + core for j in range(1, gy)]

    greet = [(c, up), (c, down), (mate, b)]
    greet += [(p, b) for p in x_peers] + [(p, b) for p in y_peers]
    if not last:
        greet += [(mate, up), (mate, down)]
    barrier = pltpu.get_barrier_semaphore()
    for dev in greet:
        pl.semaphore_signal(barrier, inc=1, device_id=dev, device_id_type=MESH)
    pl.semaphore_wait(barrier, len(greet))

    def remote(src, dst, send, recv, dev):
        return pltpu.make_async_remote_copy(
            src_ref=src, dst_ref=dst, send_sem=send, recv_sem=recv,
            device_id=dev, device_id_type=MESH,
        )

    sent = []
    later_buf[...] = scatter_rows(ptn_ref, push_ref[1])
    shift = remote(later_buf, recv_l, s_sem.at[0], r_sem.at[0], (c, up))
    shift.start()
    own = scatter_rows(pto_ref, push_ref[0])
    shift.wait_recv()
    sent.append(shift)
    p_buf[...] = own + recv_l[...]

    mine = pl.ds(pl.multiple_of(core * half, half), half)
    theirs = pl.ds(pl.multiple_of((1 - core) * half, half), half)
    rs = remote(p_buf.at[theirs], recv_core, s_sem.at[1], r_sem.at[1], (mate, b))
    rs.start()
    rs.wait_recv()
    sent.append(rs)
    part = p_buf[mine] + recv_core[...]

    for buf, pos, peers, size, ssem, rsem in (
        (xbuf, x, x_peers, gx, sx_sem, rx_sem),
        (ybuf, y, y_peers, gy, sy_sem, ry_sem),
    ):
        if size == 1:
            continue
        buf[pos] = part
        for j, p in enumerate(peers):
            cp = remote(buf.at[pos], buf.at[pos], ssem.at[j], rsem.at[pos], (p, b))
            cp.start()
            sent.append(cp)
        for j in range(1, size):
            src_pos = lax.rem(pos + size - j, size)
            remote(buf.at[src_pos], buf.at[src_pos], ssem.at[0], rsem.at[src_pos], (peers[-j], b)).wait_recv()
        part = buf[0]
        for g in range(1, size):
            part = part + buf[g]

    vel = vfree_ref[mine] + imass_ref[mine] * part
    if last:
        vel_buf[mine] = vel
        cp = remote(vel_buf.at[mine], vel_buf.at[mine], s_sem.at[2], r_sem.at[2], (mate, b))
        cp.start()
        sent.append(cp)
        remote(vel_buf.at[theirs], vel_buf.at[theirs], s_sem.at[2], r_sem.at[2], (mate, b)).wait_recv()
        vel_out[...] = vel_buf[...]
    else:
        vel_buf[mine] = vel.astype(jnp.bfloat16)
        src = vel_buf.at[mine]
        for k, (dst, dev) in enumerate((
            (vel_buf.at[mine], (mate, b)),
            (vel_next.at[mine], (c, down)),
            (vel_next.at[mine], (mate, down)),
        )):
            cp = remote(src, dst, s_sem.at[2 + k], r_sem.at[2 + k], dev)
            cp.start()
            sent.append(cp)
        for k, (dst, dev) in enumerate((
            (vel_buf.at[theirs], (mate, b)),
            (vel_next.at[mine], (c, up)),
            (vel_next.at[theirs], (mate, up)),
        )):
            remote(src, dst, s_sem.at[2 + k], r_sem.at[2 + k], dev).wait_recv()
        rows_out[0] = gather_rows(po_ref, vel_buf).astype(jnp.bfloat16)
        rows_out[1] = gather_rows(pn_ref, vel_next).astype(jnp.bfloat16)
    for cp in sent:
        cp.wait_send()


def sweep_exchange(push, pick_t_own, pick_t_next, vel_free, inv_mass, pick_own, pick_next,
                   n_contact, n_body, last):
    gx, gy = contact_groups(n_contact)
    blocks, width = vel_free.shape
    half = blocks // 2
    vspec = pl.BlockSpec(memory_space=pltpu.VMEM)
    args = [push, pick_t_own, pick_t_next, vel_free, inv_mass]
    if last:
        out_shape = jax.ShapeDtypeStruct((blocks, width), jnp.float32)
        vel_scratch = [pltpu.VMEM((blocks, width), jnp.float32)]
    else:
        args += [pick_own, pick_next]
        out_shape = jax.ShapeDtypeStruct(push.shape, jnp.bfloat16)
        vel_scratch = [pltpu.VMEM((blocks, width), jnp.bfloat16)] * 2
    scratch = [
        pltpu.VMEM((blocks, width), jnp.float32),
        pltpu.VMEM((blocks, width), jnp.float32),
        pltpu.VMEM((blocks, width), jnp.float32),
        pltpu.VMEM((half, width), jnp.float32),
        pltpu.VMEM((gx, half, width), jnp.float32),
        pltpu.VMEM((gy, half, width), jnp.float32),
        *vel_scratch,
        pltpu.SemaphoreType.DMA((5,)),
        pltpu.SemaphoreType.DMA((5,)),
        pltpu.SemaphoreType.DMA((max(gx - 1, 1),)),
        pltpu.SemaphoreType.DMA((gx,)),
        pltpu.SemaphoreType.DMA((max(gy - 1, 1),)),
        pltpu.SemaphoreType.DMA((gy,)),
    ]
    return pl.pallas_call(
        functools.partial(sweep_kernel, n_contact, n_body, last),
        out_shape=out_shape,
        in_specs=[vspec] * len(args),
        out_specs=vspec,
        scratch_shapes=scratch,
        compiler_params=pltpu.CompilerParams(
            collective_id=1 if last else 0, has_side_effects=True
        ),
    )(*args)


def per_device(
    n_contact, n_body,
    jacobian, tile_block, tile_count, vel_free, inv_mass, bias, step_scale, friction, impulse_start,
):
    tiles_here = jacobian.shape[0]
    slab_blocks = vel_free.shape[0]
    contacts = friction.shape[1]
    order = jnp.arange(tiles_here, dtype=jnp.int32)
    mask = (order < tile_count[0]).astype(jnp.float32)[:, None]
    span = jnp.arange(slab_blocks, dtype=jnp.int32)
    pick_own = (tile_block[:, 0:1] == span[None, :]).astype(jnp.float32)
    pick_next = (tile_block[:, 1:2] == span[None, :]).astype(jnp.float32)
    pick_t_own = pick_own.T
    pick_t_next = pick_next.T

    def pushes(lam):
        lamb = lam.astype(jnp.bfloat16)
        return jnp.einsum("tkbc,tc->ktb", jacobian, lamb, preferred_element_type=jnp.float32)

    lam = impulse_start * mask
    for sweep in range(ITERS):
        rows = sweep_exchange(
            pushes(lam), pick_t_own, pick_t_next, vel_free, inv_mass, pick_own, pick_next,
            n_contact, n_body, False,
        )
        rel = jnp.einsum("tkbc,ktb->tc", jacobian, rows, preferred_element_type=jnp.float32) + bias
        lam = project(lam - step_scale * rel, friction, contacts) * mask
    velocity = sweep_exchange(
        pushes(lam), pick_t_own, pick_t_next, vel_free, inv_mass, pick_own, pick_next,
        n_contact, n_body, True,
    )
    return (lam, velocity)


def solution(mesh):
    n_contact = mesh.shape["contact"]
    n_body = mesh.shape["body"]
    placed = (
        P(("contact", "body"), None, None, None),
        P(("contact", "body"), None),
        P(("contact", "body")),
        P("body", None),
        P("body", None),
        P(("contact", "body"), None),
        P(("contact", "body"), None),
        P(("contact", "body"), None),
        P(("contact", "body"), None),
    )
    return jax.shard_map(
        functools.partial(per_device, n_contact, n_body),
        mesh=mesh,
        in_specs=placed,
        out_specs=(P(("contact", "body"), None), P("body", None)),
        check_vma=False,
    )
```

```python
import functools
import math

import jax
import jax.numpy as jnp
from jax import lax
from jax.experimental import pallas as pl
from jax.experimental.pallas import tpu as pltpu
from jax.sharding import PartitionSpec as P

ITERS = 2
MESH = pl.DeviceIdType.MESH


def project(trial, friction, contacts):
    normal = trial[:, :contacts]
    first = trial[:, contacts : 2 * contacts]
    second = trial[:, 2 * contacts :]
    tangent = jnp.sqrt(first * first + second * second)
    inside = tangent <= friction * normal
    below = friction * tangent <= -normal
    moved = (normal + friction * tangent) / (1.0 + friction * friction)
    safe = jnp.where(inside | below, 1.0, tangent)
    factor = jnp.where(inside, 1.0, jnp.where(below, 0.0, friction * moved / safe))
    new_normal = jnp.where(inside, normal, jnp.where(below, 0.0, moved))
    return jnp.concatenate([new_normal, first * factor, second * factor], axis=1)


def contact_groups(n_contact):
    rest = n_contact // 2
    gy = 1
    for d in range(1, int(math.isqrt(rest)) + 1):
        if rest % d == 0:
            gy = d
    return rest // gy, gy


def scatter_rows(tb_ref, column, push_ref, blocks):
    tiles = push_ref.shape[1]
    width = push_ref.shape[2]
    slot = lax.broadcasted_iota(jnp.int32, (blocks, width), 0)
    acc = None
    for t in range(tiles):
        row = push_ref[column, t : t + 1, :]
        term = jnp.where(slot == tb_ref[t, column], row, 0.0)
        acc = term if acc is None else acc + term
    return acc


def sweep_kernel(n_contact, n_body, last, *refs):
    gx, gy = contact_groups(n_contact)
    if last:
        (tb_ref, push_ref,
         tot_out,
         own_buf, later_buf, recv3, xbuf, ybuf, tot_buf,
         s_sem, r_sem, sx_sem, rx_sem, sy_sem, ry_sem) = refs
    else:
        (tb_ref, push_ref, vfree_ref, imass_ref,
         rows_out,
         own_buf, later_buf, recv3, xbuf, ybuf, vel_buf, vel_next, velf, rows_buf,
         s_sem, r_sem, sx_sem, rx_sem, sy_sem, ry_sem) = refs
    blocks = own_buf.shape[0]
    width = own_buf.shape[1]
    half = blocks // 2
    c = lax.axis_index("contact")
    b = lax.axis_index("body")
    core = lax.rem(c, 2)
    x = lax.rem(c // 2, gx)
    y = c // (2 * gx)
    mate = c + 1 - 2 * core
    up = lax.rem(b + 1, n_body)
    down = lax.rem(b + n_body - 1, n_body)
    x_peers = [(y * gx + lax.rem(x + j, gx)) * 2 + core for j in range(1, gx)]
    y_peers = [(lax.rem(y + j, gy) * gx + x) * 2 + core for j in range(1, gy)]

    greet = [(mate, b), (c, up), (mate, up), (c, down), (mate, down)]
    greet += [(p, b) for p in x_peers] + [(p, b) for p in y_peers]
    barrier = pltpu.get_barrier_semaphore()
    for dev in greet:
        pl.semaphore_signal(barrier, inc=1, device_id=dev, device_id_type=MESH)
    pl.semaphore_wait(barrier, len(greet))

    def remote(src, dst, send, recv, dev):
        return pltpu.make_async_remote_copy(
            src_ref=src, dst_ref=dst, send_sem=send, recv_sem=recv,
            device_id=dev, device_id_type=MESH,
        )

    mine = pl.ds(pl.multiple_of(core * half, half), half)
    theirs = pl.ds(pl.multiple_of((1 - core) * half, half), half)
    sent = []
    later_buf[...] = scatter_rows(tb_ref, 1, push_ref, blocks)
    for k, (src, dev) in enumerate(((later_buf.at[mine], (c, up)), (later_buf.at[theirs], (mate, up)))):
        cp = remote(src, recv3.at[1 + k], s_sem.at[1 + k], r_sem.at[1 + k], dev)
        cp.start()
        sent.append(cp)
    own_buf[...] = scatter_rows(tb_ref, 0, push_ref, blocks)
    cp = remote(own_buf.at[theirs], recv3.at[0], s_sem.at[0], r_sem.at[0], (mate, b))
    cp.start()
    sent.append(cp)
    for k, dev in enumerate(((mate, b), (c, down), (mate, down))):
        remote(own_buf.at[mine], recv3.at[k], s_sem.at[k], r_sem.at[k], dev).wait_recv()
    part = own_buf[mine] + recv3[0] + recv3[1] + recv3[2]

    for buf, pos, peers, size, ssem, rsem in (
        (xbuf, x, x_peers, gx, sx_sem, rx_sem),
        (ybuf, y, y_peers, gy, sy_sem, ry_sem),
    ):
        if size == 1:
            continue
        buf[pos] = part
        for j, p in enumerate(peers):
            cp = remote(buf.at[pos], buf.at[pos], ssem.at[j], rsem.at[pos], (p, b))
            cp.start()
            sent.append(cp)
        for j in range(1, size):
            src_pos = lax.rem(pos + size - j, size)
            remote(buf.at[src_pos], buf.at[src_pos], ssem.at[0], rsem.at[src_pos], (peers[-j], b)).wait_recv()
        part = buf[0]
        for g in range(1, size):
            part = part + buf[g]

    if last:
        tot_buf[mine] = part
        cp = remote(tot_buf.at[mine], tot_buf.at[mine], s_sem.at[3], r_sem.at[3], (mate, b))
        cp.start()
        sent.append(cp)
        remote(tot_buf.at[theirs], tot_buf.at[theirs], s_sem.at[3], r_sem.at[3], (mate, b)).wait_recv()
        tot_out[...] = tot_buf[...]
    else:
        vel = vfree_ref[mine] + imass_ref[mine] * part
        vel_buf[mine] = vel.astype(jnp.bfloat16)
        src = vel_buf.at[mine]
        for k, (dst, dev) in enumerate((
            (vel_buf.at[mine], (mate, b)),
            (vel_next.at[mine], (c, down)),
            (vel_next.at[mine], (mate, down)),
        )):
            cp = remote(src, dst, s_sem.at[3 + k], r_sem.at[3 + k], dev)
            cp.start()
            sent.append(cp)
        for k, (dst, dev) in enumerate((
            (vel_buf.at[theirs], (mate, b)),
            (vel_next.at[mine], (c, up)),
            (vel_next.at[theirs], (mate, up)),
        )):
            remote(src, dst, s_sem.at[3 + k], r_sem.at[3 + k], dev).wait_recv()
        velf[0] = vel_buf[...].astype(jnp.float32)
        velf[1] = vel_next[...].astype(jnp.float32)
        tiles = rows_buf.shape[1]
        for column in range(2):
            for t in range(tiles):
                rows_buf[column, pl.ds(t, 1), :] = velf[column, pl.ds(tb_ref[t, column], 1), :]
            rows_out[column] = rows_buf[column].astype(jnp.bfloat16)
    for cp in sent:
        cp.wait_send()


def sweep_exchange(tile_block, push, vel_free, inv_mass, n_contact, n_body, last):
    gx, gy = contact_groups(n_contact)
    blocks, width = vel_free.shape
    tiles = push.shape[1]
    half = blocks // 2
    vspec = pl.BlockSpec(memory_space=pltpu.VMEM)
    sspec = pl.BlockSpec(memory_space=pltpu.SMEM)
    if last:
        args = [tile_block, push]
        out_shape = jax.ShapeDtypeStruct((blocks, width), jnp.float32)
        tail = [pltpu.VMEM((blocks, width), jnp.float32)]
    else:
        args = [tile_block, push, vel_free, inv_mass]
        out_shape = jax.ShapeDtypeStruct((2, tiles, width), jnp.bfloat16)
        tail = [
            pltpu.VMEM((blocks, width), jnp.bfloat16),
            pltpu.VMEM((blocks, width), jnp.bfloat16),
            pltpu.VMEM((2, blocks, width), jnp.float32),
            pltpu.VMEM((2, tiles, width), jnp.float32),
        ]
    scratch = [
        pltpu.VMEM((blocks, width), jnp.float32),
        pltpu.VMEM((blocks, width), jnp.float32),
        pltpu.VMEM((3, half, width), jnp.float32),
        pltpu.VMEM((gx, half, width), jnp.float32),
        pltpu.VMEM((gy, half, width), jnp.float32),
        *tail,
        pltpu.SemaphoreType.DMA((6,)),
        pltpu.SemaphoreType.DMA((6,)),
        pltpu.SemaphoreType.DMA((max(gx - 1, 1),)),
        pltpu.SemaphoreType.DMA((gx,)),
        pltpu.SemaphoreType.DMA((max(gy - 1, 1),)),
        pltpu.SemaphoreType.DMA((gy,)),
    ]
    return pl.pallas_call(
        functools.partial(sweep_kernel, n_contact, n_body, last),
        out_shape=out_shape,
        in_specs=[sspec] + [vspec] * (len(args) - 1),
        out_specs=vspec,
        scratch_shapes=scratch,
        compiler_params=pltpu.CompilerParams(
            collective_id=1 if last else 0, has_side_effects=True
        ),
    )(*args)


def per_device(
    n_contact, n_body,
    jacobian, tile_block, tile_count, vel_free, inv_mass, bias, step_scale, friction, impulse_start,
):
    tiles_here = jacobian.shape[0]
    contacts = friction.shape[1]
    order = jnp.arange(tiles_here, dtype=jnp.int32)
    mask = (order < tile_count[0]).astype(jnp.float32)[:, None]

    def pushes(lam):
        lamb = lam.astype(jnp.bfloat16)
        return jnp.einsum("tkbc,tc->ktb", jacobian, lamb, preferred_element_type=jnp.float32)

    lam = impulse_start * mask
    for sweep in range(ITERS):
        rows = sweep_exchange(tile_block, pushes(lam), vel_free, inv_mass, n_contact, n_body, False)
        rel = jnp.einsum("tkbc,ktb->tc", jacobian, rows, preferred_element_type=jnp.float32) + bias
        lam = project(lam - step_scale * rel, friction, contacts) * mask
    total = sweep_exchange(tile_block, pushes(lam), vel_free, inv_mass, n_contact, n_body, True)
    velocity = vel_free + inv_mass * total
    return (lam, velocity)


def solution(mesh):
    n_contact = mesh.shape["contact"]
    n_body = mesh.shape["body"]
    placed = (
        P(("contact", "body"), None, None, None),
        P(("contact", "body"), None),
        P(("contact", "body")),
        P("body", None),
        P("body", None),
        P(("contact", "body"), None),
        P(("contact", "body"), None),
        P(("contact", "body"), None),
        P(("contact", "body"), None),
    )
    return jax.shard_map(
        functools.partial(per_device, n_contact, n_body),
        mesh=mesh,
        in_specs=placed,
        out_specs=(P(("contact", "body"), None), P("body", None)),
        check_vma=False,
    )
```

```python
import functools
import math

import jax
import jax.numpy as jnp
from jax import lax
from jax.experimental import pallas as pl
from jax.experimental.pallas import tpu as pltpu
from jax.sharding import PartitionSpec as P

ITERS = 2
MESH = pl.DeviceIdType.MESH


def project(trial, friction, contacts):
    normal = trial[:, :contacts]
    first = trial[:, contacts : 2 * contacts]
    second = trial[:, 2 * contacts :]
    tangent = jnp.sqrt(first * first + second * second)
    inside = tangent <= friction * normal
    below = friction * tangent <= -normal
    moved = (normal + friction * tangent) / (1.0 + friction * friction)
    safe = jnp.where(inside | below, 1.0, tangent)
    factor = jnp.where(inside, 1.0, jnp.where(below, 0.0, friction * moved / safe))
    new_normal = jnp.where(inside, normal, jnp.where(below, 0.0, moved))
    return jnp.concatenate([new_normal, first * factor, second * factor], axis=1)


def contact_groups(n_contact):
    rest = n_contact // 2
    gy = 1
    for d in range(1, int(math.isqrt(rest)) + 1):
        if rest % d == 0:
            gy = d
    return rest // gy, gy


def scatter_rows(tb_ref, column, push_ref, blocks):
    tiles = push_ref.shape[1]
    width = push_ref.shape[2]
    slot = lax.broadcasted_iota(jnp.int32, (blocks, width), 0)
    acc = None
    for t in range(tiles):
        row = push_ref[column, t : t + 1, :]
        term = jnp.where(slot == tb_ref[column, t], row, 0.0)
        acc = term if acc is None else acc + term
    return acc


def sweep_kernel(n_contact, n_body, last, *refs):
    gx, gy = contact_groups(n_contact)
    if last:
        (tb_ref, push_ref,
         tot_out,
         own_buf, later_buf, recv3, gbuf, tot_buf,
         s_sem, r_sem, gs_sem, gr_sem) = refs
    else:
        (tb_ref, push_ref, vfree_ref, imass_ref,
         rows_out,
         own_buf, later_buf, recv3, gbuf, vel_buf, vel_next, velf, rows_buf,
         s_sem, r_sem, gs_sem, gr_sem) = refs
    blocks = own_buf.shape[0]
    width = own_buf.shape[1]
    half = blocks // 2
    c = lax.axis_index("contact")
    b = lax.axis_index("body")
    core = lax.rem(c, 2)
    x = lax.rem(c // 2, gx)
    y = c // (2 * gx)
    mate = c + 1 - 2 * core
    up = lax.rem(b + 1, n_body)
    down = lax.rem(b + n_body - 1, n_body)
    group = gx * gy
    q = c // 2
    peers = [lax.rem(q + j, group) * 2 + core for j in range(1, group)]

    greet = [(mate, b), (c, up), (mate, up), (c, down), (mate, down)]
    greet += [(p, b) for p in peers]
    barrier = pltpu.get_barrier_semaphore()
    for dev in greet:
        pl.semaphore_signal(barrier, inc=1, device_id=dev, device_id_type=MESH)
    pl.semaphore_wait(barrier, len(greet))

    def remote(src, dst, send, recv, dev):
        return pltpu.make_async_remote_copy(
            src_ref=src, dst_ref=dst, send_sem=send, recv_sem=recv,
            device_id=dev, device_id_type=MESH,
        )

    mine = pl.ds(pl.multiple_of(core * half, half), half)
    theirs = pl.ds(pl.multiple_of((1 - core) * half, half), half)
    sent = []
    later_buf[...] = scatter_rows(tb_ref, 1, push_ref, blocks)
    for k, (src, dev) in enumerate(((later_buf.at[mine], (c, up)), (later_buf.at[theirs], (mate, up)))):
        cp = remote(src, recv3.at[1 + k], s_sem.at[1 + k], r_sem.at[1 + k], dev)
        cp.start()
        sent.append(cp)
    own_buf[...] = scatter_rows(tb_ref, 0, push_ref, blocks)
    cp = remote(own_buf.at[theirs], recv3.at[0], s_sem.at[0], r_sem.at[0], (mate, b))
    cp.start()
    sent.append(cp)
    for k, dev in enumerate(((mate, b), (c, down), (mate, down))):
        remote(own_buf.at[mine], recv3.at[k], s_sem.at[k], r_sem.at[k], dev).wait_recv()
    part = own_buf[mine] + recv3[0] + recv3[1] + recv3[2]

    if group > 1:
        gbuf[q] = part
        for j, p in enumerate(peers):
            cp = remote(gbuf.at[q], gbuf.at[q], gs_sem.at[j], gr_sem.at[q], (p, b))
            cp.start()
            sent.append(cp)
        for j in range(1, group):
            src_q = lax.rem(q + group - j, group)
            remote(gbuf.at[src_q], gbuf.at[src_q], gs_sem.at[0], gr_sem.at[src_q], (peers[-j], b)).wait_recv()
        part = gbuf[0]
        for g in range(1, group):
            part = part + gbuf[g]

    if last:
        tot_buf[mine] = part
        cp = remote(tot_buf.at[mine], tot_buf.at[mine], s_sem.at[3], r_sem.at[3], (mate, b))
        cp.start()
        sent.append(cp)
        remote(tot_buf.at[theirs], tot_buf.at[theirs], s_sem.at[3], r_sem.at[3], (mate, b)).wait_recv()
        tot_out[...] = tot_buf[...]
    else:
        vel = vfree_ref[mine] + imass_ref[mine] * part
        vel_buf[mine] = vel.astype(jnp.bfloat16)
        src = vel_buf.at[mine]
        for k, (dst, dev) in enumerate((
            (vel_buf.at[mine], (mate, b)),
            (vel_next.at[mine], (c, down)),
            (vel_next.at[mine], (mate, down)),
        )):
            cp = remote(src, dst, s_sem.at[3 + k], r_sem.at[3 + k], dev)
            cp.start()
            sent.append(cp)
        for k, (dst, dev) in enumerate((
            (vel_buf.at[theirs], (mate, b)),
            (vel_next.at[mine], (c, up)),
            (vel_next.at[theirs], (mate, up)),
        )):
            remote(src, dst, s_sem.at[3 + k], r_sem.at[3 + k], dev).wait_recv()
        velf[0] = vel_buf[...].astype(jnp.float32)
        velf[1] = vel_next[...].astype(jnp.float32)
        tiles = rows_buf.shape[1]
        for column in range(2):
            for t in range(tiles):
                rows_buf[column, pl.ds(t, 1), :] = velf[column, pl.ds(tb_ref[column, t], 1), :]
            rows_out[column] = rows_buf[column].astype(jnp.bfloat16)
    for cp in sent:
        cp.wait_send()


def sweep_exchange(tile_block, push, vel_free, inv_mass, n_contact, n_body, last):
    gx, gy = contact_groups(n_contact)
    blocks, width = vel_free.shape
    tiles = push.shape[1]
    half = blocks // 2
    vspec = pl.BlockSpec(memory_space=pltpu.VMEM)
    sspec = pl.BlockSpec(memory_space=pltpu.SMEM)
    if last:
        args = [tile_block, push]
        out_shape = jax.ShapeDtypeStruct((blocks, width), jnp.float32)
        tail = [pltpu.VMEM((blocks, width), jnp.float32)]
    else:
        args = [tile_block, push, vel_free, inv_mass]
        out_shape = jax.ShapeDtypeStruct((2, tiles, width), jnp.bfloat16)
        tail = [
            pltpu.VMEM((blocks, width), jnp.bfloat16),
            pltpu.VMEM((blocks, width), jnp.bfloat16),
            pltpu.VMEM((2, blocks, width), jnp.float32),
            pltpu.VMEM((2, tiles, width), jnp.float32),
        ]
    scratch = [
        pltpu.VMEM((blocks, width), jnp.float32),
        pltpu.VMEM((blocks, width), jnp.float32),
        pltpu.VMEM((3, half, width), jnp.float32),
        pltpu.VMEM((gx * gy, half, width), jnp.float32),
        *tail,
        pltpu.SemaphoreType.DMA((6,)),
        pltpu.SemaphoreType.DMA((6,)),
        pltpu.SemaphoreType.DMA((max(gx * gy - 1, 1),)),
        pltpu.SemaphoreType.DMA((gx * gy,)),
    ]
    return pl.pallas_call(
        functools.partial(sweep_kernel, n_contact, n_body, last),
        out_shape=out_shape,
        in_specs=[sspec] + [vspec] * (len(args) - 1),
        out_specs=vspec,
        scratch_shapes=scratch,
        compiler_params=pltpu.CompilerParams(
            collective_id=1 if last else 0, has_side_effects=True
        ),
    )(*args)


def per_device(
    n_contact, n_body,
    jacobian, tile_block, tile_count, vel_free, inv_mass, bias, step_scale, friction, impulse_start,
):
    tiles_here = jacobian.shape[0]
    contacts = friction.shape[1]
    order = jnp.arange(tiles_here, dtype=jnp.int32)
    mask = (order < tile_count[0]).astype(jnp.float32)[:, None]

    def pushes(lam):
        lamb = lam.astype(jnp.bfloat16)
        return jnp.einsum("tkbc,tc->ktb", jacobian, lamb, preferred_element_type=jnp.float32)

    lam = impulse_start * mask
    for sweep in range(ITERS):
        rows = sweep_exchange(tile_block.T, pushes(lam), vel_free, inv_mass, n_contact, n_body, False)
        rel = jnp.einsum("tkbc,ktb->tc", jacobian, rows, preferred_element_type=jnp.float32) + bias
        lam = project(lam - step_scale * rel, friction, contacts) * mask
    total = sweep_exchange(tile_block.T, pushes(lam), vel_free, inv_mass, n_contact, n_body, True)
    velocity = vel_free + inv_mass * total
    return (lam, velocity)


def solution(mesh):
    n_contact = mesh.shape["contact"]
    n_body = mesh.shape["body"]
    placed = (
        P(("contact", "body"), None, None, None),
        P(("contact", "body"), None),
        P(("contact", "body")),
        P("body", None),
        P("body", None),
        P(("contact", "body"), None),
        P(("contact", "body"), None),
        P(("contact", "body"), None),
        P(("contact", "body"), None),
    )
    return jax.shard_map(
        functools.partial(per_device, n_contact, n_body),
        mesh=mesh,
        in_specs=placed,
        out_specs=(P(("contact", "body"), None), P("body", None)),
        check_vma=False,
    )
```

```python
import functools
import math

import jax
import jax.numpy as jnp
from jax import lax
from jax.experimental import pallas as pl
from jax.experimental.pallas import tpu as pltpu
from jax.sharding import PartitionSpec as P

ITERS = 2
MESH = pl.DeviceIdType.MESH


def project(trial, friction, contacts):
    normal = trial[:, :contacts]
    first = trial[:, contacts : 2 * contacts]
    second = trial[:, 2 * contacts :]
    tangent = jnp.sqrt(first * first + second * second)
    inside = tangent <= friction * normal
    below = friction * tangent <= -normal
    moved = (normal + friction * tangent) / (1.0 + friction * friction)
    safe = jnp.where(inside | below, 1.0, tangent)
    factor = jnp.where(inside, 1.0, jnp.where(below, 0.0, friction * moved / safe))
    new_normal = jnp.where(inside, normal, jnp.where(below, 0.0, moved))
    return jnp.concatenate([new_normal, first * factor, second * factor], axis=1)


def contact_groups(n_contact):
    rest = n_contact // 2
    gy = 1
    for d in range(1, int(math.isqrt(rest)) + 1):
        if rest % d == 0:
            gy = d
    return rest // gy, gy


def scatter_rows(tb_ref, column, push_ref, blocks):
    tiles = push_ref.shape[1]
    width = push_ref.shape[2]
    slot = lax.broadcasted_iota(jnp.int32, (blocks, width), 0)
    acc = None
    for t in range(tiles):
        row = push_ref[column, t : t + 1, :]
        term = jnp.where(slot == tb_ref[column, t], row, 0.0)
        acc = term if acc is None else acc + term
    return acc


def sweep_kernel(n_contact, n_body, last, *refs):
    gx, gy = contact_groups(n_contact)
    if last:
        (tb_ref, push_ref,
         tot_out,
         own_buf, later_buf, recv3, xbuf, ybuf, tot_buf,
         s_sem, r_sem, sx_sem, rx_sem, sy_sem, ry_sem) = refs
    else:
        (tb_ref, push_ref, vfree_ref, imass_ref,
         rows_out,
         own_buf, later_buf, recv3, xbuf, ybuf, vel_buf, vel_next, velf, rows_buf,
         s_sem, r_sem, sx_sem, rx_sem, sy_sem, ry_sem) = refs
    blocks = own_buf.shape[0]
    width = own_buf.shape[1]
    half = blocks // 2
    c = lax.axis_index("contact")
    b = lax.axis_index("body")
    core = lax.rem(c, 2)
    x = lax.rem(c // 2, gx)
    y = c // (2 * gx)
    mate = c + 1 - 2 * core
    up = lax.rem(b + 1, n_body)
    down = lax.rem(b + n_body - 1, n_body)
    x_peers = [(y * gx + lax.rem(x + j, gx)) * 2 + core for j in range(1, gx)]
    y_peers = [(lax.rem(y + j, gy) * gx + x) * 2 + core for j in range(1, gy)]

    greet = [(mate, b), (c, up), (mate, up), (c, down), (mate, down)]
    greet += [(p, b) for p in x_peers] + [(p, b) for p in y_peers]
    barrier = pltpu.get_barrier_semaphore()
    for dev in greet:
        pl.semaphore_signal(barrier, inc=1, device_id=dev, device_id_type=MESH)
    pl.semaphore_wait(barrier, len(greet))

    def remote(src, dst, send, recv, dev):
        return pltpu.make_async_remote_copy(
            src_ref=src, dst_ref=dst, send_sem=send, recv_sem=recv,
            device_id=dev, device_id_type=MESH,
        )

    mine = pl.ds(pl.multiple_of(core * half, half), half)
    theirs = pl.ds(pl.multiple_of((1 - core) * half, half), half)
    sent = []
    later_buf[...] = scatter_rows(tb_ref, 1, push_ref, blocks)
    for k, (src, dev) in enumerate(((later_buf.at[mine], (c, up)), (later_buf.at[theirs], (mate, up)))):
        cp = remote(src, recv3.at[1 + k], s_sem.at[1 + k], r_sem.at[1 + k], dev)
        cp.start()
        sent.append(cp)
    own_buf[...] = scatter_rows(tb_ref, 0, push_ref, blocks)
    cp = remote(own_buf.at[theirs], recv3.at[0], s_sem.at[0], r_sem.at[0], (mate, b))
    cp.start()
    sent.append(cp)
    for k, dev in enumerate(((mate, b), (c, down), (mate, down))):
        remote(own_buf.at[mine], recv3.at[k], s_sem.at[k], r_sem.at[k], dev).wait_recv()
    part = own_buf[mine] + recv3[0] + recv3[1] + recv3[2]

    for buf, pos, peers, size, ssem, rsem in (
        (xbuf, x, x_peers, gx, sx_sem, rx_sem),
        (ybuf, y, y_peers, gy, sy_sem, ry_sem),
    ):
        if size == 1:
            continue
        buf[pos] = part
        for j, p in enumerate(peers):
            cp = remote(buf.at[pos], buf.at[pos], ssem.at[j], rsem.at[pos], (p, b))
            cp.start()
            sent.append(cp)
        for j in range(1, size):
            src_pos = lax.rem(pos + size - j, size)
            remote(buf.at[src_pos], buf.at[src_pos], ssem.at[0], rsem.at[src_pos], (peers[-j], b)).wait_recv()
        part = buf[0]
        for g in range(1, size):
            part = part + buf[g]

    if last:
        tot_buf[mine] = part
        cp = remote(tot_buf.at[mine], tot_buf.at[mine], s_sem.at[3], r_sem.at[3], (mate, b))
        cp.start()
        sent.append(cp)
        remote(tot_buf.at[theirs], tot_buf.at[theirs], s_sem.at[3], r_sem.at[3], (mate, b)).wait_recv()
        tot_out[...] = tot_buf[...]
    else:
        vel = vfree_ref[mine] + imass_ref[mine] * part
        vel_buf[mine] = vel.astype(jnp.bfloat16)
        src = vel_buf.at[mine]
        for k, (dst, dev) in enumerate((
            (vel_buf.at[mine], (mate, b)),
            (vel_next.at[mine], (c, down)),
            (vel_next.at[mine], (mate, down)),
        )):
            cp = remote(src, dst, s_sem.at[3 + k], r_sem.at[3 + k], dev)
            cp.start()
            sent.append(cp)
        for k, (dst, dev) in enumerate((
            (vel_buf.at[theirs], (mate, b)),
            (vel_next.at[mine], (c, up)),
            (vel_next.at[theirs], (mate, up)),
        )):
            remote(src, dst, s_sem.at[3 + k], r_sem.at[3 + k], dev).wait_recv()
        velf[0] = vel_buf[...].astype(jnp.float32)
        velf[1] = vel_next[...].astype(jnp.float32)
        tiles = rows_buf.shape[1]
        for column in range(2):
            for t in range(tiles):
                rows_buf[column, pl.ds(t, 1), :] = velf[column, pl.ds(tb_ref[column, t], 1), :]
            rows_out[column] = rows_buf[column].astype(jnp.bfloat16)
    for cp in sent:
        cp.wait_send()


def sweep_exchange(tile_block, push, vel_free, inv_mass, n_contact, n_body, last):
    gx, gy = contact_groups(n_contact)
    blocks, width = vel_free.shape
    tiles = push.shape[1]
    half = blocks // 2
    vspec = pl.BlockSpec(memory_space=pltpu.VMEM)
    sspec = pl.BlockSpec(memory_space=pltpu.SMEM)
    if last:
        args = [tile_block, push]
        out_shape = jax.ShapeDtypeStruct((blocks, width), jnp.float32)
        tail = [pltpu.VMEM((blocks, width), jnp.float32)]
    else:
        args = [tile_block, push, vel_free, inv_mass]
        out_shape = jax.ShapeDtypeStruct((2, tiles, width), jnp.bfloat16)
        tail = [
            pltpu.VMEM((blocks, width), jnp.bfloat16),
            pltpu.VMEM((blocks, width), jnp.bfloat16),
            pltpu.VMEM((2, blocks, width), jnp.float32),
            pltpu.VMEM((2, tiles, width), jnp.float32),
        ]
    scratch = [
        pltpu.VMEM((blocks, width), jnp.float32),
        pltpu.VMEM((blocks, width), jnp.float32),
        pltpu.VMEM((3, half, width), jnp.float32),
        pltpu.VMEM((gx, half, width), jnp.float32),
        pltpu.VMEM((gy, half, width), jnp.float32),
        *tail,
        pltpu.SemaphoreType.DMA((6,)),
        pltpu.SemaphoreType.DMA((6,)),
        pltpu.SemaphoreType.DMA((max(gx - 1, 1),)),
        pltpu.SemaphoreType.DMA((gx,)),
        pltpu.SemaphoreType.DMA((max(gy - 1, 1),)),
        pltpu.SemaphoreType.DMA((gy,)),
    ]
    return pl.pallas_call(
        functools.partial(sweep_kernel, n_contact, n_body, last),
        out_shape=out_shape,
        in_specs=[sspec] + [vspec] * (len(args) - 1),
        out_specs=vspec,
        scratch_shapes=scratch,
        compiler_params=pltpu.CompilerParams(
            collective_id=1 if last else 0, has_side_effects=True
        ),
    )(*args)


def per_device(
    n_contact, n_body,
    jacobian, tile_block, tile_count, vel_free, inv_mass, bias, step_scale, friction, impulse_start,
):
    tiles_here = jacobian.shape[0]
    contacts = friction.shape[1]
    order = jnp.arange(tiles_here, dtype=jnp.int32)
    mask = (order < tile_count[0]).astype(jnp.float32)[:, None]

    def pushes(lam):
        lamb = lam.astype(jnp.bfloat16)
        return jnp.einsum("tkbc,tc->ktb", jacobian, lamb, preferred_element_type=jnp.float32)

    lam = impulse_start * mask
    for sweep in range(ITERS):
        rows = sweep_exchange(tile_block.T, pushes(lam), vel_free, inv_mass, n_contact, n_body, False)
        rel = jnp.einsum("tkbc,ktb->tc", jacobian, rows, preferred_element_type=jnp.float32) + bias
        lam = project(lam - step_scale * rel, friction, contacts) * mask
    total = sweep_exchange(tile_block.T, pushes(lam), vel_free, inv_mass, n_contact, n_body, True)
    velocity = vel_free + inv_mass * total
    return (lam, velocity)


def solution(mesh):
    n_contact = mesh.shape["contact"]
    n_body = mesh.shape["body"]
    placed = (
        P(("contact", "body"), None, None, None),
        P(("contact", "body"), None),
        P(("contact", "body")),
        P("body", None),
        P("body", None),
        P(("contact", "body"), None),
        P(("contact", "body"), None),
        P(("contact", "body"), None),
        P(("contact", "body"), None),
    )
    return jax.shard_map(
        functools.partial(per_device, n_contact, n_body),
        mesh=mesh,
        in_specs=placed,
        out_specs=(P(("contact", "body"), None), P("body", None)),
        check_vma=False,
    )
```

```python
import functools
import math

import jax
import jax.numpy as jnp
from jax import lax
from jax.experimental import pallas as pl
from jax.experimental.pallas import tpu as pltpu
from jax.sharding import PartitionSpec as P

ITERS = 2
MESH = pl.DeviceIdType.MESH


def project(trial, friction, contacts):
    normal = trial[:, :contacts]
    first = trial[:, contacts : 2 * contacts]
    second = trial[:, 2 * contacts :]
    tangent = jnp.sqrt(first * first + second * second)
    inside = tangent <= friction * normal
    below = friction * tangent <= -normal
    moved = (normal + friction * tangent) / (1.0 + friction * friction)
    safe = jnp.where(inside | below, 1.0, tangent)
    factor = jnp.where(inside, 1.0, jnp.where(below, 0.0, friction * moved / safe))
    new_normal = jnp.where(inside, normal, jnp.where(below, 0.0, moved))
    return jnp.concatenate([new_normal, first * factor, second * factor], axis=1)


def contact_groups(n_contact):
    rest = n_contact // 2
    gy = 1
    for d in range(1, int(math.isqrt(rest)) + 1):
        if rest % d == 0:
            gy = d
    return rest // gy, gy


def scatter_rows(tb_ref, column, push_ref, blocks):
    tiles = push_ref.shape[1]
    width = push_ref.shape[2]
    slot = lax.broadcasted_iota(jnp.int32, (blocks, width), 0)
    acc = None
    for t in range(tiles):
        row = push_ref[column, t : t + 1, :]
        term = jnp.where(slot == tb_ref[column, t], row, 0.0)
        acc = term if acc is None else acc + term
    return acc


def sweep_kernel(n_contact, n_body, last, *refs):
    gx, gy = contact_groups(n_contact)
    if last:
        (tb_ref, push_ref,
         tot_out,
         own_buf, later_buf, recv3, xbuf, ybuf, tot_buf,
         s_sem, r_sem, sx_sem, rx_sem, sy_sem, ry_sem) = refs
    else:
        (tb_ref, push_ref, vfree_ref, imass_ref,
         rows_out,
         own_buf, later_buf, recv3, xbuf, ybuf, vel_buf, vel_next, velf, rows_buf,
         s_sem, r_sem, sx_sem, rx_sem, sy_sem, ry_sem) = refs
    blocks = own_buf.shape[0]
    width = own_buf.shape[1]
    half = blocks // 2
    c = lax.axis_index("contact")
    b = lax.axis_index("body")
    core = lax.rem(c, 2)
    x = lax.rem(c // 2, gx)
    y = c // (2 * gx)
    mate = c + 1 - 2 * core
    up = lax.rem(b + 1, n_body)
    down = lax.rem(b + n_body - 1, n_body)
    x_peers = [(y * gx + lax.rem(x + j, gx)) * 2 + core for j in range(1, gx)]
    y_peers = [(lax.rem(y + j, gy) * gx + x) * 2 + core for j in range(1, gy)]

    greet = [(mate, b), (c, up), (mate, up), (c, down), (mate, down)]
    greet += [(p, b) for p in x_peers] + [(p, b) for p in y_peers]
    barrier = pltpu.get_barrier_semaphore()
    for dev in greet:
        pl.semaphore_signal(barrier, inc=1, device_id=dev, device_id_type=MESH)
    pl.semaphore_wait(barrier, len(greet))

    def remote(src, dst, send, recv, dev):
        return pltpu.make_async_remote_copy(
            src_ref=src, dst_ref=dst, send_sem=send, recv_sem=recv,
            device_id=dev, device_id_type=MESH,
        )

    mine = pl.ds(pl.multiple_of(core * half, half), half)
    theirs = pl.ds(pl.multiple_of((1 - core) * half, half), half)
    sent = []
    later_buf[...] = scatter_rows(tb_ref, 1, push_ref, blocks)
    for k, (src, dev) in enumerate(((later_buf.at[mine], (c, up)), (later_buf.at[theirs], (mate, up)))):
        cp = remote(src, recv3.at[1 + k], s_sem.at[1 + k], r_sem.at[1 + k], dev)
        cp.start()
        sent.append(cp)
    own_buf[...] = scatter_rows(tb_ref, 0, push_ref, blocks)
    cp = remote(own_buf.at[theirs], recv3.at[0], s_sem.at[0], r_sem.at[0], (mate, b))
    cp.start()
    sent.append(cp)
    for k, dev in enumerate(((mate, b), (c, down), (mate, down))):
        remote(own_buf.at[mine], recv3.at[k], s_sem.at[k], r_sem.at[k], dev).wait_recv()
    part = own_buf[mine] + recv3[0] + recv3[1] + recv3[2]

    for buf, pos, peers, size, ssem, rsem in (
        (xbuf, x, x_peers, gx, sx_sem, rx_sem),
        (ybuf, y, y_peers, gy, sy_sem, ry_sem),
    ):
        if size == 1:
            continue
        buf[pos] = part
        for j, p in enumerate(peers):
            cp = remote(buf.at[pos], buf.at[pos], ssem.at[j], rsem.at[pos], (p, b))
            cp.start()
            sent.append(cp)
        for j in range(1, size):
            src_pos = lax.rem(pos + size - j, size)
            remote(buf.at[src_pos], buf.at[src_pos], ssem.at[0], rsem.at[src_pos], (peers[-j], b)).wait_recv()
        part = buf[0]
        for g in range(1, size):
            part = part + buf[g]

    if last:
        tot_buf[mine] = part
        cp = remote(tot_buf.at[mine], tot_buf.at[mine], s_sem.at[3], r_sem.at[3], (mate, b))
        cp.start()
        sent.append(cp)
        remote(tot_buf.at[theirs], tot_buf.at[theirs], s_sem.at[3], r_sem.at[3], (mate, b)).wait_recv()
        tot_out[...] = tot_buf[...]
    else:
        vel = vfree_ref[mine] + imass_ref[mine] * part
        vel_buf[mine] = vel.astype(jnp.bfloat16)
        src = vel_buf.at[mine]
        for k, (dst, dev) in enumerate((
            (vel_buf.at[mine], (mate, b)),
            (vel_next.at[mine], (c, down)),
            (vel_next.at[mine], (mate, down)),
        )):
            cp = remote(src, dst, s_sem.at[3 + k], r_sem.at[3 + k], dev)
            cp.start()
            sent.append(cp)
        for k, (dst, dev) in enumerate((
            (vel_buf.at[theirs], (mate, b)),
            (vel_next.at[mine], (c, up)),
            (vel_next.at[theirs], (mate, up)),
        )):
            remote(src, dst, s_sem.at[3 + k], r_sem.at[3 + k], dev).wait_recv()
        velf[0] = vel_buf[...].astype(jnp.float32)
        velf[1] = vel_next[...].astype(jnp.float32)
        tiles = rows_buf.shape[1]
        for column in range(2):
            for t in range(tiles):
                rows_buf[column, pl.ds(t, 1), :] = velf[column, pl.ds(tb_ref[column, t], 1), :]
            rows_out[column] = rows_buf[column].astype(jnp.bfloat16)
    for cp in sent:
        cp.wait_send()


def sweep_exchange(tile_block, push, vel_free, inv_mass, n_contact, n_body, last):
    gx, gy = contact_groups(n_contact)
    blocks, width = vel_free.shape
    tiles = push.shape[1]
    half = blocks // 2
    vspec = pl.BlockSpec(memory_space=pltpu.VMEM)
    sspec = pl.BlockSpec(memory_space=pltpu.SMEM)
    if last:
        args = [tile_block, push]
        out_shape = jax.ShapeDtypeStruct((blocks, width), jnp.float32)
        tail = [pltpu.VMEM((blocks, width), jnp.float32)]
    else:
        args = [tile_block, push, vel_free, inv_mass]
        out_shape = jax.ShapeDtypeStruct((2, tiles, width), jnp.bfloat16)
        tail = [
            pltpu.VMEM((blocks, width), jnp.bfloat16),
            pltpu.VMEM((blocks, width), jnp.bfloat16),
            pltpu.VMEM((2, blocks, width), jnp.float32),
            pltpu.VMEM((2, tiles, width), jnp.float32),
        ]
    scratch = [
        pltpu.VMEM((blocks, width), jnp.float32),
        pltpu.VMEM((blocks, width), jnp.float32),
        pltpu.VMEM((3, half, width), jnp.float32),
        pltpu.VMEM((gx, half, width), jnp.float32),
        pltpu.VMEM((gy, half, width), jnp.float32),
        *tail,
        pltpu.SemaphoreType.DMA((6,)),
        pltpu.SemaphoreType.DMA((6,)),
        pltpu.SemaphoreType.DMA((max(gx - 1, 1),)),
        pltpu.SemaphoreType.DMA((gx,)),
        pltpu.SemaphoreType.DMA((max(gy - 1, 1),)),
        pltpu.SemaphoreType.DMA((gy,)),
    ]
    return pl.pallas_call(
        functools.partial(sweep_kernel, n_contact, n_body, last),
        out_shape=out_shape,
        in_specs=[sspec] + [vspec] * (len(args) - 1),
        out_specs=vspec,
        scratch_shapes=scratch,
        compiler_params=pltpu.CompilerParams(
            collective_id=1 if last else 0, has_side_effects=True
        ),
    )(*args)


def dual_kernel(n_contact, n_body, *refs):
    gx, gy = contact_groups(n_contact)
    (tb_ref, push_ref, vfree_ref, imass_ref, vnext_ref,
     rows_out,
     own_buf, later_buf, recv6, xbuf, ybuf, vel_buf, velf, rows_buf,
     s_sem, r_sem, sx_sem, rx_sem, sy_sem, ry_sem) = refs
    blocks = own_buf.shape[0]
    width = own_buf.shape[1]
    half = blocks // 2
    c = lax.axis_index("contact")
    b = lax.axis_index("body")
    core = lax.rem(c, 2)
    x = lax.rem(c // 2, gx)
    y = c // (2 * gx)
    mate = c + 1 - 2 * core
    up = lax.rem(b + 1, n_body)
    down = lax.rem(b + n_body - 1, n_body)
    x_peers = [(y * gx + lax.rem(x + j, gx)) * 2 + core for j in range(1, gx)]
    y_peers = [(lax.rem(y + j, gy) * gx + x) * 2 + core for j in range(1, gy)]

    greet = [(mate, b), (c, up), (mate, up), (c, down), (mate, down)]
    greet += [(p, b) for p in x_peers] + [(p, b) for p in y_peers]
    barrier = pltpu.get_barrier_semaphore()
    for dev in greet:
        pl.semaphore_signal(barrier, inc=1, device_id=dev, device_id_type=MESH)
    pl.semaphore_wait(barrier, len(greet))

    def remote(src, dst, send, recv, dev):
        return pltpu.make_async_remote_copy(
            src_ref=src, dst_ref=dst, send_sem=send, recv_sem=recv,
            device_id=dev, device_id_type=MESH,
        )

    mine = pl.ds(pl.multiple_of(core * half, half), half)
    theirs = pl.ds(pl.multiple_of((1 - core) * half, half), half)
    sent = []
    later_buf[...] = scatter_rows(tb_ref, 1, push_ref, blocks)
    plan = (
        (later_buf.at[mine], (c, up)),
        (later_buf.at[theirs], (mate, up)),
        (later_buf.at[theirs], (mate, b)),
    )
    for k, (src, dev) in enumerate(plan):
        cp = remote(src, recv6.at[k], s_sem.at[k], r_sem.at[k], dev)
        cp.start()
        sent.append(cp)
    own_buf[...] = scatter_rows(tb_ref, 0, push_ref, blocks)
    plan = (
        (own_buf.at[mine], (c, down)),
        (own_buf.at[theirs], (mate, down)),
        (own_buf.at[theirs], (mate, b)),
    )
    for k, (src, dev) in enumerate(plan):
        cp = remote(src, recv6.at[3 + k], s_sem.at[3 + k], r_sem.at[3 + k], dev)
        cp.start()
        sent.append(cp)
    senders = ((c, down), (mate, down), (mate, b), (c, up), (mate, up), (mate, b))
    for k, dev in enumerate(senders):
        remote(own_buf.at[mine], recv6.at[k], s_sem.at[k], r_sem.at[k], dev).wait_recv()
    part = jnp.concatenate([
        own_buf[mine] + recv6[5] + recv6[0] + recv6[1],
        later_buf[mine] + recv6[2] + recv6[3] + recv6[4],
    ], axis=0)

    for buf, pos, peers, size, ssem, rsem in (
        (xbuf, x, x_peers, gx, sx_sem, rx_sem),
        (ybuf, y, y_peers, gy, sy_sem, ry_sem),
    ):
        if size == 1:
            continue
        buf[pos] = part
        for j, p in enumerate(peers):
            cp = remote(buf.at[pos], buf.at[pos], ssem.at[j], rsem.at[pos], (p, b))
            cp.start()
            sent.append(cp)
        for j in range(1, size):
            src_pos = lax.rem(pos + size - j, size)
            remote(buf.at[src_pos], buf.at[src_pos], ssem.at[0], rsem.at[src_pos], (peers[-j], b)).wait_recv()
        part = buf[0]
        for g in range(1, size):
            part = part + buf[g]

    vel_buf[0, mine] = (vfree_ref[mine] + imass_ref[mine] * part[:half]).astype(jnp.bfloat16)
    vel_buf[1, mine] = (vnext_ref[0, mine] + vnext_ref[1, mine] * part[half:]).astype(jnp.bfloat16)
    for k in range(2):
        cp = remote(vel_buf.at[k, mine], vel_buf.at[k, mine], s_sem.at[6 + k], r_sem.at[6 + k], (mate, b))
        cp.start()
        sent.append(cp)
    for k in range(2):
        remote(vel_buf.at[k, theirs], vel_buf.at[k, theirs], s_sem.at[6 + k], r_sem.at[6 + k], (mate, b)).wait_recv()
    velf[...] = vel_buf[...].astype(jnp.float32)
    tiles = rows_buf.shape[1]
    for column in range(2):
        for t in range(tiles):
            rows_buf[column, pl.ds(t, 1), :] = velf[column, pl.ds(tb_ref[column, t], 1), :]
        rows_out[column] = rows_buf[column].astype(jnp.bfloat16)
    for cp in sent:
        cp.wait_send()


def dual_exchange(tile_block, push, vel_free, inv_mass, vnext, n_contact, n_body):
    gx, gy = contact_groups(n_contact)
    blocks, width = vel_free.shape
    tiles = push.shape[1]
    half = blocks // 2
    vspec = pl.BlockSpec(memory_space=pltpu.VMEM)
    sspec = pl.BlockSpec(memory_space=pltpu.SMEM)
    scratch = [
        pltpu.VMEM((blocks, width), jnp.float32),
        pltpu.VMEM((blocks, width), jnp.float32),
        pltpu.VMEM((6, half, width), jnp.float32),
        pltpu.VMEM((gx, blocks, width), jnp.float32),
        pltpu.VMEM((gy, blocks, width), jnp.float32),
        pltpu.VMEM((2, blocks, width), jnp.bfloat16),
        pltpu.VMEM((2, blocks, width), jnp.float32),
        pltpu.VMEM((2, tiles, width), jnp.float32),
        pltpu.SemaphoreType.DMA((8,)),
        pltpu.SemaphoreType.DMA((8,)),
        pltpu.SemaphoreType.DMA((max(gx - 1, 1),)),
        pltpu.SemaphoreType.DMA((gx,)),
        pltpu.SemaphoreType.DMA((max(gy - 1, 1),)),
        pltpu.SemaphoreType.DMA((gy,)),
    ]
    return pl.pallas_call(
        functools.partial(dual_kernel, n_contact, n_body),
        out_shape=jax.ShapeDtypeStruct((2, tiles, width), jnp.bfloat16),
        in_specs=[sspec] + [vspec] * 4,
        out_specs=vspec,
        scratch_shapes=scratch,
        compiler_params=pltpu.CompilerParams(collective_id=2, has_side_effects=True),
    )(tile_block, push, vel_free, inv_mass, vnext)


def per_device(
    n_contact, n_body,
    jacobian, tile_block, tile_count, vel_free, inv_mass, bias, step_scale, friction, impulse_start,
):
    tiles_here = jacobian.shape[0]
    contacts = friction.shape[1]
    order = jnp.arange(tiles_here, dtype=jnp.int32)
    mask = (order < tile_count[0]).astype(jnp.float32)[:, None]

    def pushes(lam):
        lamb = lam.astype(jnp.bfloat16)
        return jnp.einsum("tkbc,tc->ktb", jacobian, lamb, preferred_element_type=jnp.float32)

    count = lax.axis_size("body")
    vnext = lax.ppermute(
        jnp.stack([vel_free, inv_mass]), "body",
        [(source, (source + count - 1) % count) for source in range(count)],
    )
    lam = impulse_start * mask
    for sweep in range(ITERS):
        rows = dual_exchange(tile_block.T, pushes(lam), vel_free, inv_mass, vnext, n_contact, n_body)
        rel = jnp.einsum("tkbc,ktb->tc", jacobian, rows, preferred_element_type=jnp.float32) + bias
        lam = project(lam - step_scale * rel, friction, contacts) * mask
    total = sweep_exchange(tile_block.T, pushes(lam), vel_free, inv_mass, n_contact, n_body, True)
    velocity = vel_free + inv_mass * total
    return (lam, velocity)


def solution(mesh):
    n_contact = mesh.shape["contact"]
    n_body = mesh.shape["body"]
    placed = (
        P(("contact", "body"), None, None, None),
        P(("contact", "body"), None),
        P(("contact", "body")),
        P("body", None),
        P("body", None),
        P(("contact", "body"), None),
        P(("contact", "body"), None),
        P(("contact", "body"), None),
        P(("contact", "body"), None),
    )
    return jax.shard_map(
        functools.partial(per_device, n_contact, n_body),
        mesh=mesh,
        in_specs=placed,
        out_specs=(P(("contact", "body"), None), P("body", None)),
        check_vma=False,
    )
```

```python
import functools
import math

import jax
import jax.numpy as jnp
from jax import lax
from jax.experimental import pallas as pl
from jax.experimental.pallas import tpu as pltpu
from jax.sharding import PartitionSpec as P

ITERS = 2
MESH = pl.DeviceIdType.MESH


def project(trial, friction, contacts):
    normal = trial[:, :contacts]
    first = trial[:, contacts : 2 * contacts]
    second = trial[:, 2 * contacts :]
    tangent = jnp.sqrt(first * first + second * second)
    inside = tangent <= friction * normal
    below = friction * tangent <= -normal
    moved = (normal + friction * tangent) / (1.0 + friction * friction)
    safe = jnp.where(inside | below, 1.0, tangent)
    factor = jnp.where(inside, 1.0, jnp.where(below, 0.0, friction * moved / safe))
    new_normal = jnp.where(inside, normal, jnp.where(below, 0.0, moved))
    return jnp.concatenate([new_normal, first * factor, second * factor], axis=1)


def contact_groups(n_contact):
    rest = n_contact // 2
    gy = 1
    for d in range(1, int(math.isqrt(rest)) + 1):
        if rest % d == 0:
            gy = d
    return rest // gy, gy


def scatter_rows(tb_ref, column, push_ref, blocks):
    tiles = push_ref.shape[1]
    width = push_ref.shape[2]
    slot = lax.broadcasted_iota(jnp.int32, (blocks, width), 0)
    acc = None
    for t in range(tiles):
        row = push_ref[column, t : t + 1, :]
        term = jnp.where(slot == tb_ref[column, t], row, 0.0)
        acc = term if acc is None else acc + term
    return acc


def sweep_kernel(n_contact, n_body, last, *refs):
    gx, gy = contact_groups(n_contact)
    if last:
        (tb_ref, push_ref,
         tot_out,
         own_buf, later_buf, recv3, xbuf, ybuf, tot_buf,
         s_sem, r_sem, sx_sem, rx_sem, sy_sem, ry_sem) = refs
    else:
        (tb_ref, push_ref, vfree_ref, imass_ref,
         rows_out,
         own_buf, later_buf, recv3, xbuf, ybuf, vel_buf, vel_next, velf, rows_buf,
         s_sem, r_sem, sx_sem, rx_sem, sy_sem, ry_sem) = refs
    blocks = own_buf.shape[0]
    width = own_buf.shape[1]
    half = blocks // 2
    c = lax.axis_index("contact")
    b = lax.axis_index("body")
    core = lax.rem(c, 2)
    x = lax.rem(c // 2, gx)
    y = c // (2 * gx)
    mate = c + 1 - 2 * core
    up = lax.rem(b + 1, n_body)
    down = lax.rem(b + n_body - 1, n_body)
    x_peers = [(y * gx + lax.rem(x + j, gx)) * 2 + core for j in range(1, gx)]
    y_peers = [(lax.rem(y + j, gy) * gx + x) * 2 + core for j in range(1, gy)]

    greet = [(mate, b), (c, up), (mate, up), (c, down), (mate, down)]
    greet += [(p, b) for p in x_peers] + [(p, b) for p in y_peers]
    barrier = pltpu.get_barrier_semaphore()
    for dev in greet:
        pl.semaphore_signal(barrier, inc=1, device_id=dev, device_id_type=MESH)
    later_buf[...] = scatter_rows(tb_ref, 1, push_ref, blocks)
    own_buf[...] = scatter_rows(tb_ref, 0, push_ref, blocks)
    pl.semaphore_wait(barrier, len(greet))

    def remote(src, dst, send, recv, dev):
        return pltpu.make_async_remote_copy(
            src_ref=src, dst_ref=dst, send_sem=send, recv_sem=recv,
            device_id=dev, device_id_type=MESH,
        )

    mine = pl.ds(pl.multiple_of(core * half, half), half)
    theirs = pl.ds(pl.multiple_of((1 - core) * half, half), half)
    sent = []
    for k, (src, dev) in enumerate(((later_buf.at[mine], (c, up)), (later_buf.at[theirs], (mate, up)))):
        cp = remote(src, recv3.at[1 + k], s_sem.at[1 + k], r_sem.at[1 + k], dev)
        cp.start()
        sent.append(cp)
    cp = remote(own_buf.at[theirs], recv3.at[0], s_sem.at[0], r_sem.at[0], (mate, b))
    cp.start()
    sent.append(cp)
    for k, dev in enumerate(((mate, b), (c, down), (mate, down))):
        remote(own_buf.at[mine], recv3.at[k], s_sem.at[k], r_sem.at[k], dev).wait_recv()
    part = own_buf[mine] + recv3[0] + recv3[1] + recv3[2]

    for buf, pos, peers, size, ssem, rsem in (
        (xbuf, x, x_peers, gx, sx_sem, rx_sem),
        (ybuf, y, y_peers, gy, sy_sem, ry_sem),
    ):
        if size == 1:
            continue
        buf[pos] = part
        for j, p in enumerate(peers):
            cp = remote(buf.at[pos], buf.at[pos], ssem.at[j], rsem.at[pos], (p, b))
            cp.start()
            sent.append(cp)
        for j in range(1, size):
            src_pos = lax.rem(pos + size - j, size)
            remote(buf.at[src_pos], buf.at[src_pos], ssem.at[0], rsem.at[src_pos], (peers[-j], b)).wait_recv()
        part = buf[0]
        for g in range(1, size):
            part = part + buf[g]

    if last:
        tot_buf[mine] = part
        cp = remote(tot_buf.at[mine], tot_buf.at[mine], s_sem.at[3], r_sem.at[3], (mate, b))
        cp.start()
        sent.append(cp)
        remote(tot_buf.at[theirs], tot_buf.at[theirs], s_sem.at[3], r_sem.at[3], (mate, b)).wait_recv()
        tot_out[...] = tot_buf[...]
    else:
        vel = vfree_ref[mine] + imass_ref[mine] * part
        vel_buf[mine] = vel.astype(jnp.bfloat16)
        src = vel_buf.at[mine]
        for k, (dst, dev) in enumerate((
            (vel_buf.at[mine], (mate, b)),
            (vel_next.at[mine], (c, down)),
            (vel_next.at[mine], (mate, down)),
        )):
            cp = remote(src, dst, s_sem.at[3 + k], r_sem.at[3 + k], dev)
            cp.start()
            sent.append(cp)
        for k, (dst, dev) in enumerate((
            (vel_buf.at[theirs], (mate, b)),
            (vel_next.at[mine], (c, up)),
            (vel_next.at[theirs], (mate, up)),
        )):
            remote(src, dst, s_sem.at[3 + k], r_sem.at[3 + k], dev).wait_recv()
        velf[0] = vel_buf[...].astype(jnp.float32)
        velf[1] = vel_next[...].astype(jnp.float32)
        tiles = rows_buf.shape[1]
        for column in range(2):
            for t in range(tiles):
                rows_buf[column, pl.ds(t, 1), :] = velf[column, pl.ds(tb_ref[column, t], 1), :]
            rows_out[column] = rows_buf[column].astype(jnp.bfloat16)
    for cp in sent:
        cp.wait_send()


def sweep_exchange(tile_block, push, vel_free, inv_mass, n_contact, n_body, last):
    gx, gy = contact_groups(n_contact)
    blocks, width = vel_free.shape
    tiles = push.shape[1]
    half = blocks // 2
    vspec = pl.BlockSpec(memory_space=pltpu.VMEM)
    sspec = pl.BlockSpec(memory_space=pltpu.SMEM)
    if last:
        args = [tile_block, push]
        out_shape = jax.ShapeDtypeStruct((blocks, width), jnp.float32)
        tail = [pltpu.VMEM((blocks, width), jnp.float32)]
    else:
        args = [tile_block, push, vel_free, inv_mass]
        out_shape = jax.ShapeDtypeStruct((2, tiles, width), jnp.bfloat16)
        tail = [
            pltpu.VMEM((blocks, width), jnp.bfloat16),
            pltpu.VMEM((blocks, width), jnp.bfloat16),
            pltpu.VMEM((2, blocks, width), jnp.float32),
            pltpu.VMEM((2, tiles, width), jnp.float32),
        ]
    scratch = [
        pltpu.VMEM((blocks, width), jnp.float32),
        pltpu.VMEM((blocks, width), jnp.float32),
        pltpu.VMEM((3, half, width), jnp.float32),
        pltpu.VMEM((gx, half, width), jnp.float32),
        pltpu.VMEM((gy, half, width), jnp.float32),
        *tail,
        pltpu.SemaphoreType.DMA((6,)),
        pltpu.SemaphoreType.DMA((6,)),
        pltpu.SemaphoreType.DMA((max(gx - 1, 1),)),
        pltpu.SemaphoreType.DMA((gx,)),
        pltpu.SemaphoreType.DMA((max(gy - 1, 1),)),
        pltpu.SemaphoreType.DMA((gy,)),
    ]
    return pl.pallas_call(
        functools.partial(sweep_kernel, n_contact, n_body, last),
        out_shape=out_shape,
        in_specs=[sspec] + [vspec] * (len(args) - 1),
        out_specs=vspec,
        scratch_shapes=scratch,
        compiler_params=pltpu.CompilerParams(
            collective_id=1 if last else 0, has_side_effects=True
        ),
    )(*args)


def per_device(
    n_contact, n_body,
    jacobian, tile_block, tile_count, vel_free, inv_mass, bias, step_scale, friction, impulse_start,
):
    tiles_here = jacobian.shape[0]
    contacts = friction.shape[1]
    order = jnp.arange(tiles_here, dtype=jnp.int32)
    mask = (order < tile_count[0]).astype(jnp.float32)[:, None]

    def pushes(lam):
        lamb = lam.astype(jnp.bfloat16)
        return jnp.einsum("tkbc,tc->ktb", jacobian, lamb, preferred_element_type=jnp.float32)

    lam = impulse_start * mask
    for sweep in range(ITERS):
        rows = sweep_exchange(tile_block.T, pushes(lam), vel_free, inv_mass, n_contact, n_body, False)
        rel = jnp.einsum("tkbc,ktb->tc", jacobian, rows, preferred_element_type=jnp.float32) + bias
        lam = project(lam - step_scale * rel, friction, contacts) * mask
    total = sweep_exchange(tile_block.T, pushes(lam), vel_free, inv_mass, n_contact, n_body, True)
    velocity = vel_free + inv_mass * total
    return (lam, velocity)


def solution(mesh):
    n_contact = mesh.shape["contact"]
    n_body = mesh.shape["body"]
    placed = (
        P(("contact", "body"), None, None, None),
        P(("contact", "body"), None),
        P(("contact", "body")),
        P("body", None),
        P("body", None),
        P(("contact", "body"), None),
        P(("contact", "body"), None),
        P(("contact", "body"), None),
        P(("contact", "body"), None),
    )
    return jax.shard_map(
        functools.partial(per_device, n_contact, n_body),
        mesh=mesh,
        in_specs=placed,
        out_specs=(P(("contact", "body"), None), P("body", None)),
        check_vma=False,
    )
```

```python
import functools
import math

import jax
import jax.numpy as jnp
from jax import lax
from jax.experimental import pallas as pl
from jax.experimental.pallas import tpu as pltpu
from jax.sharding import PartitionSpec as P

ITERS = 2
MESH = pl.DeviceIdType.MESH


def project(trial, friction, contacts):
    normal = trial[:, :contacts]
    first = trial[:, contacts : 2 * contacts]
    second = trial[:, 2 * contacts :]
    tangent = jnp.sqrt(first * first + second * second)
    inside = tangent <= friction * normal
    below = friction * tangent <= -normal
    moved = (normal + friction * tangent) / (1.0 + friction * friction)
    safe = jnp.where(inside | below, 1.0, tangent)
    factor = jnp.where(inside, 1.0, jnp.where(below, 0.0, friction * moved / safe))
    new_normal = jnp.where(inside, normal, jnp.where(below, 0.0, moved))
    return jnp.concatenate([new_normal, first * factor, second * factor], axis=1)


def contact_groups(n_contact):
    rest = n_contact // 2
    gy = 1
    for d in range(1, int(math.isqrt(rest)) + 1):
        if rest % d == 0:
            gy = d
    return rest // gy, gy


def scatter_rows(tb_ref, column, push_ref, blocks):
    tiles = push_ref.shape[1]
    width = push_ref.shape[2]
    slot = lax.broadcasted_iota(jnp.int32, (blocks, width), 0)
    acc = None
    for t in range(tiles):
        row = push_ref[column, t : t + 1, :]
        term = jnp.where(slot == tb_ref[column, t], row, 0.0)
        acc = term if acc is None else acc + term
    return acc


def sweep_kernel(n_contact, n_body, last, *refs):
    gx, gy = contact_groups(n_contact)
    if last:
        (tb_ref, push_ref,
         tot_out,
         own_buf, later_buf, recv3, xbuf, ybuf, tot_buf,
         s_sem, r_sem, sx_sem, rx_sem, sy_sem, ry_sem) = refs
    else:
        (tb_ref, push_ref, vfree_ref, imass_ref,
         rows_out,
         own_buf, later_buf, recv3, xbuf, ybuf, vel_buf, vel_next, velf, rows_buf,
         s_sem, r_sem, sx_sem, rx_sem, sy_sem, ry_sem) = refs
    blocks = own_buf.shape[0]
    width = own_buf.shape[1]
    half = blocks // 2
    c = lax.axis_index("contact")
    b = lax.axis_index("body")
    core = lax.rem(c, 2)
    x = lax.rem(c // 2, gx)
    y = c // (2 * gx)
    mate = c + 1 - 2 * core
    up = lax.rem(b + 1, n_body)
    down = lax.rem(b + n_body - 1, n_body)
    x_peers = [(y * gx + lax.rem(x + j, gx)) * 2 + core for j in range(1, gx)]
    y_peers = [(lax.rem(y + j, gy) * gx + x) * 2 + core for j in range(1, gy)]

    greet = [(mate, b), (c, up), (mate, up), (c, down), (mate, down)]
    greet += [(p, b) for p in x_peers] + [(p, b) for p in y_peers]
    barrier = pltpu.get_barrier_semaphore()
    for dev in greet:
        pl.semaphore_signal(barrier, inc=1, device_id=dev, device_id_type=MESH)
    later_buf[...] = scatter_rows(tb_ref, 1, push_ref, blocks)
    own_buf[...] = scatter_rows(tb_ref, 0, push_ref, blocks)
    pl.semaphore_wait(barrier, len(greet))

    def remote(src, dst, send, recv, dev):
        return pltpu.make_async_remote_copy(
            src_ref=src, dst_ref=dst, send_sem=send, recv_sem=recv,
            device_id=dev, device_id_type=MESH,
        )

    mine = pl.ds(pl.multiple_of(core * half, half), half)
    theirs = pl.ds(pl.multiple_of((1 - core) * half, half), half)
    sent = []
    for k, (src, dev) in enumerate(((later_buf.at[mine], (c, up)), (later_buf.at[theirs], (mate, up)))):
        cp = remote(src, recv3.at[1 + k], s_sem.at[1 + k], r_sem.at[1 + k], dev)
        cp.start()
        sent.append(cp)
    cp = remote(own_buf.at[theirs], recv3.at[0], s_sem.at[0], r_sem.at[0], (mate, b))
    cp.start()
    sent.append(cp)
    for k, dev in enumerate(((mate, b), (c, down), (mate, down))):
        remote(own_buf.at[mine], recv3.at[k], s_sem.at[k], r_sem.at[k], dev).wait_recv()
    part = own_buf[mine] + recv3[0] + recv3[1] + recv3[2]

    rounds = [(xbuf, x, x_peers, gx, sx_sem, rx_sem), (ybuf, y, y_peers, gy, sy_sem, ry_sem)]
    if gx == gy:
        first = [xv * (1 - core) + yv * core for xv, yv in zip([x] + x_peers, [y] + y_peers)]
        second = [xv * core + yv * (1 - core) for xv, yv in zip([x] + x_peers, [y] + y_peers)]
        rounds = [(xbuf, first[0], first[1:], gx, sx_sem, rx_sem),
                  (ybuf, second[0], second[1:], gy, sy_sem, ry_sem)]
    for buf, pos, peers, size, ssem, rsem in rounds:
        if size == 1:
            continue
        buf[pos] = part
        for j, p in enumerate(peers):
            cp = remote(buf.at[pos], buf.at[pos], ssem.at[j], rsem.at[pos], (p, b))
            cp.start()
            sent.append(cp)
        for j in range(1, size):
            src_pos = lax.rem(pos + size - j, size)
            remote(buf.at[src_pos], buf.at[src_pos], ssem.at[0], rsem.at[src_pos], (peers[-j], b)).wait_recv()
        part = buf[0]
        for g in range(1, size):
            part = part + buf[g]

    if last:
        tot_buf[mine] = part
        cp = remote(tot_buf.at[mine], tot_buf.at[mine], s_sem.at[3], r_sem.at[3], (mate, b))
        cp.start()
        sent.append(cp)
        remote(tot_buf.at[theirs], tot_buf.at[theirs], s_sem.at[3], r_sem.at[3], (mate, b)).wait_recv()
        tot_out[...] = tot_buf[...]
    else:
        vel = vfree_ref[mine] + imass_ref[mine] * part
        vel_buf[mine] = vel.astype(jnp.bfloat16)
        src = vel_buf.at[mine]
        for k, (dst, dev) in enumerate((
            (vel_buf.at[mine], (mate, b)),
            (vel_next.at[mine], (c, down)),
            (vel_next.at[mine], (mate, down)),
        )):
            cp = remote(src, dst, s_sem.at[3 + k], r_sem.at[3 + k], dev)
            cp.start()
            sent.append(cp)
        for k, (dst, dev) in enumerate((
            (vel_buf.at[theirs], (mate, b)),
            (vel_next.at[mine], (c, up)),
            (vel_next.at[theirs], (mate, up)),
        )):
            remote(src, dst, s_sem.at[3 + k], r_sem.at[3 + k], dev).wait_recv()
        velf[0] = vel_buf[...].astype(jnp.float32)
        velf[1] = vel_next[...].astype(jnp.float32)
        tiles = rows_buf.shape[1]
        for column in range(2):
            for t in range(tiles):
                rows_buf[column, pl.ds(t, 1), :] = velf[column, pl.ds(tb_ref[column, t], 1), :]
            rows_out[column] = rows_buf[column].astype(jnp.bfloat16)
    for cp in sent:
        cp.wait_send()


def sweep_exchange(tile_block, push, vel_free, inv_mass, n_contact, n_body, last):
    gx, gy = contact_groups(n_contact)
    blocks, width = vel_free.shape
    tiles = push.shape[1]
    half = blocks // 2
    vspec = pl.BlockSpec(memory_space=pltpu.VMEM)
    sspec = pl.BlockSpec(memory_space=pltpu.SMEM)
    if last:
        args = [tile_block, push]
        out_shape = jax.ShapeDtypeStruct((blocks, width), jnp.float32)
        tail = [pltpu.VMEM((blocks, width), jnp.float32)]
    else:
        args = [tile_block, push, vel_free, inv_mass]
        out_shape = jax.ShapeDtypeStruct((2, tiles, width), jnp.bfloat16)
        tail = [
            pltpu.VMEM((blocks, width), jnp.bfloat16),
            pltpu.VMEM((blocks, width), jnp.bfloat16),
            pltpu.VMEM((2, blocks, width), jnp.float32),
            pltpu.VMEM((2, tiles, width), jnp.float32),
        ]
    scratch = [
        pltpu.VMEM((blocks, width), jnp.float32),
        pltpu.VMEM((blocks, width), jnp.float32),
        pltpu.VMEM((3, half, width), jnp.float32),
        pltpu.VMEM((gx, half, width), jnp.float32),
        pltpu.VMEM((gy, half, width), jnp.float32),
        *tail,
        pltpu.SemaphoreType.DMA((6,)),
        pltpu.SemaphoreType.DMA((6,)),
        pltpu.SemaphoreType.DMA((max(gx - 1, 1),)),
        pltpu.SemaphoreType.DMA((gx,)),
        pltpu.SemaphoreType.DMA((max(gy - 1, 1),)),
        pltpu.SemaphoreType.DMA((gy,)),
    ]
    return pl.pallas_call(
        functools.partial(sweep_kernel, n_contact, n_body, last),
        out_shape=out_shape,
        in_specs=[sspec] + [vspec] * (len(args) - 1),
        out_specs=vspec,
        scratch_shapes=scratch,
        compiler_params=pltpu.CompilerParams(
            collective_id=1 if last else 0, has_side_effects=True
        ),
    )(*args)


def per_device(
    n_contact, n_body,
    jacobian, tile_block, tile_count, vel_free, inv_mass, bias, step_scale, friction, impulse_start,
):
    tiles_here = jacobian.shape[0]
    contacts = friction.shape[1]
    order = jnp.arange(tiles_here, dtype=jnp.int32)
    mask = (order < tile_count[0]).astype(jnp.float32)[:, None]

    def pushes(lam):
        lamb = lam.astype(jnp.bfloat16)
        return jnp.einsum("tkbc,tc->ktb", jacobian, lamb, preferred_element_type=jnp.float32)

    lam = impulse_start * mask
    for sweep in range(ITERS):
        rows = sweep_exchange(tile_block.T, pushes(lam), vel_free, inv_mass, n_contact, n_body, False)
        rel = jnp.einsum("tkbc,ktb->tc", jacobian, rows, preferred_element_type=jnp.float32) + bias
        lam = project(lam - step_scale * rel, friction, contacts) * mask
    total = sweep_exchange(tile_block.T, pushes(lam), vel_free, inv_mass, n_contact, n_body, True)
    velocity = vel_free + inv_mass * total
    return (lam, velocity)


def solution(mesh):
    n_contact = mesh.shape["contact"]
    n_body = mesh.shape["body"]
    placed = (
        P(("contact", "body"), None, None, None),
        P(("contact", "body"), None),
        P(("contact", "body")),
        P("body", None),
        P("body", None),
        P(("contact", "body"), None),
        P(("contact", "body"), None),
        P(("contact", "body"), None),
        P(("contact", "body"), None),
    )
    return jax.shard_map(
        functools.partial(per_device, n_contact, n_body),
        mesh=mesh,
        in_specs=placed,
        out_specs=(P(("contact", "body"), None), P("body", None)),
        check_vma=False,
    )
```

```python
import functools
import math

import jax
import jax.numpy as jnp
from jax import lax
from jax.experimental import pallas as pl
from jax.experimental.pallas import tpu as pltpu
from jax.sharding import PartitionSpec as P

ITERS = 2
MESH = pl.DeviceIdType.MESH


def project(trial, friction, contacts):
    normal = trial[:, :contacts]
    first = trial[:, contacts : 2 * contacts]
    second = trial[:, 2 * contacts :]
    tangent = jnp.sqrt(first * first + second * second)
    inside = tangent <= friction * normal
    below = friction * tangent <= -normal
    moved = (normal + friction * tangent) / (1.0 + friction * friction)
    safe = jnp.where(inside | below, 1.0, tangent)
    factor = jnp.where(inside, 1.0, jnp.where(below, 0.0, friction * moved / safe))
    new_normal = jnp.where(inside, normal, jnp.where(below, 0.0, moved))
    return jnp.concatenate([new_normal, first * factor, second * factor], axis=1)


def contact_groups(n_contact):
    rest = n_contact // 2
    gy = 1
    for d in range(1, int(math.isqrt(rest)) + 1):
        if rest % d == 0:
            gy = d
    return rest // gy, gy


def scatter_rows(tb_ref, column, push_ref, blocks):
    tiles = push_ref.shape[1]
    width = push_ref.shape[2]
    slot = lax.broadcasted_iota(jnp.int32, (blocks, width), 0)
    acc = None
    for t in range(tiles):
        row = push_ref[column, t : t + 1, :]
        term = jnp.where(slot == tb_ref[column, t], row, 0.0)
        acc = term if acc is None else acc + term
    return acc


def sweep_kernel(n_contact, n_body, last, *refs):
    gx, gy = contact_groups(n_contact)
    if last:
        (tb_ref, push_ref,
         tot_out,
         own_buf, later_buf, recv3, xbuf, ybuf, tot_buf,
         s_sem, r_sem, sx_sem, rx_sem, sy_sem, ry_sem) = refs
    else:
        (tb_ref, push_ref, vfree_ref, imass_ref,
         rows_out,
         own_buf, later_buf, recv3, xbuf, ybuf, vel_buf, vel_next, velf, rows_buf,
         s_sem, r_sem, sx_sem, rx_sem, sy_sem, ry_sem) = refs
    blocks = own_buf.shape[0]
    width = own_buf.shape[1]
    half = blocks // 2
    c = lax.axis_index("contact")
    b = lax.axis_index("body")
    core = lax.rem(c, 2)
    x = lax.rem(c // 2, gx)
    y = c // (2 * gx)
    mate = c + 1 - 2 * core
    up = lax.rem(b + 1, n_body)
    down = lax.rem(b + n_body - 1, n_body)
    x_peers = [(y * gx + lax.rem(x + j, gx)) * 2 + core for j in range(1, gx)]
    y_peers = [(lax.rem(y + j, gy) * gx + x) * 2 + core for j in range(1, gy)]

    greet = [(mate, b), (c, up), (mate, up), (c, down), (mate, down)]
    greet += [(p, b) for p in x_peers] + [(p, b) for p in y_peers]
    barrier = pltpu.get_barrier_semaphore()
    for dev in greet:
        pl.semaphore_signal(barrier, inc=1, device_id=dev, device_id_type=MESH)
    later_buf[...] = scatter_rows(tb_ref, 1, push_ref, blocks)
    own_buf[...] = scatter_rows(tb_ref, 0, push_ref, blocks)
    pl.semaphore_wait(barrier, len(greet))

    def remote(src, dst, send, recv, dev):
        return pltpu.make_async_remote_copy(
            src_ref=src, dst_ref=dst, send_sem=send, recv_sem=recv,
            device_id=dev, device_id_type=MESH,
        )

    mine = pl.ds(pl.multiple_of(core * half, half), half)
    theirs = pl.ds(pl.multiple_of((1 - core) * half, half), half)
    sent = []
    for k, (src, dev) in enumerate(((later_buf.at[mine], (c, up)), (later_buf.at[theirs], (mate, up)))):
        cp = remote(src, recv3.at[1 + k], s_sem.at[1 + k], r_sem.at[1 + k], dev)
        cp.start()
        sent.append(cp)
    cp = remote(own_buf.at[theirs], recv3.at[0], s_sem.at[0], r_sem.at[0], (mate, b))
    cp.start()
    sent.append(cp)
    for k, dev in enumerate(((mate, b), (c, down), (mate, down))):
        remote(own_buf.at[mine], recv3.at[k], s_sem.at[k], r_sem.at[k], dev).wait_recv()
    part = own_buf[mine] + recv3[0] + recv3[1] + recv3[2]

    rounds = [(xbuf, x, x_peers, gx, sx_sem, rx_sem), (ybuf, y, y_peers, gy, sy_sem, ry_sem)]
    if gx == gy:
        first = [xv * (1 - core) + yv * core for xv, yv in zip([x] + x_peers, [y] + y_peers)]
        second = [xv * core + yv * (1 - core) for xv, yv in zip([x] + x_peers, [y] + y_peers)]
        rounds = [(xbuf, first[0], first[1:], gx, sx_sem, rx_sem),
                  (ybuf, second[0], second[1:], gy, sy_sem, ry_sem)]
    for buf, pos, peers, size, ssem, rsem in rounds:
        if size == 1:
            continue
        buf[pos] = part
        for j, p in enumerate(peers):
            cp = remote(buf.at[pos], buf.at[pos], ssem.at[j], rsem.at[pos], (p, b))
            cp.start()
            sent.append(cp)
        for j in range(1, size):
            src_pos = lax.rem(pos + size - j, size)
            remote(buf.at[src_pos], buf.at[src_pos], ssem.at[0], rsem.at[src_pos], (peers[-j], b)).wait_recv()
        part = buf[0]
        for g in range(1, size):
            part = part + buf[g]

    if last:
        tot_buf[mine] = part
        cp = remote(tot_buf.at[mine], tot_buf.at[mine], s_sem.at[3], r_sem.at[3], (mate, b))
        cp.start()
        sent.append(cp)
        remote(tot_buf.at[theirs], tot_buf.at[theirs], s_sem.at[3], r_sem.at[3], (mate, b)).wait_recv()
        tot_out[...] = tot_buf[...]
    else:
        vel = vfree_ref[mine] + imass_ref[mine] * part
        vel_buf[mine] = vel.astype(jnp.bfloat16)
        src = vel_buf.at[mine]
        for k, (dst, dev) in enumerate((
            (vel_buf.at[mine], (mate, b)),
            (vel_next.at[mine], (c, down)),
            (vel_next.at[mine], (mate, down)),
        )):
            cp = remote(src, dst, s_sem.at[3 + k], r_sem.at[3 + k], dev)
            cp.start()
            sent.append(cp)
        for k, (dst, dev) in enumerate((
            (vel_buf.at[theirs], (mate, b)),
            (vel_next.at[mine], (c, up)),
            (vel_next.at[theirs], (mate, up)),
        )):
            remote(src, dst, s_sem.at[3 + k], r_sem.at[3 + k], dev).wait_recv()
        velf[0] = vel_buf[...].astype(jnp.float32)
        velf[1] = vel_next[...].astype(jnp.float32)
        tiles = rows_buf.shape[1]
        for column in range(2):
            for t in range(tiles):
                rows_buf[column, pl.ds(t, 1), :] = velf[column, pl.ds(tb_ref[column, t], 1), :]
            rows_out[column] = rows_buf[column].astype(jnp.bfloat16)
    for cp in sent:
        cp.wait_send()


def sweep_exchange(tile_block, push, vel_free, inv_mass, n_contact, n_body, last):
    gx, gy = contact_groups(n_contact)
    blocks, width = vel_free.shape
    tiles = push.shape[1]
    half = blocks // 2
    vspec = pl.BlockSpec(memory_space=pltpu.VMEM)
    sspec = pl.BlockSpec(memory_space=pltpu.SMEM)
    if last:
        args = [tile_block, push]
        out_shape = jax.ShapeDtypeStruct((blocks, width), jnp.float32)
        tail = [pltpu.VMEM((blocks, width), jnp.float32)]
    else:
        args = [tile_block, push, vel_free, inv_mass]
        out_shape = jax.ShapeDtypeStruct((2, tiles, width), jnp.bfloat16)
        tail = [
            pltpu.VMEM((blocks, width), jnp.bfloat16),
            pltpu.VMEM((blocks, width), jnp.bfloat16),
            pltpu.VMEM((2, blocks, width), jnp.float32),
            pltpu.VMEM((2, tiles, width), jnp.float32),
        ]
    scratch = [
        pltpu.VMEM((blocks, width), jnp.float32),
        pltpu.VMEM((blocks, width), jnp.float32),
        pltpu.VMEM((3, half, width), jnp.float32),
        pltpu.VMEM((gx, half, width), jnp.float32),
        pltpu.VMEM((gy, half, width), jnp.float32),
        *tail,
        pltpu.SemaphoreType.DMA((6,)),
        pltpu.SemaphoreType.DMA((6,)),
        pltpu.SemaphoreType.DMA((max(gx - 1, 1),)),
        pltpu.SemaphoreType.DMA((gx,)),
        pltpu.SemaphoreType.DMA((max(gy - 1, 1),)),
        pltpu.SemaphoreType.DMA((gy,)),
    ]
    return pl.pallas_call(
        functools.partial(sweep_kernel, n_contact, n_body, last),
        out_shape=out_shape,
        in_specs=[sspec] + [vspec] * (len(args) - 1),
        out_specs=vspec,
        scratch_shapes=scratch,
        compiler_params=pltpu.CompilerParams(
            collective_id=1 if last else 0, has_side_effects=True
        ),
    )(*args)


def dual_kernel(n_contact, n_body, *refs):
    gx, gy = contact_groups(n_contact)
    (tb_ref, push_ref, vfree_ref, imass_ref,
     rows_out,
     own_buf, later_buf, recv6, xbuf, ybuf, vel_buf, velf, rows_buf, vn_send, vnext_ref,
     s_sem, r_sem, sx_sem, rx_sem, sy_sem, ry_sem) = refs
    blocks = own_buf.shape[0]
    width = own_buf.shape[1]
    half = blocks // 2
    c = lax.axis_index("contact")
    b = lax.axis_index("body")
    core = lax.rem(c, 2)
    x = lax.rem(c // 2, gx)
    y = c // (2 * gx)
    mate = c + 1 - 2 * core
    up = lax.rem(b + 1, n_body)
    down = lax.rem(b + n_body - 1, n_body)
    x_peers = [(y * gx + lax.rem(x + j, gx)) * 2 + core for j in range(1, gx)]
    y_peers = [(lax.rem(y + j, gy) * gx + x) * 2 + core for j in range(1, gy)]

    greet = [(mate, b), (c, up), (mate, up), (c, down), (mate, down)]
    greet += [(p, b) for p in x_peers] + [(p, b) for p in y_peers]
    barrier = pltpu.get_barrier_semaphore()
    for dev in greet:
        pl.semaphore_signal(barrier, inc=1, device_id=dev, device_id_type=MESH)
    pl.semaphore_wait(barrier, len(greet))

    def remote(src, dst, send, recv, dev):
        return pltpu.make_async_remote_copy(
            src_ref=src, dst_ref=dst, send_sem=send, recv_sem=recv,
            device_id=dev, device_id_type=MESH,
        )

    mine = pl.ds(pl.multiple_of(core * half, half), half)
    theirs = pl.ds(pl.multiple_of((1 - core) * half, half), half)
    sent = []
    later_buf[...] = scatter_rows(tb_ref, 1, push_ref, blocks)
    plan = (
        (later_buf.at[mine], (c, up)),
        (later_buf.at[theirs], (mate, up)),
        (later_buf.at[theirs], (mate, b)),
    )
    for k, (src, dev) in enumerate(plan):
        cp = remote(src, recv6.at[k], s_sem.at[k], r_sem.at[k], dev)
        cp.start()
        sent.append(cp)
    own_buf[...] = scatter_rows(tb_ref, 0, push_ref, blocks)
    plan = (
        (own_buf.at[mine], (c, down)),
        (own_buf.at[theirs], (mate, down)),
        (own_buf.at[theirs], (mate, b)),
    )
    for k, (src, dev) in enumerate(plan):
        cp = remote(src, recv6.at[3 + k], s_sem.at[3 + k], r_sem.at[3 + k], dev)
        cp.start()
        sent.append(cp)
    vn_send[0] = vfree_ref[mine]
    vn_send[1] = imass_ref[mine]
    vcp = remote(vn_send, vnext_ref, s_sem.at[8], r_sem.at[8], (c, down))
    vcp.start()
    sent.append(vcp)
    senders = ((c, down), (mate, down), (mate, b), (c, up), (mate, up), (mate, b))
    for k, dev in enumerate(senders):
        remote(own_buf.at[mine], recv6.at[k], s_sem.at[k], r_sem.at[k], dev).wait_recv()
    part = jnp.concatenate([
        own_buf[mine] + recv6[5] + recv6[0] + recv6[1],
        later_buf[mine] + recv6[2] + recv6[3] + recv6[4],
    ], axis=0)

    rounds = [(xbuf, x, x_peers, gx, sx_sem, rx_sem), (ybuf, y, y_peers, gy, sy_sem, ry_sem)]
    if gx == gy:
        first = [xv * (1 - core) + yv * core for xv, yv in zip([x] + x_peers, [y] + y_peers)]
        second = [xv * core + yv * (1 - core) for xv, yv in zip([x] + x_peers, [y] + y_peers)]
        rounds = [(xbuf, first[0], first[1:], gx, sx_sem, rx_sem),
                  (ybuf, second[0], second[1:], gy, sy_sem, ry_sem)]
    for buf, pos, peers, size, ssem, rsem in rounds:
        if size == 1:
            continue
        buf[pos] = part
        for j, p in enumerate(peers):
            cp = remote(buf.at[pos], buf.at[pos], ssem.at[j], rsem.at[pos], (p, b))
            cp.start()
            sent.append(cp)
        for j in range(1, size):
            src_pos = lax.rem(pos + size - j, size)
            remote(buf.at[src_pos], buf.at[src_pos], ssem.at[0], rsem.at[src_pos], (peers[-j], b)).wait_recv()
        part = buf[0]
        for g in range(1, size):
            part = part + buf[g]

    vel_buf[0, mine] = (vfree_ref[mine] + imass_ref[mine] * part[:half]).astype(jnp.bfloat16)
    remote(vn_send, vnext_ref, s_sem.at[8], r_sem.at[8], (c, up)).wait_recv()
    vel_buf[1, mine] = (vnext_ref[0] + vnext_ref[1] * part[half:]).astype(jnp.bfloat16)
    for k in range(2):
        cp = remote(vel_buf.at[k, mine], vel_buf.at[k, mine], s_sem.at[6 + k], r_sem.at[6 + k], (mate, b))
        cp.start()
        sent.append(cp)
    for k in range(2):
        remote(vel_buf.at[k, theirs], vel_buf.at[k, theirs], s_sem.at[6 + k], r_sem.at[6 + k], (mate, b)).wait_recv()
    velf[...] = vel_buf[...].astype(jnp.float32)
    tiles = rows_buf.shape[1]
    for column in range(2):
        for t in range(tiles):
            rows_buf[column, pl.ds(t, 1), :] = velf[column, pl.ds(tb_ref[column, t], 1), :]
        rows_out[column] = rows_buf[column].astype(jnp.bfloat16)
    for cp in sent:
        cp.wait_send()


def dual_exchange(tile_block, push, vel_free, inv_mass, n_contact, n_body):
    gx, gy = contact_groups(n_contact)
    blocks, width = vel_free.shape
    tiles = push.shape[1]
    half = blocks // 2
    vspec = pl.BlockSpec(memory_space=pltpu.VMEM)
    sspec = pl.BlockSpec(memory_space=pltpu.SMEM)
    scratch = [
        pltpu.VMEM((blocks, width), jnp.float32),
        pltpu.VMEM((blocks, width), jnp.float32),
        pltpu.VMEM((6, half, width), jnp.float32),
        pltpu.VMEM((gx, blocks, width), jnp.float32),
        pltpu.VMEM((gy, blocks, width), jnp.float32),
        pltpu.VMEM((2, blocks, width), jnp.bfloat16),
        pltpu.VMEM((2, blocks, width), jnp.float32),
        pltpu.VMEM((2, tiles, width), jnp.float32),
        pltpu.VMEM((2, half, width), jnp.float32),
        pltpu.VMEM((2, half, width), jnp.float32),
        pltpu.SemaphoreType.DMA((9,)),
        pltpu.SemaphoreType.DMA((9,)),
        pltpu.SemaphoreType.DMA((max(gx - 1, 1),)),
        pltpu.SemaphoreType.DMA((gx,)),
        pltpu.SemaphoreType.DMA((max(gy - 1, 1),)),
        pltpu.SemaphoreType.DMA((gy,)),
    ]
    return pl.pallas_call(
        functools.partial(dual_kernel, n_contact, n_body),
        out_shape=jax.ShapeDtypeStruct((2, tiles, width), jnp.bfloat16),
        in_specs=[sspec] + [vspec] * 3,
        out_specs=vspec,
        scratch_shapes=scratch,
        compiler_params=pltpu.CompilerParams(collective_id=2, has_side_effects=True),
    )(tile_block, push, vel_free, inv_mass)


def per_device(
    n_contact, n_body,
    jacobian, tile_block, tile_count, vel_free, inv_mass, bias, step_scale, friction, impulse_start,
):
    tiles_here = jacobian.shape[0]
    contacts = friction.shape[1]
    order = jnp.arange(tiles_here, dtype=jnp.int32)
    mask = (order < tile_count[0]).astype(jnp.float32)[:, None]

    def pushes(lam):
        lamb = lam.astype(jnp.bfloat16)
        return jnp.einsum("tkbc,tc->ktb", jacobian, lamb, preferred_element_type=jnp.float32)

    lam = impulse_start * mask
    for sweep in range(ITERS):
        rows = dual_exchange(tile_block.T, pushes(lam), vel_free, inv_mass, n_contact, n_body)
        rel = jnp.einsum("tkbc,ktb->tc", jacobian, rows, preferred_element_type=jnp.float32) + bias
        lam = project(lam - step_scale * rel, friction, contacts) * mask
    total = sweep_exchange(tile_block.T, pushes(lam), vel_free, inv_mass, n_contact, n_body, True)
    velocity = vel_free + inv_mass * total
    return (lam, velocity)


def solution(mesh):
    n_contact = mesh.shape["contact"]
    n_body = mesh.shape["body"]
    placed = (
        P(("contact", "body"), None, None, None),
        P(("contact", "body"), None),
        P(("contact", "body")),
        P("body", None),
        P("body", None),
        P(("contact", "body"), None),
        P(("contact", "body"), None),
        P(("contact", "body"), None),
        P(("contact", "body"), None),
    )
    return jax.shard_map(
        functools.partial(per_device, n_contact, n_body),
        mesh=mesh,
        in_specs=placed,
        out_specs=(P(("contact", "body"), None), P("body", None)),
        check_vma=False,
    )
```

```python
import functools
import math

import jax
import jax.numpy as jnp
from jax import lax
from jax.experimental import pallas as pl
from jax.experimental.pallas import tpu as pltpu
from jax.sharding import PartitionSpec as P

ITERS = 2
MESH = pl.DeviceIdType.MESH


def project(trial, friction, contacts):
    normal = trial[:, :contacts]
    first = trial[:, contacts : 2 * contacts]
    second = trial[:, 2 * contacts :]
    tangent = jnp.sqrt(first * first + second * second)
    inside = tangent <= friction * normal
    below = friction * tangent <= -normal
    moved = (normal + friction * tangent) / (1.0 + friction * friction)
    safe = jnp.where(inside | below, 1.0, tangent)
    factor = jnp.where(inside, 1.0, jnp.where(below, 0.0, friction * moved / safe))
    new_normal = jnp.where(inside, normal, jnp.where(below, 0.0, moved))
    return jnp.concatenate([new_normal, first * factor, second * factor], axis=1)


def contact_groups(n_contact):
    rest = n_contact // 2
    gy = 1
    for d in range(1, int(math.isqrt(rest)) + 1):
        if rest % d == 0:
            gy = d
    return rest // gy, gy


def scatter_rows(tb_ref, column, push_ref, blocks):
    tiles = push_ref.shape[0]
    width = push_ref.shape[2]
    slot = lax.broadcasted_iota(jnp.int32, (blocks, width), 0)
    acc = None
    for t in range(tiles):
        row = push_ref[t, column : column + 1, :]
        term = jnp.where(slot == tb_ref[column, t], row, 0.0)
        acc = term if acc is None else acc + term
    return acc


def sweep_kernel(n_contact, n_body, last, *refs):
    gx, gy = contact_groups(n_contact)
    if last:
        (tb_ref, push_ref,
         tot_out,
         own_buf, later_buf, recv3, xbuf, ybuf, tot_buf,
         s_sem, r_sem, sx_sem, rx_sem, sy_sem, ry_sem) = refs
    else:
        (tb_ref, push_ref, vfree_ref, imass_ref,
         rows_out,
         own_buf, later_buf, recv3, xbuf, ybuf, vel_buf, vel_next, velf, rows_buf,
         s_sem, r_sem, sx_sem, rx_sem, sy_sem, ry_sem) = refs
    blocks = own_buf.shape[0]
    width = own_buf.shape[1]
    half = blocks // 2
    c = lax.axis_index("contact")
    b = lax.axis_index("body")
    core = lax.rem(c, 2)
    x = lax.rem(c // 2, gx)
    y = c // (2 * gx)
    mate = c + 1 - 2 * core
    up = lax.rem(b + 1, n_body)
    down = lax.rem(b + n_body - 1, n_body)
    x_peers = [(y * gx + lax.rem(x + j, gx)) * 2 + core for j in range(1, gx)]
    y_peers = [(lax.rem(y + j, gy) * gx + x) * 2 + core for j in range(1, gy)]

    greet = [(mate, b), (c, up), (mate, up), (c, down), (mate, down)]
    greet += [(p, b) for p in x_peers] + [(p, b) for p in y_peers]
    barrier = pltpu.get_barrier_semaphore()
    for dev in greet:
        pl.semaphore_signal(barrier, inc=1, device_id=dev, device_id_type=MESH)
    later_buf[...] = scatter_rows(tb_ref, 1, push_ref, blocks)
    own_buf[...] = scatter_rows(tb_ref, 0, push_ref, blocks)
    pl.semaphore_wait(barrier, len(greet))

    def remote(src, dst, send, recv, dev):
        return pltpu.make_async_remote_copy(
            src_ref=src, dst_ref=dst, send_sem=send, recv_sem=recv,
            device_id=dev, device_id_type=MESH,
        )

    mine = pl.ds(pl.multiple_of(core * half, half), half)
    theirs = pl.ds(pl.multiple_of((1 - core) * half, half), half)
    sent = []
    for k, (src, dev) in enumerate(((later_buf.at[mine], (c, up)), (later_buf.at[theirs], (mate, up)))):
        cp = remote(src, recv3.at[1 + k], s_sem.at[1 + k], r_sem.at[1 + k], dev)
        cp.start()
        sent.append(cp)
    cp = remote(own_buf.at[theirs], recv3.at[0], s_sem.at[0], r_sem.at[0], (mate, b))
    cp.start()
    sent.append(cp)
    for k, dev in enumerate(((mate, b), (c, down), (mate, down))):
        remote(own_buf.at[mine], recv3.at[k], s_sem.at[k], r_sem.at[k], dev).wait_recv()
    part = own_buf[mine] + recv3[0] + recv3[1] + recv3[2]

    rounds = [(xbuf, x, x_peers, gx, sx_sem, rx_sem), (ybuf, y, y_peers, gy, sy_sem, ry_sem)]
    if gx == gy:
        first = [xv * (1 - core) + yv * core for xv, yv in zip([x] + x_peers, [y] + y_peers)]
        second = [xv * core + yv * (1 - core) for xv, yv in zip([x] + x_peers, [y] + y_peers)]
        rounds = [(xbuf, first[0], first[1:], gx, sx_sem, rx_sem),
                  (ybuf, second[0], second[1:], gy, sy_sem, ry_sem)]
    for buf, pos, peers, size, ssem, rsem in rounds:
        if size == 1:
            continue
        buf[pos] = part
        for j, p in enumerate(peers):
            cp = remote(buf.at[pos], buf.at[pos], ssem.at[j], rsem.at[pos], (p, b))
            cp.start()
            sent.append(cp)
        for j in range(1, size):
            src_pos = lax.rem(pos + size - j, size)
            remote(buf.at[src_pos], buf.at[src_pos], ssem.at[0], rsem.at[src_pos], (peers[-j], b)).wait_recv()
        part = buf[0]
        for g in range(1, size):
            part = part + buf[g]

    if last:
        tot_buf[mine] = part
        cp = remote(tot_buf.at[mine], tot_buf.at[mine], s_sem.at[3], r_sem.at[3], (mate, b))
        cp.start()
        sent.append(cp)
        remote(tot_buf.at[theirs], tot_buf.at[theirs], s_sem.at[3], r_sem.at[3], (mate, b)).wait_recv()
        tot_out[...] = tot_buf[...]
    else:
        vel = vfree_ref[mine] + imass_ref[mine] * part
        vel_buf[mine] = vel.astype(jnp.bfloat16)
        src = vel_buf.at[mine]
        for k, (dst, dev) in enumerate((
            (vel_buf.at[mine], (mate, b)),
            (vel_next.at[mine], (c, down)),
            (vel_next.at[mine], (mate, down)),
        )):
            cp = remote(src, dst, s_sem.at[3 + k], r_sem.at[3 + k], dev)
            cp.start()
            sent.append(cp)
        for k, (dst, dev) in enumerate((
            (vel_buf.at[theirs], (mate, b)),
            (vel_next.at[mine], (c, up)),
            (vel_next.at[theirs], (mate, up)),
        )):
            remote(src, dst, s_sem.at[3 + k], r_sem.at[3 + k], dev).wait_recv()
        velf[0] = vel_buf[...].astype(jnp.float32)
        velf[1] = vel_next[...].astype(jnp.float32)
        tiles = rows_buf.shape[1]
        for column in range(2):
            for t in range(tiles):
                rows_buf[column, pl.ds(t, 1), :] = velf[column, pl.ds(tb_ref[column, t], 1), :]
            rows_out[column] = rows_buf[column].astype(jnp.bfloat16)
    for cp in sent:
        cp.wait_send()


def sweep_exchange(tile_block, push, vel_free, inv_mass, n_contact, n_body, last):
    gx, gy = contact_groups(n_contact)
    blocks, width = vel_free.shape
    tiles = push.shape[0]
    half = blocks // 2
    vspec = pl.BlockSpec(memory_space=pltpu.VMEM)
    sspec = pl.BlockSpec(memory_space=pltpu.SMEM)
    if last:
        args = [tile_block, push]
        out_shape = jax.ShapeDtypeStruct((blocks, width), jnp.float32)
        tail = [pltpu.VMEM((blocks, width), jnp.float32)]
    else:
        args = [tile_block, push, vel_free, inv_mass]
        out_shape = jax.ShapeDtypeStruct((2, tiles, width), jnp.bfloat16)
        tail = [
            pltpu.VMEM((blocks, width), jnp.bfloat16),
            pltpu.VMEM((blocks, width), jnp.bfloat16),
            pltpu.VMEM((2, blocks, width), jnp.float32),
            pltpu.VMEM((2, tiles, width), jnp.float32),
        ]
    scratch = [
        pltpu.VMEM((blocks, width), jnp.float32),
        pltpu.VMEM((blocks, width), jnp.float32),
        pltpu.VMEM((3, half, width), jnp.float32),
        pltpu.VMEM((gx, half, width), jnp.float32),
        pltpu.VMEM((gy, half, width), jnp.float32),
        *tail,
        pltpu.SemaphoreType.DMA((6,)),
        pltpu.SemaphoreType.DMA((6,)),
        pltpu.SemaphoreType.DMA((max(gx - 1, 1),)),
        pltpu.SemaphoreType.DMA((gx,)),
        pltpu.SemaphoreType.DMA((max(gy - 1, 1),)),
        pltpu.SemaphoreType.DMA((gy,)),
    ]
    return pl.pallas_call(
        functools.partial(sweep_kernel, n_contact, n_body, last),
        out_shape=out_shape,
        in_specs=[sspec] + [vspec] * (len(args) - 1),
        out_specs=vspec,
        scratch_shapes=scratch,
        compiler_params=pltpu.CompilerParams(
            collective_id=1 if last else 0, has_side_effects=True
        ),
    )(*args)


def dual_kernel(n_contact, n_body, *refs):
    gx, gy = contact_groups(n_contact)
    (tb_ref, push_ref, vfree_ref, imass_ref,
     rows_out,
     own_buf, later_buf, recv6, xbuf, ybuf, vel_buf, velf, rows_buf, vn_send, vnext_ref,
     s_sem, r_sem, sx_sem, rx_sem, sy_sem, ry_sem) = refs
    blocks = own_buf.shape[0]
    width = own_buf.shape[1]
    half = blocks // 2
    c = lax.axis_index("contact")
    b = lax.axis_index("body")
    core = lax.rem(c, 2)
    x = lax.rem(c // 2, gx)
    y = c // (2 * gx)
    mate = c + 1 - 2 * core
    up = lax.rem(b + 1, n_body)
    down = lax.rem(b + n_body - 1, n_body)
    x_peers = [(y * gx + lax.rem(x + j, gx)) * 2 + core for j in range(1, gx)]
    y_peers = [(lax.rem(y + j, gy) * gx + x) * 2 + core for j in range(1, gy)]

    greet = [(mate, b), (c, up), (mate, up), (c, down), (mate, down)]
    greet += [(p, b) for p in x_peers] + [(p, b) for p in y_peers]
    barrier = pltpu.get_barrier_semaphore()
    for dev in greet:
        pl.semaphore_signal(barrier, inc=1, device_id=dev, device_id_type=MESH)
    pl.semaphore_wait(barrier, len(greet))

    def remote(src, dst, send, recv, dev):
        return pltpu.make_async_remote_copy(
            src_ref=src, dst_ref=dst, send_sem=send, recv_sem=recv,
            device_id=dev, device_id_type=MESH,
        )

    mine = pl.ds(pl.multiple_of(core * half, half), half)
    theirs = pl.ds(pl.multiple_of((1 - core) * half, half), half)
    sent = []
    later_buf[...] = scatter_rows(tb_ref, 1, push_ref, blocks)
    plan = (
        (later_buf.at[mine], (c, up)),
        (later_buf.at[theirs], (mate, up)),
        (later_buf.at[theirs], (mate, b)),
    )
    for k, (src, dev) in enumerate(plan):
        cp = remote(src, recv6.at[k], s_sem.at[k], r_sem.at[k], dev)
        cp.start()
        sent.append(cp)
    own_buf[...] = scatter_rows(tb_ref, 0, push_ref, blocks)
    plan = (
        (own_buf.at[mine], (c, down)),
        (own_buf.at[theirs], (mate, down)),
        (own_buf.at[theirs], (mate, b)),
    )
    for k, (src, dev) in enumerate(plan):
        cp = remote(src, recv6.at[3 + k], s_sem.at[3 + k], r_sem.at[3 + k], dev)
        cp.start()
        sent.append(cp)
    vn_send[0] = vfree_ref[mine]
    vn_send[1] = imass_ref[mine]
    vcp = remote(vn_send, vnext_ref, s_sem.at[8], r_sem.at[8], (c, down))
    vcp.start()
    sent.append(vcp)
    senders = ((c, down), (mate, down), (mate, b), (c, up), (mate, up), (mate, b))
    for k, dev in enumerate(senders):
        remote(own_buf.at[mine], recv6.at[k], s_sem.at[k], r_sem.at[k], dev).wait_recv()
    part = jnp.concatenate([
        own_buf[mine] + recv6[5] + recv6[0] + recv6[1],
        later_buf[mine] + recv6[2] + recv6[3] + recv6[4],
    ], axis=0)

    rounds = [(xbuf, x, x_peers, gx, sx_sem, rx_sem), (ybuf, y, y_peers, gy, sy_sem, ry_sem)]
    if gx == gy:
        first = [xv * (1 - core) + yv * core for xv, yv in zip([x] + x_peers, [y] + y_peers)]
        second = [xv * core + yv * (1 - core) for xv, yv in zip([x] + x_peers, [y] + y_peers)]
        rounds = [(xbuf, first[0], first[1:], gx, sx_sem, rx_sem),
                  (ybuf, second[0], second[1:], gy, sy_sem, ry_sem)]
    for buf, pos, peers, size, ssem, rsem in rounds:
        if size == 1:
            continue
        buf[pos] = part
        for j, p in enumerate(peers):
            cp = remote(buf.at[pos], buf.at[pos], ssem.at[j], rsem.at[pos], (p, b))
            cp.start()
            sent.append(cp)
        for j in range(1, size):
            src_pos = lax.rem(pos + size - j, size)
            remote(buf.at[src_pos], buf.at[src_pos], ssem.at[0], rsem.at[src_pos], (peers[-j], b)).wait_recv()
        part = buf[0]
        for g in range(1, size):
            part = part + buf[g]

    vel_buf[0, mine] = (vfree_ref[mine] + imass_ref[mine] * part[:half]).astype(jnp.bfloat16)
    remote(vn_send, vnext_ref, s_sem.at[8], r_sem.at[8], (c, up)).wait_recv()
    vel_buf[1, mine] = (vnext_ref[0] + vnext_ref[1] * part[half:]).astype(jnp.bfloat16)
    for k in range(2):
        cp = remote(vel_buf.at[k, mine], vel_buf.at[k, mine], s_sem.at[6 + k], r_sem.at[6 + k], (mate, b))
        cp.start()
        sent.append(cp)
    for k in range(2):
        remote(vel_buf.at[k, theirs], vel_buf.at[k, theirs], s_sem.at[6 + k], r_sem.at[6 + k], (mate, b)).wait_recv()
    velf[...] = vel_buf[...].astype(jnp.float32)
    tiles = rows_buf.shape[1]
    for column in range(2):
        for t in range(tiles):
            rows_buf[column, pl.ds(t, 1), :] = velf[column, pl.ds(tb_ref[column, t], 1), :]
        rows_out[column] = rows_buf[column].astype(jnp.bfloat16)
    for cp in sent:
        cp.wait_send()


def dual_exchange(tile_block, push, vel_free, inv_mass, n_contact, n_body):
    gx, gy = contact_groups(n_contact)
    blocks, width = vel_free.shape
    tiles = push.shape[0]
    half = blocks // 2
    vspec = pl.BlockSpec(memory_space=pltpu.VMEM)
    sspec = pl.BlockSpec(memory_space=pltpu.SMEM)
    scratch = [
        pltpu.VMEM((blocks, width), jnp.float32),
        pltpu.VMEM((blocks, width), jnp.float32),
        pltpu.VMEM((6, half, width), jnp.float32),
        pltpu.VMEM((gx, blocks, width), jnp.float32),
        pltpu.VMEM((gy, blocks, width), jnp.float32),
        pltpu.VMEM((2, blocks, width), jnp.bfloat16),
        pltpu.VMEM((2, blocks, width), jnp.float32),
        pltpu.VMEM((2, tiles, width), jnp.float32),
        pltpu.VMEM((2, half, width), jnp.float32),
        pltpu.VMEM((2, half, width), jnp.float32),
        pltpu.SemaphoreType.DMA((9,)),
        pltpu.SemaphoreType.DMA((9,)),
        pltpu.SemaphoreType.DMA((max(gx - 1, 1),)),
        pltpu.SemaphoreType.DMA((gx,)),
        pltpu.SemaphoreType.DMA((max(gy - 1, 1),)),
        pltpu.SemaphoreType.DMA((gy,)),
    ]
    return pl.pallas_call(
        functools.partial(dual_kernel, n_contact, n_body),
        out_shape=jax.ShapeDtypeStruct((2, tiles, width), jnp.bfloat16),
        in_specs=[sspec] + [vspec] * 3,
        out_specs=vspec,
        scratch_shapes=scratch,
        compiler_params=pltpu.CompilerParams(collective_id=2, has_side_effects=True),
    )(tile_block, push, vel_free, inv_mass)


def per_device(
    n_contact, n_body,
    jacobian, tile_block, tile_count, vel_free, inv_mass, bias, step_scale, friction, impulse_start,
):
    tiles_here = jacobian.shape[0]
    contacts = friction.shape[1]
    order = jnp.arange(tiles_here, dtype=jnp.int32)
    mask = (order < tile_count[0]).astype(jnp.float32)[:, None]

    def pushes(lam):
        lamb = lam.astype(jnp.bfloat16)
        product = jacobian.astype(jnp.float32) * lamb.astype(jnp.float32)[:, None, None, :]
        return jnp.sum(product, axis=-1)

    lam = impulse_start * mask
    for sweep in range(ITERS):
        rows = dual_exchange(tile_block.T, pushes(lam), vel_free, inv_mass, n_contact, n_body)
        rel = jnp.einsum("tkbc,ktb->tc", jacobian, rows, preferred_element_type=jnp.float32) + bias
        lam = project(lam - step_scale * rel, friction, contacts) * mask
    total = sweep_exchange(tile_block.T, pushes(lam), vel_free, inv_mass, n_contact, n_body, True)
    velocity = vel_free + inv_mass * total
    return (lam, velocity)


def solution(mesh):
    n_contact = mesh.shape["contact"]
    n_body = mesh.shape["body"]
    placed = (
        P(("contact", "body"), None, None, None),
        P(("contact", "body"), None),
        P(("contact", "body")),
        P("body", None),
        P("body", None),
        P(("contact", "body"), None),
        P(("contact", "body"), None),
        P(("contact", "body"), None),
        P(("contact", "body"), None),
    )
    return jax.shard_map(
        functools.partial(per_device, n_contact, n_body),
        mesh=mesh,
        in_specs=placed,
        out_specs=(P(("contact", "body"), None), P("body", None)),
        check_vma=False,
    )
```

```python
import functools
import math

import jax
import jax.numpy as jnp
from jax import lax
from jax.experimental import pallas as pl
from jax.experimental.pallas import tpu as pltpu
from jax.sharding import PartitionSpec as P

ITERS = 2
MESH = pl.DeviceIdType.MESH


def project(trial, friction, contacts):
    normal = trial[:, :contacts]
    first = trial[:, contacts : 2 * contacts]
    second = trial[:, 2 * contacts :]
    tangent = jnp.sqrt(first * first + second * second)
    inside = tangent <= friction * normal
    below = friction * tangent <= -normal
    moved = (normal + friction * tangent) / (1.0 + friction * friction)
    safe = jnp.where(inside | below, 1.0, tangent)
    factor = jnp.where(inside, 1.0, jnp.where(below, 0.0, friction * moved / safe))
    new_normal = jnp.where(inside, normal, jnp.where(below, 0.0, moved))
    return jnp.concatenate([new_normal, first * factor, second * factor], axis=1)


def contact_groups(n_contact):
    rest = n_contact // 2
    gy = 1
    for d in range(1, int(math.isqrt(rest)) + 1):
        if rest % d == 0:
            gy = d
    return rest // gy, gy


def scatter_rows(tb_ref, column, push_ref, blocks):
    tiles = push_ref.shape[1]
    width = push_ref.shape[2]
    slot = lax.broadcasted_iota(jnp.int32, (blocks, width), 0)
    acc = None
    for t in range(tiles):
        row = push_ref[column, t : t + 1, :]
        term = jnp.where(slot == tb_ref[column, t], row, 0.0)
        acc = term if acc is None else acc + term
    return acc


def sweep_kernel(n_contact, n_body, last, *refs):
    gx, gy = contact_groups(n_contact)
    if last:
        (tb_ref, push_ref,
         tot_out,
         own_buf, later_buf, recv3, xbuf, ybuf, tot_buf,
         s_sem, r_sem, sx_sem, rx_sem, sy_sem, ry_sem) = refs
    else:
        (tb_ref, push_ref, vfree_ref, imass_ref,
         rows_out,
         own_buf, later_buf, recv3, xbuf, ybuf, vel_buf, vel_next, velf, rows_buf,
         s_sem, r_sem, sx_sem, rx_sem, sy_sem, ry_sem) = refs
    blocks = own_buf.shape[0]
    width = own_buf.shape[1]
    half = blocks // 2
    c = lax.axis_index("contact")
    b = lax.axis_index("body")
    core = lax.rem(c, 2)
    x = lax.rem(c // 2, gx)
    y = c // (2 * gx)
    mate = c + 1 - 2 * core
    up = lax.rem(b + 1, n_body)
    down = lax.rem(b + n_body - 1, n_body)
    x_peers = [(y * gx + lax.rem(x + j, gx)) * 2 + core for j in range(1, gx)]
    y_peers = [(lax.rem(y + j, gy) * gx + x) * 2 + core for j in range(1, gy)]

    greet = [(mate, b), (c, up), (mate, up), (c, down), (mate, down)]
    greet += [(p, b) for p in x_peers] + [(p, b) for p in y_peers]
    barrier = pltpu.get_barrier_semaphore()
    for dev in greet:
        pl.semaphore_signal(barrier, inc=1, device_id=dev, device_id_type=MESH)
    later_buf[...] = scatter_rows(tb_ref, 1, push_ref, blocks)
    own_buf[...] = scatter_rows(tb_ref, 0, push_ref, blocks)
    pl.semaphore_wait(barrier, len(greet))

    def remote(src, dst, send, recv, dev):
        return pltpu.make_async_remote_copy(
            src_ref=src, dst_ref=dst, send_sem=send, recv_sem=recv,
            device_id=dev, device_id_type=MESH,
        )

    mine = pl.ds(pl.multiple_of(core * half, half), half)
    theirs = pl.ds(pl.multiple_of((1 - core) * half, half), half)
    sent = []
    for k, (src, dev) in enumerate(((later_buf.at[mine], (c, up)), (later_buf.at[theirs], (mate, up)))):
        cp = remote(src, recv3.at[1 + k], s_sem.at[1 + k], r_sem.at[1 + k], dev)
        cp.start()
        sent.append(cp)
    cp = remote(own_buf.at[theirs], recv3.at[0], s_sem.at[0], r_sem.at[0], (mate, b))
    cp.start()
    sent.append(cp)
    for k, dev in enumerate(((mate, b), (c, down), (mate, down))):
        remote(own_buf.at[mine], recv3.at[k], s_sem.at[k], r_sem.at[k], dev).wait_recv()
    part = own_buf[mine] + recv3[0] + recv3[1] + recv3[2]

    rounds = [(xbuf, x, x_peers, gx, sx_sem, rx_sem), (ybuf, y, y_peers, gy, sy_sem, ry_sem)]
    if gx == gy:
        first = [xv * (1 - core) + yv * core for xv, yv in zip([x] + x_peers, [y] + y_peers)]
        second = [xv * core + yv * (1 - core) for xv, yv in zip([x] + x_peers, [y] + y_peers)]
        rounds = [(xbuf, first[0], first[1:], gx, sx_sem, rx_sem),
                  (ybuf, second[0], second[1:], gy, sy_sem, ry_sem)]
    for buf, pos, peers, size, ssem, rsem in rounds:
        if size == 1:
            continue
        buf[pos] = part
        for j, p in enumerate(peers):
            cp = remote(buf.at[pos], buf.at[pos], ssem.at[j], rsem.at[pos], (p, b))
            cp.start()
            sent.append(cp)
        for j in range(1, size):
            src_pos = lax.rem(pos + size - j, size)
            remote(buf.at[src_pos], buf.at[src_pos], ssem.at[0], rsem.at[src_pos], (peers[-j], b)).wait_recv()
        part = buf[0]
        for g in range(1, size):
            part = part + buf[g]

    if last:
        tot_buf[mine] = part
        cp = remote(tot_buf.at[mine], tot_buf.at[mine], s_sem.at[3], r_sem.at[3], (mate, b))
        cp.start()
        sent.append(cp)
        remote(tot_buf.at[theirs], tot_buf.at[theirs], s_sem.at[3], r_sem.at[3], (mate, b)).wait_recv()
        tot_out[...] = tot_buf[...]
    else:
        vel = vfree_ref[mine] + imass_ref[mine] * part
        vel_buf[mine] = vel.astype(jnp.bfloat16)
        src = vel_buf.at[mine]
        for k, (dst, dev) in enumerate((
            (vel_buf.at[mine], (mate, b)),
            (vel_next.at[mine], (c, down)),
            (vel_next.at[mine], (mate, down)),
        )):
            cp = remote(src, dst, s_sem.at[3 + k], r_sem.at[3 + k], dev)
            cp.start()
            sent.append(cp)
        for k, (dst, dev) in enumerate((
            (vel_buf.at[theirs], (mate, b)),
            (vel_next.at[mine], (c, up)),
            (vel_next.at[theirs], (mate, up)),
        )):
            remote(src, dst, s_sem.at[3 + k], r_sem.at[3 + k], dev).wait_recv()
        velf[0] = vel_buf[...].astype(jnp.float32)
        velf[1] = vel_next[...].astype(jnp.float32)
        tiles = rows_buf.shape[1]
        for column in range(2):
            for t in range(tiles):
                rows_buf[column, pl.ds(t, 1), :] = velf[column, pl.ds(tb_ref[column, t], 1), :]
            rows_out[column] = rows_buf[column].astype(jnp.bfloat16)
    for cp in sent:
        cp.wait_send()


def sweep_exchange(tile_block, push, vel_free, inv_mass, n_contact, n_body, last):
    gx, gy = contact_groups(n_contact)
    blocks, width = vel_free.shape
    tiles = push.shape[1]
    half = blocks // 2
    vspec = pl.BlockSpec(memory_space=pltpu.VMEM)
    sspec = pl.BlockSpec(memory_space=pltpu.SMEM)
    if last:
        args = [tile_block, push]
        out_shape = jax.ShapeDtypeStruct((blocks, width), jnp.float32)
        tail = [pltpu.VMEM((blocks, width), jnp.float32)]
    else:
        args = [tile_block, push, vel_free, inv_mass]
        out_shape = jax.ShapeDtypeStruct((2, tiles, width), jnp.bfloat16)
        tail = [
            pltpu.VMEM((blocks, width), jnp.bfloat16),
            pltpu.VMEM((blocks, width), jnp.bfloat16),
            pltpu.VMEM((2, blocks, width), jnp.float32),
            pltpu.VMEM((2, tiles, width), jnp.float32),
        ]
    scratch = [
        pltpu.VMEM((blocks, width), jnp.float32),
        pltpu.VMEM((blocks, width), jnp.float32),
        pltpu.VMEM((3, half, width), jnp.float32),
        pltpu.VMEM((gx, half, width), jnp.float32),
        pltpu.VMEM((gy, half, width), jnp.float32),
        *tail,
        pltpu.SemaphoreType.DMA((6,)),
        pltpu.SemaphoreType.DMA((6,)),
        pltpu.SemaphoreType.DMA((max(gx - 1, 1),)),
        pltpu.SemaphoreType.DMA((gx,)),
        pltpu.SemaphoreType.DMA((max(gy - 1, 1),)),
        pltpu.SemaphoreType.DMA((gy,)),
    ]
    return pl.pallas_call(
        functools.partial(sweep_kernel, n_contact, n_body, last),
        out_shape=out_shape,
        in_specs=[sspec] + [vspec] * (len(args) - 1),
        out_specs=vspec,
        scratch_shapes=scratch,
        compiler_params=pltpu.CompilerParams(
            collective_id=1 if last else 0, has_side_effects=True
        ),
    )(*args)


def dual_kernel(n_contact, n_body, *refs):
    gx, gy = contact_groups(n_contact)
    (tb_ref, push_ref, vfree_ref, imass_ref,
     rows_out,
     own_buf, later_buf, recv6, xbuf, ybuf, vel_buf, velf, rows_buf, vn_send, vnext_ref,
     s_sem, r_sem, sx_sem, rx_sem, sy_sem, ry_sem) = refs
    blocks = own_buf.shape[0]
    width = own_buf.shape[1]
    half = blocks // 2
    c = lax.axis_index("contact")
    b = lax.axis_index("body")
    core = lax.rem(c, 2)
    x = lax.rem(c // 2, gx)
    y = c // (2 * gx)
    mate = c + 1 - 2 * core
    up = lax.rem(b + 1, n_body)
    down = lax.rem(b + n_body - 1, n_body)
    x_peers = [(y * gx + lax.rem(x + j, gx)) * 2 + core for j in range(1, gx)]
    y_peers = [(lax.rem(y + j, gy) * gx + x) * 2 + core for j in range(1, gy)]

    greet = [(mate, b), (c, up), (mate, up), (c, down), (mate, down)]
    greet += [(p, b) for p in x_peers] + [(p, b) for p in y_peers]
    mine = pl.ds(pl.multiple_of(core * half, half), half)
    theirs = pl.ds(pl.multiple_of((1 - core) * half, half), half)
    barrier = pltpu.get_barrier_semaphore()
    for dev in greet:
        pl.semaphore_signal(barrier, inc=1, device_id=dev, device_id_type=MESH)
    later_buf[...] = scatter_rows(tb_ref, 1, push_ref, blocks)
    own_buf[...] = scatter_rows(tb_ref, 0, push_ref, blocks)
    vn_send[0] = vfree_ref[mine]
    vn_send[1] = imass_ref[mine]
    pl.semaphore_wait(barrier, len(greet))

    def remote(src, dst, send, recv, dev):
        return pltpu.make_async_remote_copy(
            src_ref=src, dst_ref=dst, send_sem=send, recv_sem=recv,
            device_id=dev, device_id_type=MESH,
        )

    sent = []
    plan = (
        (later_buf.at[mine], (c, up)),
        (later_buf.at[theirs], (mate, up)),
        (later_buf.at[theirs], (mate, b)),
    )
    for k, (src, dev) in enumerate(plan):
        cp = remote(src, recv6.at[k], s_sem.at[k], r_sem.at[k], dev)
        cp.start()
        sent.append(cp)
    plan = (
        (own_buf.at[mine], (c, down)),
        (own_buf.at[theirs], (mate, down)),
        (own_buf.at[theirs], (mate, b)),
    )
    for k, (src, dev) in enumerate(plan):
        cp = remote(src, recv6.at[3 + k], s_sem.at[3 + k], r_sem.at[3 + k], dev)
        cp.start()
        sent.append(cp)
    vcp = remote(vn_send, vnext_ref, s_sem.at[8], r_sem.at[8], (c, down))
    vcp.start()
    sent.append(vcp)
    senders = ((c, down), (mate, down), (mate, b), (c, up), (mate, up), (mate, b))
    for k, dev in enumerate(senders):
        remote(own_buf.at[mine], recv6.at[k], s_sem.at[k], r_sem.at[k], dev).wait_recv()
    part = jnp.concatenate([
        own_buf[mine] + recv6[5] + recv6[0] + recv6[1],
        later_buf[mine] + recv6[2] + recv6[3] + recv6[4],
    ], axis=0)

    rounds = [(xbuf, x, x_peers, gx, sx_sem, rx_sem), (ybuf, y, y_peers, gy, sy_sem, ry_sem)]
    if gx == gy:
        first = [xv * (1 - core) + yv * core for xv, yv in zip([x] + x_peers, [y] + y_peers)]
        second = [xv * core + yv * (1 - core) for xv, yv in zip([x] + x_peers, [y] + y_peers)]
        rounds = [(xbuf, first[0], first[1:], gx, sx_sem, rx_sem),
                  (ybuf, second[0], second[1:], gy, sy_sem, ry_sem)]
    for buf, pos, peers, size, ssem, rsem in rounds:
        if size == 1:
            continue
        buf[pos] = part
        for j, p in enumerate(peers):
            cp = remote(buf.at[pos], buf.at[pos], ssem.at[j], rsem.at[pos], (p, b))
            cp.start()
            sent.append(cp)
        for j in range(1, size):
            src_pos = lax.rem(pos + size - j, size)
            remote(buf.at[src_pos], buf.at[src_pos], ssem.at[0], rsem.at[src_pos], (peers[-j], b)).wait_recv()
        part = buf[0]
        for g in range(1, size):
            part = part + buf[g]

    vel_buf[0, mine] = (vfree_ref[mine] + imass_ref[mine] * part[:half]).astype(jnp.bfloat16)
    remote(vn_send, vnext_ref, s_sem.at[8], r_sem.at[8], (c, up)).wait_recv()
    vel_buf[1, mine] = (vnext_ref[0] + vnext_ref[1] * part[half:]).astype(jnp.bfloat16)
    for k in range(2):
        cp = remote(vel_buf.at[k, mine], vel_buf.at[k, mine], s_sem.at[6 + k], r_sem.at[6 + k], (mate, b))
        cp.start()
        sent.append(cp)
    for k in range(2):
        remote(vel_buf.at[k, theirs], vel_buf.at[k, theirs], s_sem.at[6 + k], r_sem.at[6 + k], (mate, b)).wait_recv()
    velf[...] = vel_buf[...].astype(jnp.float32)
    tiles = rows_buf.shape[1]
    for column in range(2):
        for t in range(tiles):
            rows_buf[column, pl.ds(t, 1), :] = velf[column, pl.ds(tb_ref[column, t], 1), :]
        rows_out[column] = rows_buf[column].astype(jnp.bfloat16)
    for cp in sent:
        cp.wait_send()


def dual_exchange(tile_block, push, vel_free, inv_mass, n_contact, n_body):
    gx, gy = contact_groups(n_contact)
    blocks, width = vel_free.shape
    tiles = push.shape[1]
    half = blocks // 2
    vspec = pl.BlockSpec(memory_space=pltpu.VMEM)
    sspec = pl.BlockSpec(memory_space=pltpu.SMEM)
    scratch = [
        pltpu.VMEM((blocks, width), jnp.float32),
        pltpu.VMEM((blocks, width), jnp.float32),
        pltpu.VMEM((6, half, width), jnp.float32),
        pltpu.VMEM((gx, blocks, width), jnp.float32),
        pltpu.VMEM((gy, blocks, width), jnp.float32),
        pltpu.VMEM((2, blocks, width), jnp.bfloat16),
        pltpu.VMEM((2, blocks, width), jnp.float32),
        pltpu.VMEM((2, tiles, width), jnp.float32),
        pltpu.VMEM((2, half, width), jnp.float32),
        pltpu.VMEM((2, half, width), jnp.float32),
        pltpu.SemaphoreType.DMA((9,)),
        pltpu.SemaphoreType.DMA((9,)),
        pltpu.SemaphoreType.DMA((max(gx - 1, 1),)),
        pltpu.SemaphoreType.DMA((gx,)),
        pltpu.SemaphoreType.DMA((max(gy - 1, 1),)),
        pltpu.SemaphoreType.DMA((gy,)),
    ]
    return pl.pallas_call(
        functools.partial(dual_kernel, n_contact, n_body),
        out_shape=jax.ShapeDtypeStruct((2, tiles, width), jnp.bfloat16),
        in_specs=[sspec] + [vspec] * 3,
        out_specs=vspec,
        scratch_shapes=scratch,
        compiler_params=pltpu.CompilerParams(collective_id=2, has_side_effects=True),
    )(tile_block, push, vel_free, inv_mass)


def per_device(
    n_contact, n_body,
    jacobian, tile_block, tile_count, vel_free, inv_mass, bias, step_scale, friction, impulse_start,
):
    tiles_here = jacobian.shape[0]
    contacts = friction.shape[1]
    order = jnp.arange(tiles_here, dtype=jnp.int32)
    mask = (order < tile_count[0]).astype(jnp.float32)[:, None]

    def pushes(lam):
        lamb = lam.astype(jnp.bfloat16)
        return jnp.einsum("tkbc,tc->ktb", jacobian, lamb, preferred_element_type=jnp.float32)

    lam = impulse_start * mask
    for sweep in range(ITERS):
        rows = dual_exchange(tile_block.T, pushes(lam), vel_free, inv_mass, n_contact, n_body)
        rel = jnp.einsum("tkbc,ktb->tc", jacobian, rows, preferred_element_type=jnp.float32) + bias
        lam = project(lam - step_scale * rel, friction, contacts) * mask
    total = sweep_exchange(tile_block.T, pushes(lam), vel_free, inv_mass, n_contact, n_body, True)
    velocity = vel_free + inv_mass * total
    return (lam, velocity)


def solution(mesh):
    n_contact = mesh.shape["contact"]
    n_body = mesh.shape["body"]
    placed = (
        P(("contact", "body"), None, None, None),
        P(("contact", "body"), None),
        P(("contact", "body")),
        P("body", None),
        P("body", None),
        P(("contact", "body"), None),
        P(("contact", "body"), None),
        P(("contact", "body"), None),
        P(("contact", "body"), None),
    )
    return jax.shard_map(
        functools.partial(per_device, n_contact, n_body),
        mesh=mesh,
        in_specs=placed,
        out_specs=(P(("contact", "body"), None), P("body", None)),
        check_vma=False,
    )
```

```python
import functools
import math

import jax
import jax.numpy as jnp
from jax import lax
from jax.experimental import pallas as pl
from jax.experimental.pallas import tpu as pltpu
from jax.sharding import PartitionSpec as P

ITERS = 2
MESH = pl.DeviceIdType.MESH


def project(trial, friction, contacts):
    normal = trial[:, :contacts]
    first = trial[:, contacts : 2 * contacts]
    second = trial[:, 2 * contacts :]
    tangent = jnp.sqrt(first * first + second * second)
    inside = tangent <= friction * normal
    below = friction * tangent <= -normal
    moved = (normal + friction * tangent) / (1.0 + friction * friction)
    safe = jnp.where(inside | below, 1.0, tangent)
    factor = jnp.where(inside, 1.0, jnp.where(below, 0.0, friction * moved / safe))
    new_normal = jnp.where(inside, normal, jnp.where(below, 0.0, moved))
    return jnp.concatenate([new_normal, first * factor, second * factor], axis=1)


def contact_groups(n_contact):
    rest = n_contact // 2
    gy = 1
    for d in range(1, int(math.isqrt(rest)) + 1):
        if rest % d == 0:
            gy = d
    return rest // gy, gy


def scatter_rows(tb_ref, column, push_ref, blocks):
    tiles = push_ref.shape[1]
    width = push_ref.shape[2]
    slot = lax.broadcasted_iota(jnp.int32, (blocks, width), 0)
    acc = None
    for t in range(tiles):
        row = push_ref[column, t : t + 1, :]
        term = jnp.where(slot == tb_ref[column, t], row, 0.0)
        acc = term if acc is None else acc + term
    return acc


def sweep_kernel(n_contact, n_body, last, *refs):
    gx, gy = contact_groups(n_contact)
    if last:
        (tb_ref, push_ref,
         tot_out,
         own_buf, later_buf, recv3, xbuf, ybuf, tot_buf,
         s_sem, r_sem, sx_sem, rx_sem, sy_sem, ry_sem) = refs
    else:
        (tb_ref, push_ref, vfree_ref, imass_ref,
         rows_out,
         own_buf, later_buf, recv3, xbuf, ybuf, vel_buf, vel_next, velf, rows_buf,
         s_sem, r_sem, sx_sem, rx_sem, sy_sem, ry_sem) = refs
    blocks = own_buf.shape[0]
    width = own_buf.shape[1]
    half = blocks // 2
    c = lax.axis_index("contact")
    b = lax.axis_index("body")
    core = lax.rem(c, 2)
    x = lax.rem(c // 2, gx)
    y = c // (2 * gx)
    mate = c + 1 - 2 * core
    up = lax.rem(b + 1, n_body)
    down = lax.rem(b + n_body - 1, n_body)
    x_peers = [(y * gx + lax.rem(x + j, gx)) * 2 + core for j in range(1, gx)]
    y_peers = [(lax.rem(y + j, gy) * gx + x) * 2 + core for j in range(1, gy)]

    greet = [(mate, b), (c, up), (mate, up), (c, down), (mate, down)]
    greet += [(p, b) for p in x_peers] + [(p, b) for p in y_peers]
    barrier = pltpu.get_barrier_semaphore()
    for dev in greet:
        pl.semaphore_signal(barrier, inc=1, device_id=dev, device_id_type=MESH)
    later_buf[...] = scatter_rows(tb_ref, 1, push_ref, blocks)
    own_buf[...] = scatter_rows(tb_ref, 0, push_ref, blocks)
    pl.semaphore_wait(barrier, len(greet))

    def remote(src, dst, send, recv, dev):
        return pltpu.make_async_remote_copy(
            src_ref=src, dst_ref=dst, send_sem=send, recv_sem=recv,
            device_id=dev, device_id_type=MESH,
        )

    mine = pl.ds(pl.multiple_of(core * half, half), half)
    theirs = pl.ds(pl.multiple_of((1 - core) * half, half), half)
    sent = []
    for k, (src, dev) in enumerate(((later_buf.at[mine], (c, up)), (later_buf.at[theirs], (mate, up)))):
        cp = remote(src, recv3.at[1 + k], s_sem.at[1 + k], r_sem.at[1 + k], dev)
        cp.start()
        sent.append(cp)
    cp = remote(own_buf.at[theirs], recv3.at[0], s_sem.at[0], r_sem.at[0], (mate, b))
    cp.start()
    sent.append(cp)
    for k, dev in enumerate(((mate, b), (c, down), (mate, down))):
        remote(own_buf.at[mine], recv3.at[k], s_sem.at[k], r_sem.at[k], dev).wait_recv()
    part = own_buf[mine] + recv3[0] + recv3[1] + recv3[2]

    rounds = [(xbuf, x, x_peers, gx, sx_sem, rx_sem), (ybuf, y, y_peers, gy, sy_sem, ry_sem)]
    if gx == gy:
        first = [xv * (1 - core) + yv * core for xv, yv in zip([x] + x_peers, [y] + y_peers)]
        second = [xv * core + yv * (1 - core) for xv, yv in zip([x] + x_peers, [y] + y_peers)]
        rounds = [(xbuf, first[0], first[1:], gx, sx_sem, rx_sem),
                  (ybuf, second[0], second[1:], gy, sy_sem, ry_sem)]
    for buf, pos, peers, size, ssem, rsem in rounds:
        if size == 1:
            continue
        buf[pos] = part
        for j, p in enumerate(peers):
            cp = remote(buf.at[pos], buf.at[pos], ssem.at[j], rsem.at[pos], (p, b))
            cp.start()
            sent.append(cp)
        for j in range(1, size):
            src_pos = lax.rem(pos + size - j, size)
            remote(buf.at[src_pos], buf.at[src_pos], ssem.at[0], rsem.at[src_pos], (peers[-j], b)).wait_recv()
        part = buf[0]
        for g in range(1, size):
            part = part + buf[g]

    if last:
        tot_buf[mine] = part
        cp = remote(tot_buf.at[mine], tot_buf.at[mine], s_sem.at[3], r_sem.at[3], (mate, b))
        cp.start()
        sent.append(cp)
        remote(tot_buf.at[theirs], tot_buf.at[theirs], s_sem.at[3], r_sem.at[3], (mate, b)).wait_recv()
        tot_out[...] = tot_buf[...]
    else:
        vel = vfree_ref[mine] + imass_ref[mine] * part
        vel_buf[mine] = vel.astype(jnp.bfloat16)
        src = vel_buf.at[mine]
        for k, (dst, dev) in enumerate((
            (vel_buf.at[mine], (mate, b)),
            (vel_next.at[mine], (c, down)),
            (vel_next.at[mine], (mate, down)),
        )):
            cp = remote(src, dst, s_sem.at[3 + k], r_sem.at[3 + k], dev)
            cp.start()
            sent.append(cp)
        for k, (dst, dev) in enumerate((
            (vel_buf.at[theirs], (mate, b)),
            (vel_next.at[mine], (c, up)),
            (vel_next.at[theirs], (mate, up)),
        )):
            remote(src, dst, s_sem.at[3 + k], r_sem.at[3 + k], dev).wait_recv()
        velf[0] = vel_buf[...].astype(jnp.float32)
        velf[1] = vel_next[...].astype(jnp.float32)
        tiles = rows_buf.shape[1]
        for column in range(2):
            for t in range(tiles):
                rows_buf[column, pl.ds(t, 1), :] = velf[column, pl.ds(tb_ref[column, t], 1), :]
            rows_out[column] = rows_buf[column].astype(jnp.bfloat16)
    for cp in sent:
        cp.wait_send()


def sweep_exchange(tile_block, push, vel_free, inv_mass, n_contact, n_body, last):
    gx, gy = contact_groups(n_contact)
    blocks, width = vel_free.shape
    tiles = push.shape[1]
    half = blocks // 2
    vspec = pl.BlockSpec(memory_space=pltpu.VMEM)
    sspec = pl.BlockSpec(memory_space=pltpu.SMEM)
    if last:
        args = [tile_block, push]
        out_shape = jax.ShapeDtypeStruct((blocks, width), jnp.float32)
        tail = [pltpu.VMEM((blocks, width), jnp.float32)]
    else:
        args = [tile_block, push, vel_free, inv_mass]
        out_shape = jax.ShapeDtypeStruct((2, tiles, width), jnp.bfloat16)
        tail = [
            pltpu.VMEM((blocks, width), jnp.bfloat16),
            pltpu.VMEM((blocks, width), jnp.bfloat16),
            pltpu.VMEM((2, blocks, width), jnp.float32),
            pltpu.VMEM((2, tiles, width), jnp.float32),
        ]
    scratch = [
        pltpu.VMEM((blocks, width), jnp.float32),
        pltpu.VMEM((blocks, width), jnp.float32),
        pltpu.VMEM((3, half, width), jnp.float32),
        pltpu.VMEM((gx, half, width), jnp.float32),
        pltpu.VMEM((gy, half, width), jnp.float32),
        *tail,
        pltpu.SemaphoreType.DMA((6,)),
        pltpu.SemaphoreType.DMA((6,)),
        pltpu.SemaphoreType.DMA((max(gx - 1, 1),)),
        pltpu.SemaphoreType.DMA((gx,)),
        pltpu.SemaphoreType.DMA((max(gy - 1, 1),)),
        pltpu.SemaphoreType.DMA((gy,)),
    ]
    return pl.pallas_call(
        functools.partial(sweep_kernel, n_contact, n_body, last),
        out_shape=out_shape,
        in_specs=[sspec] + [vspec] * (len(args) - 1),
        out_specs=vspec,
        scratch_shapes=scratch,
        compiler_params=pltpu.CompilerParams(
            collective_id=1 if last else 0, has_side_effects=True
        ),
    )(*args)


def dual_kernel(n_contact, n_body, *refs):
    gx, gy = contact_groups(n_contact)
    (tb_ref, push_ref, vfree_ref, imass_ref,
     rows_out,
     own_buf, later_buf, recv6, xbuf, ybuf, vel_buf, velf, rows_buf, vn_send, vnext_ref,
     s_sem, r_sem, sx_sem, rx_sem, sy_sem, ry_sem) = refs
    blocks = own_buf.shape[0]
    width = own_buf.shape[1]
    half = blocks // 2
    c = lax.axis_index("contact")
    b = lax.axis_index("body")
    core = lax.rem(c, 2)
    x = lax.rem(c // 2, gx)
    y = c // (2 * gx)
    mate = c + 1 - 2 * core
    up = lax.rem(b + 1, n_body)
    down = lax.rem(b + n_body - 1, n_body)
    x_peers = [(y * gx + lax.rem(x + j, gx)) * 2 + core for j in range(1, gx)]
    y_peers = [(lax.rem(y + j, gy) * gx + x) * 2 + core for j in range(1, gy)]

    greet = [(mate, b), (c, up), (mate, up), (c, down), (mate, down)]
    greet += [(p, b) for p in x_peers] + [(p, b) for p in y_peers]
    mine = pl.ds(pl.multiple_of(core * half, half), half)
    theirs = pl.ds(pl.multiple_of((1 - core) * half, half), half)
    barrier = pltpu.get_barrier_semaphore()
    for dev in greet:
        pl.semaphore_signal(barrier, inc=1, device_id=dev, device_id_type=MESH)
    later_buf[...] = scatter_rows(tb_ref, 1, push_ref, blocks)
    own_buf[...] = scatter_rows(tb_ref, 0, push_ref, blocks)
    vn_send[0] = vfree_ref[mine]
    vn_send[1] = imass_ref[mine]
    pl.semaphore_wait(barrier, len(greet))

    def remote(src, dst, send, recv, dev):
        return pltpu.make_async_remote_copy(
            src_ref=src, dst_ref=dst, send_sem=send, recv_sem=recv,
            device_id=dev, device_id_type=MESH,
        )

    sent = []
    plan = (
        (later_buf.at[mine], (c, up)),
        (later_buf.at[theirs], (mate, up)),
        (later_buf.at[theirs], (mate, b)),
    )
    for k, (src, dev) in enumerate(plan):
        cp = remote(src, recv6.at[k], s_sem.at[k], r_sem.at[k], dev)
        cp.start()
        sent.append(cp)
    plan = (
        (own_buf.at[mine], (c, down)),
        (own_buf.at[theirs], (mate, down)),
        (own_buf.at[theirs], (mate, b)),
    )
    for k, (src, dev) in enumerate(plan):
        cp = remote(src, recv6.at[3 + k], s_sem.at[3 + k], r_sem.at[3 + k], dev)
        cp.start()
        sent.append(cp)
    vcp = remote(vn_send, vnext_ref, s_sem.at[8], r_sem.at[8], (c, down))
    vcp.start()
    sent.append(vcp)
    senders = ((c, down), (mate, down), (mate, b), (c, up), (mate, up), (mate, b))
    for k, dev in enumerate(senders):
        remote(own_buf.at[mine], recv6.at[k], s_sem.at[k], r_sem.at[k], dev).wait_recv()
    part = jnp.concatenate([
        own_buf[mine] + recv6[5] + recv6[0] + recv6[1],
        later_buf[mine] + recv6[2] + recv6[3] + recv6[4],
    ], axis=0)

    rounds = [(xbuf, x, x_peers, gx, sx_sem, rx_sem), (ybuf, y, y_peers, gy, sy_sem, ry_sem)]
    if gx == gy:
        first = [xv * (1 - core) + yv * core for xv, yv in zip([x] + x_peers, [y] + y_peers)]
        second = [xv * core + yv * (1 - core) for xv, yv in zip([x] + x_peers, [y] + y_peers)]
        rounds = [(xbuf, first[0], first[1:], gx, sx_sem, rx_sem),
                  (ybuf, second[0], second[1:], gy, sy_sem, ry_sem)]
    for buf, pos, peers, size, ssem, rsem in rounds:
        if size == 1:
            continue
        buf[pos] = part
        for j, p in enumerate(peers):
            cp = remote(buf.at[pos], buf.at[pos], ssem.at[j], rsem.at[pos], (p, b))
            cp.start()
            sent.append(cp)
        for j in range(1, size):
            src_pos = lax.rem(pos + size - j, size)
            remote(buf.at[src_pos], buf.at[src_pos], ssem.at[0], rsem.at[src_pos], (peers[-j], b)).wait_recv()
        part = buf[0]
        for g in range(1, size):
            part = part + buf[g]

    vel_buf[0, mine] = (vfree_ref[mine] + imass_ref[mine] * part[:half]).astype(jnp.bfloat16)
    remote(vn_send, vnext_ref, s_sem.at[8], r_sem.at[8], (c, up)).wait_recv()
    vel_buf[1, mine] = (vnext_ref[0] + vnext_ref[1] * part[half:]).astype(jnp.bfloat16)
    for k in range(2):
        cp = remote(vel_buf.at[k, mine], vel_buf.at[k, mine], s_sem.at[6 + k], r_sem.at[6 + k], (mate, b))
        cp.start()
        sent.append(cp)
    for k in range(2):
        remote(vel_buf.at[k, theirs], vel_buf.at[k, theirs], s_sem.at[6 + k], r_sem.at[6 + k], (mate, b)).wait_recv()
    velf[...] = vel_buf[...].astype(jnp.float32)
    tiles = rows_buf.shape[1]
    for column in range(2):
        for t in range(tiles):
            rows_buf[column, pl.ds(t, 1), :] = velf[column, pl.ds(tb_ref[column, t], 1), :]
        rows_out[column] = rows_buf[column].astype(jnp.bfloat16)
    for cp in sent:
        cp.wait_send()


def dual_exchange(tile_block, push, vel_free, inv_mass, n_contact, n_body):
    gx, gy = contact_groups(n_contact)
    blocks, width = vel_free.shape
    tiles = push.shape[1]
    half = blocks // 2
    vspec = pl.BlockSpec(memory_space=pltpu.VMEM)
    sspec = pl.BlockSpec(memory_space=pltpu.SMEM)
    scratch = [
        pltpu.VMEM((blocks, width), jnp.float32),
        pltpu.VMEM((blocks, width), jnp.float32),
        pltpu.VMEM((6, half, width), jnp.float32),
        pltpu.VMEM((gx, blocks, width), jnp.float32),
        pltpu.VMEM((gy, blocks, width), jnp.float32),
        pltpu.VMEM((2, blocks, width), jnp.bfloat16),
        pltpu.VMEM((2, blocks, width), jnp.float32),
        pltpu.VMEM((2, tiles, width), jnp.float32),
        pltpu.VMEM((2, half, width), jnp.float32),
        pltpu.VMEM((2, half, width), jnp.float32),
        pltpu.SemaphoreType.DMA((9,)),
        pltpu.SemaphoreType.DMA((9,)),
        pltpu.SemaphoreType.DMA((max(gx - 1, 1),)),
        pltpu.SemaphoreType.DMA((gx,)),
        pltpu.SemaphoreType.DMA((max(gy - 1, 1),)),
        pltpu.SemaphoreType.DMA((gy,)),
    ]
    return pl.pallas_call(
        functools.partial(dual_kernel, n_contact, n_body),
        out_shape=jax.ShapeDtypeStruct((2, tiles, width), jnp.bfloat16),
        in_specs=[sspec] + [vspec] * 3,
        out_specs=vspec,
        scratch_shapes=scratch,
        compiler_params=pltpu.CompilerParams(collective_id=2, has_side_effects=True),
    )(tile_block, push, vel_free, inv_mass)


def final_kernel(n_contact, n_body, *refs):
    gx, gy = contact_groups(n_contact)
    (tb_ref, push_ref,
     tot_out,
     own_buf, later_buf, recv2, fbuf, lsend, sbuf, tot_buf,
     s_sem, r_sem, fs_sem, fr_sem, ss_sem, sr_sem) = refs
    blocks = own_buf.shape[0]
    half = blocks // 2
    c = lax.axis_index("contact")
    b = lax.axis_index("body")
    core = lax.rem(c, 2)
    x = lax.rem(c // 2, gx)
    y = c // (2 * gx)
    mate = c + 1 - 2 * core
    up = lax.rem(b + 1, n_body)
    down = lax.rem(b + n_body - 1, n_body)
    x_peers = [(y * gx + lax.rem(x + j, gx)) * 2 + core for j in range(1, gx)]
    y_peers = [(lax.rem(y + j, gy) * gx + x) * 2 + core for j in range(1, gy)]
    pos1, peers1, size1, pos2, peers2, size2 = x, x_peers, gx, y, y_peers, gy
    if gx == gy:
        first = [xv * (1 - core) + yv * core for xv, yv in zip([x] + x_peers, [y] + y_peers)]
        second = [xv * core + yv * (1 - core) for xv, yv in zip([x] + x_peers, [y] + y_peers)]
        pos1, peers1, pos2, peers2 = first[0], first[1:], second[0], second[1:]

    greet = [(mate, b), (c, up), (c, down)]
    greet += [(p, b) for p in peers1] + [(p, up) for p in peers1] + [(p, down) for p in peers1]
    greet += [(p, b) for p in peers2]
    barrier = pltpu.get_barrier_semaphore()
    for dev in greet:
        pl.semaphore_signal(barrier, inc=1, device_id=dev, device_id_type=MESH)
    later_buf[...] = scatter_rows(tb_ref, 1, push_ref, blocks)
    own_buf[...] = scatter_rows(tb_ref, 0, push_ref, blocks)
    pl.semaphore_wait(barrier, len(greet))

    def remote(src, dst, send, recv, dev):
        return pltpu.make_async_remote_copy(
            src_ref=src, dst_ref=dst, send_sem=send, recv_sem=recv,
            device_id=dev, device_id_type=MESH,
        )

    mine = pl.ds(pl.multiple_of(core * half, half), half)
    theirs = pl.ds(pl.multiple_of((1 - core) * half, half), half)
    sent = []
    for k, src in enumerate((own_buf.at[theirs], later_buf.at[theirs])):
        cp = remote(src, recv2.at[k], s_sem.at[k], r_sem.at[k], (mate, b))
        cp.start()
        sent.append(cp)
    for k in range(2):
        remote(own_buf.at[mine], recv2.at[k], s_sem.at[k], r_sem.at[k], (mate, b)).wait_recv()
    fbuf[pos1] = own_buf[mine] + recv2[0]
    lsend[...] = later_buf[mine] + recv2[1]

    for j, p in enumerate(peers1):
        cp = remote(fbuf.at[pos1], fbuf.at[pos1], fs_sem.at[j], fr_sem.at[pos1], (p, b))
        cp.start()
        sent.append(cp)
    for j, p in enumerate([c] + peers1):
        cp = remote(lsend, fbuf.at[size1 + pos1], fs_sem.at[size1 - 1 + j],
                    fr_sem.at[size1 + pos1], (p, up))
        cp.start()
        sent.append(cp)
    for j in range(1, size1):
        q = lax.rem(pos1 + j, size1)
        remote(lsend, fbuf.at[q], fs_sem.at[0], fr_sem.at[q], (peers1[j - 1], b)).wait_recv()
    for j, p in enumerate([c] + peers1):
        q = lax.rem(pos1 + j, size1)
        remote(lsend, fbuf.at[size1 + q], fs_sem.at[0], fr_sem.at[size1 + q], (p, down)).wait_recv()
    part = fbuf[0]
    for g in range(1, 2 * size1):
        part = part + fbuf[g]

    if size2 > 1:
        sbuf[pos2] = part
        for j, p in enumerate(peers2):
            cp = remote(sbuf.at[pos2], sbuf.at[pos2], ss_sem.at[j], sr_sem.at[pos2], (p, b))
            cp.start()
            sent.append(cp)
        for j in range(1, size2):
            src_pos = lax.rem(pos2 + size2 - j, size2)
            remote(sbuf.at[src_pos], sbuf.at[src_pos], ss_sem.at[0], sr_sem.at[src_pos], (peers2[-j], b)).wait_recv()
        part = sbuf[0]
        for g in range(1, size2):
            part = part + sbuf[g]

    tot_buf[mine] = part
    cp = remote(tot_buf.at[mine], tot_buf.at[mine], s_sem.at[2], r_sem.at[2], (mate, b))
    cp.start()
    sent.append(cp)
    remote(tot_buf.at[theirs], tot_buf.at[theirs], s_sem.at[2], r_sem.at[2], (mate, b)).wait_recv()
    tot_out[...] = tot_buf[...]
    for cp in sent:
        cp.wait_send()


def final_exchange(tile_block, push, vel_free, n_contact, n_body):
    gx, gy = contact_groups(n_contact)
    blocks, width = vel_free.shape
    half = blocks // 2
    vspec = pl.BlockSpec(memory_space=pltpu.VMEM)
    sspec = pl.BlockSpec(memory_space=pltpu.SMEM)
    scratch = [
        pltpu.VMEM((blocks, width), jnp.float32),
        pltpu.VMEM((blocks, width), jnp.float32),
        pltpu.VMEM((2, half, width), jnp.float32),
        pltpu.VMEM((2 * gx, half, width), jnp.float32),
        pltpu.VMEM((half, width), jnp.float32),
        pltpu.VMEM((gy, half, width), jnp.float32),
        pltpu.VMEM((blocks, width), jnp.float32),
        pltpu.SemaphoreType.DMA((3,)),
        pltpu.SemaphoreType.DMA((3,)),
        pltpu.SemaphoreType.DMA((2 * gx,)),
        pltpu.SemaphoreType.DMA((2 * gx,)),
        pltpu.SemaphoreType.DMA((max(gy - 1, 1),)),
        pltpu.SemaphoreType.DMA((gy,)),
    ]
    return pl.pallas_call(
        functools.partial(final_kernel, n_contact, n_body),
        out_shape=jax.ShapeDtypeStruct((blocks, width), jnp.float32),
        in_specs=[sspec, vspec],
        out_specs=vspec,
        scratch_shapes=scratch,
        compiler_params=pltpu.CompilerParams(collective_id=1, has_side_effects=True),
    )(tile_block, push)


def per_device(
    n_contact, n_body,
    jacobian, tile_block, tile_count, vel_free, inv_mass, bias, step_scale, friction, impulse_start,
):
    tiles_here = jacobian.shape[0]
    contacts = friction.shape[1]
    order = jnp.arange(tiles_here, dtype=jnp.int32)
    mask = (order < tile_count[0]).astype(jnp.float32)[:, None]

    def pushes(lam):
        lamb = lam.astype(jnp.bfloat16)
        return jnp.einsum("tkbc,tc->ktb", jacobian, lamb, preferred_element_type=jnp.float32)

    lam = impulse_start * mask
    for sweep in range(ITERS):
        rows = dual_exchange(tile_block.T, pushes(lam), vel_free, inv_mass, n_contact, n_body)
        rel = jnp.einsum("tkbc,ktb->tc", jacobian, rows, preferred_element_type=jnp.float32) + bias
        lam = project(lam - step_scale * rel, friction, contacts) * mask
    total = final_exchange(tile_block.T, pushes(lam), vel_free, n_contact, n_body)
    velocity = vel_free + inv_mass * total
    return (lam, velocity)


def solution(mesh):
    n_contact = mesh.shape["contact"]
    n_body = mesh.shape["body"]
    placed = (
        P(("contact", "body"), None, None, None),
        P(("contact", "body"), None),
        P(("contact", "body")),
        P("body", None),
        P("body", None),
        P(("contact", "body"), None),
        P(("contact", "body"), None),
        P(("contact", "body"), None),
        P(("contact", "body"), None),
    )
    return jax.shard_map(
        functools.partial(per_device, n_contact, n_body),
        mesh=mesh,
        in_specs=placed,
        out_specs=(P(("contact", "body"), None), P("body", None)),
        check_vma=False,
    )
```

```python
import functools
import math

import jax
import jax.numpy as jnp
from jax import lax
from jax.experimental import pallas as pl
from jax.experimental.pallas import tpu as pltpu
from jax.sharding import PartitionSpec as P

ITERS = 2
MESH = pl.DeviceIdType.MESH


def project(trial, friction, contacts):
    normal = trial[:, :contacts]
    first = trial[:, contacts : 2 * contacts]
    second = trial[:, 2 * contacts :]
    tangent = jnp.sqrt(first * first + second * second)
    inside = tangent <= friction * normal
    below = friction * tangent <= -normal
    moved = (normal + friction * tangent) / (1.0 + friction * friction)
    safe = jnp.where(inside | below, 1.0, tangent)
    factor = jnp.where(inside, 1.0, jnp.where(below, 0.0, friction * moved / safe))
    new_normal = jnp.where(inside, normal, jnp.where(below, 0.0, moved))
    return jnp.concatenate([new_normal, first * factor, second * factor], axis=1)


def contact_groups(n_contact):
    rest = n_contact // 2
    gy = 1
    for d in range(1, int(math.isqrt(rest)) + 1):
        if rest % d == 0:
            gy = d
    return rest // gy, gy


def scatter_rows(tb_ref, column, push_ref, blocks, tile_major=False):
    tiles = push_ref.shape[0] if tile_major else push_ref.shape[1]
    width = push_ref.shape[2]
    slot = lax.broadcasted_iota(jnp.int32, (blocks, width), 0)
    acc = None
    for t in range(tiles):
        if tile_major:
            row = push_ref[t, column : column + 1, :]
        else:
            row = push_ref[column, t : t + 1, :]
        term = jnp.where(slot == tb_ref[column, t], row, 0.0)
        acc = term if acc is None else acc + term
    return acc


def sweep_kernel(n_contact, n_body, last, *refs):
    gx, gy = contact_groups(n_contact)
    if last:
        (tb_ref, push_ref,
         tot_out,
         own_buf, later_buf, recv3, xbuf, ybuf, tot_buf,
         s_sem, r_sem, sx_sem, rx_sem, sy_sem, ry_sem) = refs
    else:
        (tb_ref, push_ref, vfree_ref, imass_ref,
         rows_out,
         own_buf, later_buf, recv3, xbuf, ybuf, vel_buf, vel_next, velf, rows_buf,
         s_sem, r_sem, sx_sem, rx_sem, sy_sem, ry_sem) = refs
    blocks = own_buf.shape[0]
    width = own_buf.shape[1]
    half = blocks // 2
    c = lax.axis_index("contact")
    b = lax.axis_index("body")
    core = lax.rem(c, 2)
    x = lax.rem(c // 2, gx)
    y = c // (2 * gx)
    mate = c + 1 - 2 * core
    up = lax.rem(b + 1, n_body)
    down = lax.rem(b + n_body - 1, n_body)
    x_peers = [(y * gx + lax.rem(x + j, gx)) * 2 + core for j in range(1, gx)]
    y_peers = [(lax.rem(y + j, gy) * gx + x) * 2 + core for j in range(1, gy)]

    greet = [(mate, b), (c, up), (mate, up), (c, down), (mate, down)]
    greet += [(p, b) for p in x_peers] + [(p, b) for p in y_peers]
    barrier = pltpu.get_barrier_semaphore()
    for dev in greet:
        pl.semaphore_signal(barrier, inc=1, device_id=dev, device_id_type=MESH)
    later_buf[...] = scatter_rows(tb_ref, 1, push_ref, blocks, last)
    own_buf[...] = scatter_rows(tb_ref, 0, push_ref, blocks, last)
    pl.semaphore_wait(barrier, len(greet))

    def remote(src, dst, send, recv, dev):
        return pltpu.make_async_remote_copy(
            src_ref=src, dst_ref=dst, send_sem=send, recv_sem=recv,
            device_id=dev, device_id_type=MESH,
        )

    mine = pl.ds(pl.multiple_of(core * half, half), half)
    theirs = pl.ds(pl.multiple_of((1 - core) * half, half), half)
    sent = []
    for k, (src, dev) in enumerate(((later_buf.at[mine], (c, up)), (later_buf.at[theirs], (mate, up)))):
        cp = remote(src, recv3.at[1 + k], s_sem.at[1 + k], r_sem.at[1 + k], dev)
        cp.start()
        sent.append(cp)
    cp = remote(own_buf.at[theirs], recv3.at[0], s_sem.at[0], r_sem.at[0], (mate, b))
    cp.start()
    sent.append(cp)
    for k, dev in enumerate(((mate, b), (c, down), (mate, down))):
        remote(own_buf.at[mine], recv3.at[k], s_sem.at[k], r_sem.at[k], dev).wait_recv()
    part = own_buf[mine] + recv3[0] + recv3[1] + recv3[2]

    rounds = [(xbuf, x, x_peers, gx, sx_sem, rx_sem), (ybuf, y, y_peers, gy, sy_sem, ry_sem)]
    if gx == gy:
        first = [xv * (1 - core) + yv * core for xv, yv in zip([x] + x_peers, [y] + y_peers)]
        second = [xv * core + yv * (1 - core) for xv, yv in zip([x] + x_peers, [y] + y_peers)]
        rounds = [(xbuf, first[0], first[1:], gx, sx_sem, rx_sem),
                  (ybuf, second[0], second[1:], gy, sy_sem, ry_sem)]
    for buf, pos, peers, size, ssem, rsem in rounds:
        if size == 1:
            continue
        buf[pos] = part
        for j, p in enumerate(peers):
            cp = remote(buf.at[pos], buf.at[pos], ssem.at[j], rsem.at[pos], (p, b))
            cp.start()
            sent.append(cp)
        for j in range(1, size):
            src_pos = lax.rem(pos + size - j, size)
            remote(buf.at[src_pos], buf.at[src_pos], ssem.at[0], rsem.at[src_pos], (peers[-j], b)).wait_recv()
        part = buf[0]
        for g in range(1, size):
            part = part + buf[g]

    if last:
        tot_buf[mine] = part
        cp = remote(tot_buf.at[mine], tot_buf.at[mine], s_sem.at[3], r_sem.at[3], (mate, b))
        cp.start()
        sent.append(cp)
        remote(tot_buf.at[theirs], tot_buf.at[theirs], s_sem.at[3], r_sem.at[3], (mate, b)).wait_recv()
        tot_out[...] = tot_buf[...]
    else:
        vel = vfree_ref[mine] + imass_ref[mine] * part
        vel_buf[mine] = vel.astype(jnp.bfloat16)
        src = vel_buf.at[mine]
        for k, (dst, dev) in enumerate((
            (vel_buf.at[mine], (mate, b)),
            (vel_next.at[mine], (c, down)),
            (vel_next.at[mine], (mate, down)),
        )):
            cp = remote(src, dst, s_sem.at[3 + k], r_sem.at[3 + k], dev)
            cp.start()
            sent.append(cp)
        for k, (dst, dev) in enumerate((
            (vel_buf.at[theirs], (mate, b)),
            (vel_next.at[mine], (c, up)),
            (vel_next.at[theirs], (mate, up)),
        )):
            remote(src, dst, s_sem.at[3 + k], r_sem.at[3 + k], dev).wait_recv()
        velf[0] = vel_buf[...].astype(jnp.float32)
        velf[1] = vel_next[...].astype(jnp.float32)
        tiles = rows_buf.shape[1]
        for column in range(2):
            for t in range(tiles):
                rows_buf[column, pl.ds(t, 1), :] = velf[column, pl.ds(tb_ref[column, t], 1), :]
            rows_out[column] = rows_buf[column].astype(jnp.bfloat16)
    for cp in sent:
        cp.wait_send()


def sweep_exchange(tile_block, push, vel_free, inv_mass, n_contact, n_body, last):
    gx, gy = contact_groups(n_contact)
    blocks, width = vel_free.shape
    tiles = push.shape[0] if last else push.shape[1]
    half = blocks // 2
    vspec = pl.BlockSpec(memory_space=pltpu.VMEM)
    sspec = pl.BlockSpec(memory_space=pltpu.SMEM)
    if last:
        args = [tile_block, push]
        out_shape = jax.ShapeDtypeStruct((blocks, width), jnp.float32)
        tail = [pltpu.VMEM((blocks, width), jnp.float32)]
    else:
        args = [tile_block, push, vel_free, inv_mass]
        out_shape = jax.ShapeDtypeStruct((2, tiles, width), jnp.bfloat16)
        tail = [
            pltpu.VMEM((blocks, width), jnp.bfloat16),
            pltpu.VMEM((blocks, width), jnp.bfloat16),
            pltpu.VMEM((2, blocks, width), jnp.float32),
            pltpu.VMEM((2, tiles, width), jnp.float32),
        ]
    scratch = [
        pltpu.VMEM((blocks, width), jnp.float32),
        pltpu.VMEM((blocks, width), jnp.float32),
        pltpu.VMEM((3, half, width), jnp.float32),
        pltpu.VMEM((gx, half, width), jnp.float32),
        pltpu.VMEM((gy, half, width), jnp.float32),
        *tail,
        pltpu.SemaphoreType.DMA((6,)),
        pltpu.SemaphoreType.DMA((6,)),
        pltpu.SemaphoreType.DMA((max(gx - 1, 1),)),
        pltpu.SemaphoreType.DMA((gx,)),
        pltpu.SemaphoreType.DMA((max(gy - 1, 1),)),
        pltpu.SemaphoreType.DMA((gy,)),
    ]
    return pl.pallas_call(
        functools.partial(sweep_kernel, n_contact, n_body, last),
        out_shape=out_shape,
        in_specs=[sspec] + [vspec] * (len(args) - 1),
        out_specs=vspec,
        scratch_shapes=scratch,
        compiler_params=pltpu.CompilerParams(
            collective_id=1 if last else 0, has_side_effects=True
        ),
    )(*args)


def dual_kernel(n_contact, n_body, *refs):
    gx, gy = contact_groups(n_contact)
    (tb_ref, push_ref, vfree_ref, imass_ref,
     rows_out,
     own_buf, later_buf, recv6, xbuf, ybuf, vel_buf, velf, rows_buf, vn_send, vnext_ref,
     s_sem, r_sem, sx_sem, rx_sem, sy_sem, ry_sem) = refs
    blocks = own_buf.shape[0]
    width = own_buf.shape[1]
    half = blocks // 2
    c = lax.axis_index("contact")
    b = lax.axis_index("body")
    core = lax.rem(c, 2)
    x = lax.rem(c // 2, gx)
    y = c // (2 * gx)
    mate = c + 1 - 2 * core
    up = lax.rem(b + 1, n_body)
    down = lax.rem(b + n_body - 1, n_body)
    x_peers = [(y * gx + lax.rem(x + j, gx)) * 2 + core for j in range(1, gx)]
    y_peers = [(lax.rem(y + j, gy) * gx + x) * 2 + core for j in range(1, gy)]

    greet = [(mate, b), (c, up), (mate, up), (c, down), (mate, down)]
    greet += [(p, b) for p in x_peers] + [(p, b) for p in y_peers]
    mine = pl.ds(pl.multiple_of(core * half, half), half)
    theirs = pl.ds(pl.multiple_of((1 - core) * half, half), half)
    barrier = pltpu.get_barrier_semaphore()
    for dev in greet:
        pl.semaphore_signal(barrier, inc=1, device_id=dev, device_id_type=MESH)
    later_buf[...] = scatter_rows(tb_ref, 1, push_ref, blocks)
    own_buf[...] = scatter_rows(tb_ref, 0, push_ref, blocks)
    vn_send[0] = vfree_ref[mine]
    vn_send[1] = imass_ref[mine]
    pl.semaphore_wait(barrier, len(greet))

    def remote(src, dst, send, recv, dev):
        return pltpu.make_async_remote_copy(
            src_ref=src, dst_ref=dst, send_sem=send, recv_sem=recv,
            device_id=dev, device_id_type=MESH,
        )

    sent = []
    plan = (
        (later_buf.at[mine], (c, up)),
        (later_buf.at[theirs], (mate, up)),
        (later_buf.at[theirs], (mate, b)),
    )
    for k, (src, dev) in enumerate(plan):
        cp = remote(src, recv6.at[k], s_sem.at[k], r_sem.at[k], dev)
        cp.start()
        sent.append(cp)
    plan = (
        (own_buf.at[mine], (c, down)),
        (own_buf.at[theirs], (mate, down)),
        (own_buf.at[theirs], (mate, b)),
    )
    for k, (src, dev) in enumerate(plan):
        cp = remote(src, recv6.at[3 + k], s_sem.at[3 + k], r_sem.at[3 + k], dev)
        cp.start()
        sent.append(cp)
    vcp = remote(vn_send, vnext_ref, s_sem.at[8], r_sem.at[8], (c, down))
    vcp.start()
    sent.append(vcp)
    senders = ((c, down), (mate, down), (mate, b), (c, up), (mate, up), (mate, b))
    for k, dev in enumerate(senders):
        remote(own_buf.at[mine], recv6.at[k], s_sem.at[k], r_sem.at[k], dev).wait_recv()
    part = jnp.concatenate([
        own_buf[mine] + recv6[5] + recv6[0] + recv6[1],
        later_buf[mine] + recv6[2] + recv6[3] + recv6[4],
    ], axis=0)

    rounds = [(xbuf, x, x_peers, gx, sx_sem, rx_sem), (ybuf, y, y_peers, gy, sy_sem, ry_sem)]
    if gx == gy:
        first = [xv * (1 - core) + yv * core for xv, yv in zip([x] + x_peers, [y] + y_peers)]
        second = [xv * core + yv * (1 - core) for xv, yv in zip([x] + x_peers, [y] + y_peers)]
        rounds = [(xbuf, first[0], first[1:], gx, sx_sem, rx_sem),
                  (ybuf, second[0], second[1:], gy, sy_sem, ry_sem)]
    for buf, pos, peers, size, ssem, rsem in rounds:
        if size == 1:
            continue
        buf[pos] = part
        for j, p in enumerate(peers):
            cp = remote(buf.at[pos], buf.at[pos], ssem.at[j], rsem.at[pos], (p, b))
            cp.start()
            sent.append(cp)
        for j in range(1, size):
            src_pos = lax.rem(pos + size - j, size)
            remote(buf.at[src_pos], buf.at[src_pos], ssem.at[0], rsem.at[src_pos], (peers[-j], b)).wait_recv()
        part = buf[0]
        for g in range(1, size):
            part = part + buf[g]

    vel_buf[0, mine] = (vfree_ref[mine] + imass_ref[mine] * part[:half]).astype(jnp.bfloat16)
    remote(vn_send, vnext_ref, s_sem.at[8], r_sem.at[8], (c, up)).wait_recv()
    vel_buf[1, mine] = (vnext_ref[0] + vnext_ref[1] * part[half:]).astype(jnp.bfloat16)
    for k in range(2):
        cp = remote(vel_buf.at[k, mine], vel_buf.at[k, mine], s_sem.at[6 + k], r_sem.at[6 + k], (mate, b))
        cp.start()
        sent.append(cp)
    for k in range(2):
        remote(vel_buf.at[k, theirs], vel_buf.at[k, theirs], s_sem.at[6 + k], r_sem.at[6 + k], (mate, b)).wait_recv()
    velf[...] = vel_buf[...].astype(jnp.float32)
    tiles = rows_buf.shape[1]
    for column in range(2):
        for t in range(tiles):
            rows_buf[column, pl.ds(t, 1), :] = velf[column, pl.ds(tb_ref[column, t], 1), :]
        rows_out[column] = rows_buf[column].astype(jnp.bfloat16)
    for cp in sent:
        cp.wait_send()


def dual_exchange(tile_block, push, vel_free, inv_mass, n_contact, n_body):
    gx, gy = contact_groups(n_contact)
    blocks, width = vel_free.shape
    tiles = push.shape[1]
    half = blocks // 2
    vspec = pl.BlockSpec(memory_space=pltpu.VMEM)
    sspec = pl.BlockSpec(memory_space=pltpu.SMEM)
    scratch = [
        pltpu.VMEM((blocks, width), jnp.float32),
        pltpu.VMEM((blocks, width), jnp.float32),
        pltpu.VMEM((6, half, width), jnp.float32),
        pltpu.VMEM((gx, blocks, width), jnp.float32),
        pltpu.VMEM((gy, blocks, width), jnp.float32),
        pltpu.VMEM((2, blocks, width), jnp.bfloat16),
        pltpu.VMEM((2, blocks, width), jnp.float32),
        pltpu.VMEM((2, tiles, width), jnp.float32),
        pltpu.VMEM((2, half, width), jnp.float32),
        pltpu.VMEM((2, half, width), jnp.float32),
        pltpu.SemaphoreType.DMA((9,)),
        pltpu.SemaphoreType.DMA((9,)),
        pltpu.SemaphoreType.DMA((max(gx - 1, 1),)),
        pltpu.SemaphoreType.DMA((gx,)),
        pltpu.SemaphoreType.DMA((max(gy - 1, 1),)),
        pltpu.SemaphoreType.DMA((gy,)),
    ]
    return pl.pallas_call(
        functools.partial(dual_kernel, n_contact, n_body),
        out_shape=jax.ShapeDtypeStruct((2, tiles, width), jnp.bfloat16),
        in_specs=[sspec] + [vspec] * 3,
        out_specs=vspec,
        scratch_shapes=scratch,
        compiler_params=pltpu.CompilerParams(collective_id=2, has_side_effects=True),
    )(tile_block, push, vel_free, inv_mass)


def per_device(
    n_contact, n_body,
    jacobian, tile_block, tile_count, vel_free, inv_mass, bias, step_scale, friction, impulse_start,
):
    tiles_here = jacobian.shape[0]
    contacts = friction.shape[1]
    order = jnp.arange(tiles_here, dtype=jnp.int32)
    mask = (order < tile_count[0]).astype(jnp.float32)[:, None]

    def pushes(lam):
        lamb = lam.astype(jnp.bfloat16)
        return jnp.einsum("tkbc,tc->ktb", jacobian, lamb, preferred_element_type=jnp.float32)

    lam = impulse_start * mask
    for sweep in range(ITERS):
        rows = dual_exchange(tile_block.T, pushes(lam), vel_free, inv_mass, n_contact, n_body)
        rel = jnp.einsum("tkbc,ktb->tc", jacobian, rows, preferred_element_type=jnp.float32) + bias
        lam = project(lam - step_scale * rel, friction, contacts) * mask
    lamb = lam.astype(jnp.bfloat16).astype(jnp.float32)
    push = jnp.sum(jacobian.astype(jnp.float32) * lamb[:, None, None, :], axis=-1)
    total = sweep_exchange(tile_block.T, push, vel_free, inv_mass, n_contact, n_body, True)
    velocity = vel_free + inv_mass * total
    return (lam, velocity)


def solution(mesh):
    n_contact = mesh.shape["contact"]
    n_body = mesh.shape["body"]
    placed = (
        P(("contact", "body"), None, None, None),
        P(("contact", "body"), None),
        P(("contact", "body")),
        P("body", None),
        P("body", None),
        P(("contact", "body"), None),
        P(("contact", "body"), None),
        P(("contact", "body"), None),
        P(("contact", "body"), None),
    )
    return jax.shard_map(
        functools.partial(per_device, n_contact, n_body),
        mesh=mesh,
        in_specs=placed,
        out_specs=(P(("contact", "body"), None), P("body", None)),
        check_vma=False,
    )
```

```python
import functools
import math

import jax
import jax.numpy as jnp
from jax import lax
from jax.experimental import pallas as pl
from jax.experimental.pallas import tpu as pltpu
from jax.sharding import PartitionSpec as P

ITERS = 2
MESH = pl.DeviceIdType.MESH


def project(trial, friction, contacts):
    normal = trial[:, :contacts]
    first = trial[:, contacts : 2 * contacts]
    second = trial[:, 2 * contacts :]
    tangent = jnp.sqrt(first * first + second * second)
    inside = tangent <= friction * normal
    below = friction * tangent <= -normal
    moved = (normal + friction * tangent) / (1.0 + friction * friction)
    safe = jnp.where(inside | below, 1.0, tangent)
    factor = jnp.where(inside, 1.0, jnp.where(below, 0.0, friction * moved / safe))
    new_normal = jnp.where(inside, normal, jnp.where(below, 0.0, moved))
    return jnp.concatenate([new_normal, first * factor, second * factor], axis=1)


def contact_groups(n_contact):
    rest = n_contact // 2
    gy = 1
    for d in range(1, int(math.isqrt(rest)) + 1):
        if rest % d == 0:
            gy = d
    return rest // gy, gy


def scatter_rows(tb_ref, column, push_ref, blocks, tile_major=False):
    tiles = push_ref.shape[0] if tile_major else push_ref.shape[1]
    width = push_ref.shape[2]
    slot = lax.broadcasted_iota(jnp.int32, (blocks, width), 0)
    acc = None
    for t in range(tiles):
        if tile_major:
            row = push_ref[t, column : column + 1, :]
        else:
            row = push_ref[column, t : t + 1, :]
        term = jnp.where(slot == tb_ref[column, t], row, 0.0)
        acc = term if acc is None else acc + term
    return acc


def sweep_kernel(n_contact, n_body, last, *refs):
    gx, gy = contact_groups(n_contact)
    if last:
        (tb_ref, push_ref,
         tot_out,
         own_buf, later_buf, recv3, xbuf, ybuf, tot_buf,
         s_sem, r_sem, sx_sem, rx_sem, sy_sem, ry_sem) = refs
    else:
        (tb_ref, push_ref, vfree_ref, imass_ref,
         rows_out,
         own_buf, later_buf, recv3, xbuf, ybuf, vel_buf, vel_next, velf, rows_buf,
         s_sem, r_sem, sx_sem, rx_sem, sy_sem, ry_sem) = refs
    blocks = own_buf.shape[0]
    width = own_buf.shape[1]
    half = blocks // 2
    c = lax.axis_index("contact")
    b = lax.axis_index("body")
    core = lax.rem(c, 2)
    x = lax.rem(c // 2, gx)
    y = c // (2 * gx)
    mate = c + 1 - 2 * core
    up = lax.rem(b + 1, n_body)
    down = lax.rem(b + n_body - 1, n_body)
    x_peers = [(y * gx + lax.rem(x + j, gx)) * 2 + core for j in range(1, gx)]
    y_peers = [(lax.rem(y + j, gy) * gx + x) * 2 + core for j in range(1, gy)]

    greet = [(mate, b), (c, up), (mate, up), (c, down), (mate, down)]
    greet += [(p, b) for p in x_peers] + [(p, b) for p in y_peers]
    barrier = pltpu.get_barrier_semaphore()
    for dev in greet:
        pl.semaphore_signal(barrier, inc=1, device_id=dev, device_id_type=MESH)
    later_buf[...] = scatter_rows(tb_ref, 1, push_ref, blocks, last)
    own_buf[...] = scatter_rows(tb_ref, 0, push_ref, blocks, last)
    pl.semaphore_wait(barrier, len(greet))

    def remote(src, dst, send, recv, dev):
        return pltpu.make_async_remote_copy(
            src_ref=src, dst_ref=dst, send_sem=send, recv_sem=recv,
            device_id=dev, device_id_type=MESH,
        )

    mine = pl.ds(pl.multiple_of(core * half, half), half)
    theirs = pl.ds(pl.multiple_of((1 - core) * half, half), half)
    sent = []
    for k, (src, dev) in enumerate(((later_buf.at[mine], (c, up)), (later_buf.at[theirs], (mate, up)))):
        cp = remote(src, recv3.at[1 + k], s_sem.at[1 + k], r_sem.at[1 + k], dev)
        cp.start()
        sent.append(cp)
    cp = remote(own_buf.at[theirs], recv3.at[0], s_sem.at[0], r_sem.at[0], (mate, b))
    cp.start()
    sent.append(cp)
    for k, dev in enumerate(((mate, b), (c, down), (mate, down))):
        remote(own_buf.at[mine], recv3.at[k], s_sem.at[k], r_sem.at[k], dev).wait_recv()
    part = own_buf[mine] + recv3[0] + recv3[1] + recv3[2]

    rounds = [(xbuf, x, x_peers, gx, sx_sem, rx_sem), (ybuf, y, y_peers, gy, sy_sem, ry_sem)]
    if gx == gy:
        first = [xv * (1 - core) + yv * core for xv, yv in zip([x] + x_peers, [y] + y_peers)]
        second = [xv * core + yv * (1 - core) for xv, yv in zip([x] + x_peers, [y] + y_peers)]
        rounds = [(xbuf, first[0], first[1:], gx, sx_sem, rx_sem),
                  (ybuf, second[0], second[1:], gy, sy_sem, ry_sem)]
    for buf, pos, peers, size, ssem, rsem in rounds:
        if size == 1:
            continue
        buf[pos] = part
        for j in sorted(range(size - 1), key=lambda j: -min(j + 1, size - 1 - j)):
            p = peers[j]
            cp = remote(buf.at[pos], buf.at[pos], ssem.at[j], rsem.at[pos], (p, b))
            cp.start()
            sent.append(cp)
        for j in range(1, size):
            src_pos = lax.rem(pos + size - j, size)
            remote(buf.at[src_pos], buf.at[src_pos], ssem.at[0], rsem.at[src_pos], (peers[-j], b)).wait_recv()
        part = buf[0]
        for g in range(1, size):
            part = part + buf[g]

    if last:
        tot_buf[mine] = part
        cp = remote(tot_buf.at[mine], tot_buf.at[mine], s_sem.at[3], r_sem.at[3], (mate, b))
        cp.start()
        sent.append(cp)
        remote(tot_buf.at[theirs], tot_buf.at[theirs], s_sem.at[3], r_sem.at[3], (mate, b)).wait_recv()
        tot_out[...] = tot_buf[...]
    else:
        vel = vfree_ref[mine] + imass_ref[mine] * part
        vel_buf[mine] = vel.astype(jnp.bfloat16)
        src = vel_buf.at[mine]
        for k, (dst, dev) in enumerate((
            (vel_buf.at[mine], (mate, b)),
            (vel_next.at[mine], (c, down)),
            (vel_next.at[mine], (mate, down)),
        )):
            cp = remote(src, dst, s_sem.at[3 + k], r_sem.at[3 + k], dev)
            cp.start()
            sent.append(cp)
        for k, (dst, dev) in enumerate((
            (vel_buf.at[theirs], (mate, b)),
            (vel_next.at[mine], (c, up)),
            (vel_next.at[theirs], (mate, up)),
        )):
            remote(src, dst, s_sem.at[3 + k], r_sem.at[3 + k], dev).wait_recv()
        velf[0] = vel_buf[...].astype(jnp.float32)
        velf[1] = vel_next[...].astype(jnp.float32)
        tiles = rows_buf.shape[1]
        for column in range(2):
            for t in range(tiles):
                rows_buf[column, pl.ds(t, 1), :] = velf[column, pl.ds(tb_ref[column, t], 1), :]
            rows_out[column] = rows_buf[column].astype(jnp.bfloat16)
    for cp in sent:
        cp.wait_send()


def sweep_exchange(tile_block, push, vel_free, inv_mass, n_contact, n_body, last):
    gx, gy = contact_groups(n_contact)
    blocks, width = vel_free.shape
    tiles = push.shape[0] if last else push.shape[1]
    half = blocks // 2
    vspec = pl.BlockSpec(memory_space=pltpu.VMEM)
    sspec = pl.BlockSpec(memory_space=pltpu.SMEM)
    if last:
        args = [tile_block, push]
        out_shape = jax.ShapeDtypeStruct((blocks, width), jnp.float32)
        tail = [pltpu.VMEM((blocks, width), jnp.float32)]
    else:
        args = [tile_block, push, vel_free, inv_mass]
        out_shape = jax.ShapeDtypeStruct((2, tiles, width), jnp.bfloat16)
        tail = [
            pltpu.VMEM((blocks, width), jnp.bfloat16),
            pltpu.VMEM((blocks, width), jnp.bfloat16),
            pltpu.VMEM((2, blocks, width), jnp.float32),
            pltpu.VMEM((2, tiles, width), jnp.float32),
        ]
    scratch = [
        pltpu.VMEM((blocks, width), jnp.float32),
        pltpu.VMEM((blocks, width), jnp.float32),
        pltpu.VMEM((3, half, width), jnp.float32),
        pltpu.VMEM((gx, half, width), jnp.float32),
        pltpu.VMEM((gy, half, width), jnp.float32),
        *tail,
        pltpu.SemaphoreType.DMA((6,)),
        pltpu.SemaphoreType.DMA((6,)),
        pltpu.SemaphoreType.DMA((max(gx - 1, 1),)),
        pltpu.SemaphoreType.DMA((gx,)),
        pltpu.SemaphoreType.DMA((max(gy - 1, 1),)),
        pltpu.SemaphoreType.DMA((gy,)),
    ]
    return pl.pallas_call(
        functools.partial(sweep_kernel, n_contact, n_body, last),
        out_shape=out_shape,
        in_specs=[sspec] + [vspec] * (len(args) - 1),
        out_specs=vspec,
        scratch_shapes=scratch,
        compiler_params=pltpu.CompilerParams(
            collective_id=1 if last else 0, has_side_effects=True
        ),
    )(*args)


def dual_kernel(n_contact, n_body, *refs):
    gx, gy = contact_groups(n_contact)
    (tb_ref, push_ref, vfree_ref, imass_ref,
     rows_out,
     own_buf, later_buf, recv6, xbuf, ybuf, vel_buf, velf, rows_buf, vn_send, vnext_ref,
     s_sem, r_sem, sx_sem, rx_sem, sy_sem, ry_sem) = refs
    blocks = own_buf.shape[0]
    width = own_buf.shape[1]
    half = blocks // 2
    c = lax.axis_index("contact")
    b = lax.axis_index("body")
    core = lax.rem(c, 2)
    x = lax.rem(c // 2, gx)
    y = c // (2 * gx)
    mate = c + 1 - 2 * core
    up = lax.rem(b + 1, n_body)
    down = lax.rem(b + n_body - 1, n_body)
    x_peers = [(y * gx + lax.rem(x + j, gx)) * 2 + core for j in range(1, gx)]
    y_peers = [(lax.rem(y + j, gy) * gx + x) * 2 + core for j in range(1, gy)]

    greet = [(mate, b), (c, up), (mate, up), (c, down), (mate, down)]
    greet += [(p, b) for p in x_peers] + [(p, b) for p in y_peers]
    mine = pl.ds(pl.multiple_of(core * half, half), half)
    theirs = pl.ds(pl.multiple_of((1 - core) * half, half), half)
    barrier = pltpu.get_barrier_semaphore()
    for dev in greet:
        pl.semaphore_signal(barrier, inc=1, device_id=dev, device_id_type=MESH)
    later_buf[...] = scatter_rows(tb_ref, 1, push_ref, blocks)
    own_buf[...] = scatter_rows(tb_ref, 0, push_ref, blocks)
    vn_send[0] = vfree_ref[mine]
    vn_send[1] = imass_ref[mine]
    pl.semaphore_wait(barrier, len(greet))

    def remote(src, dst, send, recv, dev):
        return pltpu.make_async_remote_copy(
            src_ref=src, dst_ref=dst, send_sem=send, recv_sem=recv,
            device_id=dev, device_id_type=MESH,
        )

    sent = []
    plan = (
        (later_buf.at[mine], (c, up)),
        (later_buf.at[theirs], (mate, up)),
        (later_buf.at[theirs], (mate, b)),
    )
    for k, (src, dev) in enumerate(plan):
        cp = remote(src, recv6.at[k], s_sem.at[k], r_sem.at[k], dev)
        cp.start()
        sent.append(cp)
    plan = (
        (own_buf.at[mine], (c, down)),
        (own_buf.at[theirs], (mate, down)),
        (own_buf.at[theirs], (mate, b)),
    )
    for k, (src, dev) in enumerate(plan):
        cp = remote(src, recv6.at[3 + k], s_sem.at[3 + k], r_sem.at[3 + k], dev)
        cp.start()
        sent.append(cp)
    vcp = remote(vn_send, vnext_ref, s_sem.at[8], r_sem.at[8], (c, down))
    vcp.start()
    sent.append(vcp)
    senders = ((c, down), (mate, down), (mate, b), (c, up), (mate, up), (mate, b))
    for k, dev in enumerate(senders):
        remote(own_buf.at[mine], recv6.at[k], s_sem.at[k], r_sem.at[k], dev).wait_recv()
    part = jnp.concatenate([
        own_buf[mine] + recv6[5] + recv6[0] + recv6[1],
        later_buf[mine] + recv6[2] + recv6[3] + recv6[4],
    ], axis=0)

    rounds = [(xbuf, x, x_peers, gx, sx_sem, rx_sem), (ybuf, y, y_peers, gy, sy_sem, ry_sem)]
    if gx == gy:
        first = [xv * (1 - core) + yv * core for xv, yv in zip([x] + x_peers, [y] + y_peers)]
        second = [xv * core + yv * (1 - core) for xv, yv in zip([x] + x_peers, [y] + y_peers)]
        rounds = [(xbuf, first[0], first[1:], gx, sx_sem, rx_sem),
                  (ybuf, second[0], second[1:], gy, sy_sem, ry_sem)]
    for buf, pos, peers, size, ssem, rsem in rounds:
        if size == 1:
            continue
        buf[pos] = part
        for j in sorted(range(size - 1), key=lambda j: -min(j + 1, size - 1 - j)):
            p = peers[j]
            cp = remote(buf.at[pos], buf.at[pos], ssem.at[j], rsem.at[pos], (p, b))
            cp.start()
            sent.append(cp)
        for j in range(1, size):
            src_pos = lax.rem(pos + size - j, size)
            remote(buf.at[src_pos], buf.at[src_pos], ssem.at[0], rsem.at[src_pos], (peers[-j], b)).wait_recv()
        part = buf[0]
        for g in range(1, size):
            part = part + buf[g]

    vel_buf[0, mine] = (vfree_ref[mine] + imass_ref[mine] * part[:half]).astype(jnp.bfloat16)
    remote(vn_send, vnext_ref, s_sem.at[8], r_sem.at[8], (c, up)).wait_recv()
    vel_buf[1, mine] = (vnext_ref[0] + vnext_ref[1] * part[half:]).astype(jnp.bfloat16)
    for k in range(2):
        cp = remote(vel_buf.at[k, mine], vel_buf.at[k, mine], s_sem.at[6 + k], r_sem.at[6 + k], (mate, b))
        cp.start()
        sent.append(cp)
    for k in range(2):
        remote(vel_buf.at[k, theirs], vel_buf.at[k, theirs], s_sem.at[6 + k], r_sem.at[6 + k], (mate, b)).wait_recv()
    velf[...] = vel_buf[...].astype(jnp.float32)
    tiles = rows_buf.shape[1]
    for column in range(2):
        for t in range(tiles):
            rows_buf[column, pl.ds(t, 1), :] = velf[column, pl.ds(tb_ref[column, t], 1), :]
        rows_out[column] = rows_buf[column].astype(jnp.bfloat16)
    for cp in sent:
        cp.wait_send()


def dual_exchange(tile_block, push, vel_free, inv_mass, n_contact, n_body):
    gx, gy = contact_groups(n_contact)
    blocks, width = vel_free.shape
    tiles = push.shape[1]
    half = blocks // 2
    vspec = pl.BlockSpec(memory_space=pltpu.VMEM)
    sspec = pl.BlockSpec(memory_space=pltpu.SMEM)
    scratch = [
        pltpu.VMEM((blocks, width), jnp.float32),
        pltpu.VMEM((blocks, width), jnp.float32),
        pltpu.VMEM((6, half, width), jnp.float32),
        pltpu.VMEM((gx, blocks, width), jnp.float32),
        pltpu.VMEM((gy, blocks, width), jnp.float32),
        pltpu.VMEM((2, blocks, width), jnp.bfloat16),
        pltpu.VMEM((2, blocks, width), jnp.float32),
        pltpu.VMEM((2, tiles, width), jnp.float32),
        pltpu.VMEM((2, half, width), jnp.float32),
        pltpu.VMEM((2, half, width), jnp.float32),
        pltpu.SemaphoreType.DMA((9,)),
        pltpu.SemaphoreType.DMA((9,)),
        pltpu.SemaphoreType.DMA((max(gx - 1, 1),)),
        pltpu.SemaphoreType.DMA((gx,)),
        pltpu.SemaphoreType.DMA((max(gy - 1, 1),)),
        pltpu.SemaphoreType.DMA((gy,)),
    ]
    return pl.pallas_call(
        functools.partial(dual_kernel, n_contact, n_body),
        out_shape=jax.ShapeDtypeStruct((2, tiles, width), jnp.bfloat16),
        in_specs=[sspec] + [vspec] * 3,
        out_specs=vspec,
        scratch_shapes=scratch,
        compiler_params=pltpu.CompilerParams(collective_id=2, has_side_effects=True),
    )(tile_block, push, vel_free, inv_mass)


def per_device(
    n_contact, n_body,
    jacobian, tile_block, tile_count, vel_free, inv_mass, bias, step_scale, friction, impulse_start,
):
    tiles_here = jacobian.shape[0]
    contacts = friction.shape[1]
    order = jnp.arange(tiles_here, dtype=jnp.int32)
    mask = (order < tile_count[0]).astype(jnp.float32)[:, None]

    def pushes(lam):
        lamb = lam.astype(jnp.bfloat16)
        return jnp.einsum("tkbc,tc->ktb", jacobian, lamb, preferred_element_type=jnp.float32)

    lam = impulse_start * mask
    for sweep in range(ITERS):
        rows = dual_exchange(tile_block.T, pushes(lam), vel_free, inv_mass, n_contact, n_body)
        rel = jnp.einsum("tkbc,ktb->tc", jacobian, rows, preferred_element_type=jnp.float32) + bias
        lam = project(lam - step_scale * rel, friction, contacts) * mask
    lamb = lam.astype(jnp.bfloat16).astype(jnp.float32)
    push = jnp.sum(jacobian.astype(jnp.float32) * lamb[:, None, None, :], axis=-1)
    total = sweep_exchange(tile_block.T, push, vel_free, inv_mass, n_contact, n_body, True)
    velocity = vel_free + inv_mass * total
    return (lam, velocity)


def solution(mesh):
    n_contact = mesh.shape["contact"]
    n_body = mesh.shape["body"]
    placed = (
        P(("contact", "body"), None, None, None),
        P(("contact", "body"), None),
        P(("contact", "body")),
        P("body", None),
        P("body", None),
        P(("contact", "body"), None),
        P(("contact", "body"), None),
        P(("contact", "body"), None),
        P(("contact", "body"), None),
    )
    return jax.shard_map(
        functools.partial(per_device, n_contact, n_body),
        mesh=mesh,
        in_specs=placed,
        out_specs=(P(("contact", "body"), None), P("body", None)),
        check_vma=False,
    )
```

```python
import functools
import math

import jax
import jax.numpy as jnp
from jax import lax
from jax.experimental import pallas as pl
from jax.experimental.pallas import tpu as pltpu
from jax.sharding import PartitionSpec as P

ITERS = 2
MESH = pl.DeviceIdType.MESH


def project(trial, friction, contacts):
    normal = trial[:, :contacts]
    first = trial[:, contacts : 2 * contacts]
    second = trial[:, 2 * contacts :]
    tangent = jnp.sqrt(first * first + second * second)
    inside = tangent <= friction * normal
    below = friction * tangent <= -normal
    moved = (normal + friction * tangent) / (1.0 + friction * friction)
    safe = jnp.where(inside | below, 1.0, tangent)
    factor = jnp.where(inside, 1.0, jnp.where(below, 0.0, friction * moved / safe))
    new_normal = jnp.where(inside, normal, jnp.where(below, 0.0, moved))
    return jnp.concatenate([new_normal, first * factor, second * factor], axis=1)


def contact_groups(n_contact):
    rest = n_contact // 2
    gy = 1
    for d in range(1, int(math.isqrt(rest)) + 1):
        if rest % d == 0:
            gy = d
    return rest // gy, gy


def scatter_rows(tb_ref, column, push_ref, blocks, tile_major=False):
    tiles = push_ref.shape[0] if tile_major else push_ref.shape[1]
    width = push_ref.shape[2]
    slot = lax.broadcasted_iota(jnp.int32, (blocks, width), 0)
    acc = None
    for t in range(tiles):
        if tile_major:
            row = push_ref[t, column : column + 1, :]
        else:
            row = push_ref[column, t : t + 1, :]
        term = jnp.where(slot == tb_ref[column, t], row, 0.0)
        acc = term if acc is None else acc + term
    return acc


def sweep_kernel(n_contact, n_body, last, *refs):
    gx, gy = contact_groups(n_contact)
    if last:
        (tb_ref, push_ref,
         tot_out,
         own_buf, later_buf, recv3, xbuf, ybuf, tot_buf,
         s_sem, r_sem, sx_sem, rx_sem, sy_sem, ry_sem) = refs
    else:
        (tb_ref, push_ref, vfree_ref, imass_ref,
         rows_out,
         own_buf, later_buf, recv3, xbuf, ybuf, vel_buf, vel_next, velf, rows_buf,
         s_sem, r_sem, sx_sem, rx_sem, sy_sem, ry_sem) = refs
    blocks = own_buf.shape[0]
    width = own_buf.shape[1]
    half = blocks // 2
    c = lax.axis_index("contact")
    b = lax.axis_index("body")
    core = lax.rem(c, 2)
    x = lax.rem(c // 2, gx)
    y = c // (2 * gx)
    mate = c + 1 - 2 * core
    up = lax.rem(b + 1, n_body)
    down = lax.rem(b + n_body - 1, n_body)
    x_peers = [(y * gx + lax.rem(x + j, gx)) * 2 + core for j in range(1, gx)]
    y_peers = [(lax.rem(y + j, gy) * gx + x) * 2 + core for j in range(1, gy)]

    greet = [(mate, b), (c, up), (mate, up), (c, down), (mate, down)]
    greet += [(p, b) for p in x_peers] + [(p, b) for p in y_peers]
    barrier = pltpu.get_barrier_semaphore()
    for dev in greet:
        pl.semaphore_signal(barrier, inc=1, device_id=dev, device_id_type=MESH)
    later_buf[...] = scatter_rows(tb_ref, 1, push_ref, blocks, last)
    own_buf[...] = scatter_rows(tb_ref, 0, push_ref, blocks, last)
    pl.semaphore_wait(barrier, len(greet))

    def remote(src, dst, send, recv, dev):
        return pltpu.make_async_remote_copy(
            src_ref=src, dst_ref=dst, send_sem=send, recv_sem=recv,
            device_id=dev, device_id_type=MESH,
        )

    mine = pl.ds(pl.multiple_of(core * half, half), half)
    theirs = pl.ds(pl.multiple_of((1 - core) * half, half), half)
    sent = []
    for k, (src, dev) in enumerate(((later_buf.at[mine], (c, up)), (later_buf.at[theirs], (mate, up)))):
        cp = remote(src, recv3.at[1 + k], s_sem.at[1 + k], r_sem.at[1 + k], dev)
        cp.start()
        sent.append(cp)
    cp = remote(own_buf.at[theirs], recv3.at[0], s_sem.at[0], r_sem.at[0], (mate, b))
    cp.start()
    sent.append(cp)
    for k, dev in enumerate(((mate, b), (c, down), (mate, down))):
        remote(own_buf.at[mine], recv3.at[k], s_sem.at[k], r_sem.at[k], dev).wait_recv()
    part = own_buf[mine] + recv3[0] + recv3[1] + recv3[2]

    rounds = [(xbuf, x, x_peers, gx, sx_sem, rx_sem), (ybuf, y, y_peers, gy, sy_sem, ry_sem)]
    if gx == gy:
        first = [xv * (1 - core) + yv * core for xv, yv in zip([x] + x_peers, [y] + y_peers)]
        second = [xv * core + yv * (1 - core) for xv, yv in zip([x] + x_peers, [y] + y_peers)]
        rounds = [(xbuf, first[0], first[1:], gx, sx_sem, rx_sem),
                  (ybuf, second[0], second[1:], gy, sy_sem, ry_sem)]
    for buf, pos, peers, size, ssem, rsem in rounds:
        if size == 1:
            continue
        buf[pos] = part
        for j in sorted(range(size - 1), key=lambda j: -min(j + 1, size - 1 - j)):
            p = peers[j]
            cp = remote(buf.at[pos], buf.at[pos], ssem.at[j], rsem.at[pos], (p, b))
            cp.start()
            sent.append(cp)
        for j in range(1, size):
            src_pos = lax.rem(pos + size - j, size)
            remote(buf.at[src_pos], buf.at[src_pos], ssem.at[0], rsem.at[src_pos], (peers[-j], b)).wait_recv()
        part = buf[0]
        for g in range(1, size):
            part = part + buf[g]

    if last:
        tot_buf[mine] = part
        cp = remote(tot_buf.at[mine], tot_buf.at[mine], s_sem.at[3], r_sem.at[3], (mate, b))
        cp.start()
        sent.append(cp)
        remote(tot_buf.at[theirs], tot_buf.at[theirs], s_sem.at[3], r_sem.at[3], (mate, b)).wait_recv()
        tot_out[...] = tot_buf[...]
    else:
        vel = vfree_ref[mine] + imass_ref[mine] * part
        vel_buf[mine] = vel.astype(jnp.bfloat16)
        src = vel_buf.at[mine]
        for k, (dst, dev) in enumerate((
            (vel_buf.at[mine], (mate, b)),
            (vel_next.at[mine], (c, down)),
            (vel_next.at[mine], (mate, down)),
        )):
            cp = remote(src, dst, s_sem.at[3 + k], r_sem.at[3 + k], dev)
            cp.start()
            sent.append(cp)
        for k, (dst, dev) in enumerate((
            (vel_buf.at[theirs], (mate, b)),
            (vel_next.at[mine], (c, up)),
            (vel_next.at[theirs], (mate, up)),
        )):
            remote(src, dst, s_sem.at[3 + k], r_sem.at[3 + k], dev).wait_recv()
        velf[0] = vel_buf[...].astype(jnp.float32)
        velf[1] = vel_next[...].astype(jnp.float32)
        tiles = rows_buf.shape[1]
        for column in range(2):
            for t in range(tiles):
                rows_buf[column, pl.ds(t, 1), :] = velf[column, pl.ds(tb_ref[column, t], 1), :]
            rows_out[column] = rows_buf[column].astype(jnp.bfloat16)
    for cp in sent:
        cp.wait_send()


def sweep_exchange(tile_block, push, vel_free, inv_mass, n_contact, n_body, last):
    gx, gy = contact_groups(n_contact)
    blocks, width = vel_free.shape
    tiles = push.shape[0] if last else push.shape[1]
    half = blocks // 2
    vspec = pl.BlockSpec(memory_space=pltpu.VMEM)
    sspec = pl.BlockSpec(memory_space=pltpu.SMEM)
    if last:
        args = [tile_block, push]
        out_shape = jax.ShapeDtypeStruct((blocks, width), jnp.float32)
        tail = [pltpu.VMEM((blocks, width), jnp.float32)]
    else:
        args = [tile_block, push, vel_free, inv_mass]
        out_shape = jax.ShapeDtypeStruct((2, tiles, width), jnp.bfloat16)
        tail = [
            pltpu.VMEM((blocks, width), jnp.bfloat16),
            pltpu.VMEM((blocks, width), jnp.bfloat16),
            pltpu.VMEM((2, blocks, width), jnp.float32),
            pltpu.VMEM((2, tiles, width), jnp.float32),
        ]
    scratch = [
        pltpu.VMEM((blocks, width), jnp.float32),
        pltpu.VMEM((blocks, width), jnp.float32),
        pltpu.VMEM((3, half, width), jnp.float32),
        pltpu.VMEM((gx, half, width), jnp.float32),
        pltpu.VMEM((gy, half, width), jnp.float32),
        *tail,
        pltpu.SemaphoreType.DMA((6,)),
        pltpu.SemaphoreType.DMA((6,)),
        pltpu.SemaphoreType.DMA((max(gx - 1, 1),)),
        pltpu.SemaphoreType.DMA((gx,)),
        pltpu.SemaphoreType.DMA((max(gy - 1, 1),)),
        pltpu.SemaphoreType.DMA((gy,)),
    ]
    return pl.pallas_call(
        functools.partial(sweep_kernel, n_contact, n_body, last),
        out_shape=out_shape,
        in_specs=[sspec] + [vspec] * (len(args) - 1),
        out_specs=vspec,
        scratch_shapes=scratch,
        compiler_params=pltpu.CompilerParams(
            collective_id=1 if last else 0, has_side_effects=True
        ),
    )(*args)


def dual_kernel(n_contact, n_body, *refs):
    gx, gy = contact_groups(n_contact)
    (tb_ref, push_ref, vfree_ref, imass_ref,
     rows_out,
     own_buf, later_buf, recv6, xbuf, ybuf, vel_buf, velf, rows_buf, vn_send, vnext_ref,
     s_sem, r_sem, sx_sem, rx_sem, sy_sem, ry_sem) = refs
    blocks = own_buf.shape[0]
    width = own_buf.shape[1]
    half = blocks // 2
    c = lax.axis_index("contact")
    b = lax.axis_index("body")
    core = lax.rem(c, 2)
    x = lax.rem(c // 2, gx)
    y = c // (2 * gx)
    mate = c + 1 - 2 * core
    up = lax.rem(b + 1, n_body)
    down = lax.rem(b + n_body - 1, n_body)
    x_peers = [(y * gx + lax.rem(x + j, gx)) * 2 + core for j in range(1, gx)]
    y_peers = [(lax.rem(y + j, gy) * gx + x) * 2 + core for j in range(1, gy)]

    greet = [(mate, b), (c, up), (mate, up), (c, down), (mate, down)]
    greet += [(p, b) for p in x_peers] + [(p, b) for p in y_peers]
    mine = pl.ds(pl.multiple_of(core * half, half), half)
    theirs = pl.ds(pl.multiple_of((1 - core) * half, half), half)
    barrier = pltpu.get_barrier_semaphore()
    for dev in greet:
        pl.semaphore_signal(barrier, inc=1, device_id=dev, device_id_type=MESH)
    later_buf[...] = scatter_rows(tb_ref, 1, push_ref, blocks)
    own_buf[...] = scatter_rows(tb_ref, 0, push_ref, blocks)
    vn_send[0] = vfree_ref[mine]
    vn_send[1] = imass_ref[mine]
    pl.semaphore_wait(barrier, len(greet))

    def remote(src, dst, send, recv, dev):
        return pltpu.make_async_remote_copy(
            src_ref=src, dst_ref=dst, send_sem=send, recv_sem=recv,
            device_id=dev, device_id_type=MESH,
        )

    sent = []
    plan = (
        (later_buf.at[mine], (c, up)),
        (later_buf.at[theirs], (mate, up)),
        (later_buf.at[theirs], (mate, b)),
        (own_buf.at[mine], (c, down)),
        (own_buf.at[theirs], (mate, down)),
        (own_buf.at[theirs], (mate, b)),
    )
    for k in (0, 1, 3, 4, 2, 5):
        src, dev = plan[k]
        cp = remote(src, recv6.at[k], s_sem.at[k], r_sem.at[k], dev)
        cp.start()
        sent.append(cp)
    vcp = remote(vn_send, vnext_ref, s_sem.at[8], r_sem.at[8], (c, down))
    vcp.start()
    sent.append(vcp)
    senders = ((c, down), (mate, down), (mate, b), (c, up), (mate, up), (mate, b))
    for k, dev in enumerate(senders):
        remote(own_buf.at[mine], recv6.at[k], s_sem.at[k], r_sem.at[k], dev).wait_recv()
    part = jnp.concatenate([
        own_buf[mine] + recv6[5] + recv6[0] + recv6[1],
        later_buf[mine] + recv6[2] + recv6[3] + recv6[4],
    ], axis=0)

    rounds = [(xbuf, x, x_peers, gx, sx_sem, rx_sem), (ybuf, y, y_peers, gy, sy_sem, ry_sem)]
    if gx == gy:
        first = [xv * (1 - core) + yv * core for xv, yv in zip([x] + x_peers, [y] + y_peers)]
        second = [xv * core + yv * (1 - core) for xv, yv in zip([x] + x_peers, [y] + y_peers)]
        rounds = [(xbuf, first[0], first[1:], gx, sx_sem, rx_sem),
                  (ybuf, second[0], second[1:], gy, sy_sem, ry_sem)]
    for buf, pos, peers, size, ssem, rsem in rounds:
        if size == 1:
            continue
        buf[pos] = part
        for j in sorted(range(size - 1), key=lambda j: -min(j + 1, size - 1 - j)):
            p = peers[j]
            cp = remote(buf.at[pos], buf.at[pos], ssem.at[j], rsem.at[pos], (p, b))
            cp.start()
            sent.append(cp)
        for j in range(1, size):
            src_pos = lax.rem(pos + size - j, size)
            remote(buf.at[src_pos], buf.at[src_pos], ssem.at[0], rsem.at[src_pos], (peers[-j], b)).wait_recv()
        part = buf[0]
        for g in range(1, size):
            part = part + buf[g]

    vel_buf[0, mine] = (vfree_ref[mine] + imass_ref[mine] * part[:half]).astype(jnp.bfloat16)
    remote(vn_send, vnext_ref, s_sem.at[8], r_sem.at[8], (c, up)).wait_recv()
    vel_buf[1, mine] = (vnext_ref[0] + vnext_ref[1] * part[half:]).astype(jnp.bfloat16)
    for k in range(2):
        cp = remote(vel_buf.at[k, mine], vel_buf.at[k, mine], s_sem.at[6 + k], r_sem.at[6 + k], (mate, b))
        cp.start()
        sent.append(cp)
    for k in range(2):
        remote(vel_buf.at[k, theirs], vel_buf.at[k, theirs], s_sem.at[6 + k], r_sem.at[6 + k], (mate, b)).wait_recv()
    velf[...] = vel_buf[...].astype(jnp.float32)
    tiles = rows_buf.shape[1]
    for column in range(2):
        for t in range(tiles):
            rows_buf[column, pl.ds(t, 1), :] = velf[column, pl.ds(tb_ref[column, t], 1), :]
        rows_out[column] = rows_buf[column].astype(jnp.bfloat16)
    for cp in sent:
        cp.wait_send()


def dual_exchange(tile_block, push, vel_free, inv_mass, n_contact, n_body):
    gx, gy = contact_groups(n_contact)
    blocks, width = vel_free.shape
    tiles = push.shape[1]
    half = blocks // 2
    vspec = pl.BlockSpec(memory_space=pltpu.VMEM)
    sspec = pl.BlockSpec(memory_space=pltpu.SMEM)
    scratch = [
        pltpu.VMEM((blocks, width), jnp.float32),
        pltpu.VMEM((blocks, width), jnp.float32),
        pltpu.VMEM((6, half, width), jnp.float32),
        pltpu.VMEM((gx, blocks, width), jnp.float32),
        pltpu.VMEM((gy, blocks, width), jnp.float32),
        pltpu.VMEM((2, blocks, width), jnp.bfloat16),
        pltpu.VMEM((2, blocks, width), jnp.float32),
        pltpu.VMEM((2, tiles, width), jnp.float32),
        pltpu.VMEM((2, half, width), jnp.float32),
        pltpu.VMEM((2, half, width), jnp.float32),
        pltpu.SemaphoreType.DMA((9,)),
        pltpu.SemaphoreType.DMA((9,)),
        pltpu.SemaphoreType.DMA((max(gx - 1, 1),)),
        pltpu.SemaphoreType.DMA((gx,)),
        pltpu.SemaphoreType.DMA((max(gy - 1, 1),)),
        pltpu.SemaphoreType.DMA((gy,)),
    ]
    return pl.pallas_call(
        functools.partial(dual_kernel, n_contact, n_body),
        out_shape=jax.ShapeDtypeStruct((2, tiles, width), jnp.bfloat16),
        in_specs=[sspec] + [vspec] * 3,
        out_specs=vspec,
        scratch_shapes=scratch,
        compiler_params=pltpu.CompilerParams(collective_id=2, has_side_effects=True),
    )(tile_block, push, vel_free, inv_mass)


def per_device(
    n_contact, n_body,
    jacobian, tile_block, tile_count, vel_free, inv_mass, bias, step_scale, friction, impulse_start,
):
    tiles_here = jacobian.shape[0]
    contacts = friction.shape[1]
    order = jnp.arange(tiles_here, dtype=jnp.int32)
    mask = (order < tile_count[0]).astype(jnp.float32)[:, None]

    def pushes(lam):
        lamb = lam.astype(jnp.bfloat16)
        return jnp.einsum("tkbc,tc->ktb", jacobian, lamb, preferred_element_type=jnp.float32)

    lam = impulse_start * mask
    for sweep in range(ITERS):
        rows = dual_exchange(tile_block.T, pushes(lam), vel_free, inv_mass, n_contact, n_body)
        rel = jnp.einsum("tkbc,ktb->tc", jacobian, rows, preferred_element_type=jnp.float32) + bias
        lam = project(lam - step_scale * rel, friction, contacts) * mask
    lamb = lam.astype(jnp.bfloat16).astype(jnp.float32)
    push = jnp.sum(jacobian.astype(jnp.float32) * lamb[:, None, None, :], axis=-1)
    total = sweep_exchange(tile_block.T, push, vel_free, inv_mass, n_contact, n_body, True)
    velocity = vel_free + inv_mass * total
    return (lam, velocity)


def solution(mesh):
    n_contact = mesh.shape["contact"]
    n_body = mesh.shape["body"]
    placed = (
        P(("contact", "body"), None, None, None),
        P(("contact", "body"), None),
        P(("contact", "body")),
        P("body", None),
        P("body", None),
        P(("contact", "body"), None),
        P(("contact", "body"), None),
        P(("contact", "body"), None),
        P(("contact", "body"), None),
    )
    return jax.shard_map(
        functools.partial(per_device, n_contact, n_body),
        mesh=mesh,
        in_specs=placed,
        out_specs=(P(("contact", "body"), None), P("body", None)),
        check_vma=False,
    )
```
